32 devices in a mesh: arc: 2 (over core), par: 16 (over z, y, x).
Axes of the slice: x: 2, y: 2, z: 4, core: 2. Of those that a mesh axis runs over, the one named last changes fastest.
Arguments:
- design: bfloat16 [4, 1024, 40960], P('arc', None, 'par'), may hold values from -0.1875 to 0.1875
- cov_factor: float32 [4, 1024, 1024], P('arc', 'par'), may hold values from -1 to 3, as said below
- active_blocks: int32 [4, 80], P('arc'), may hold values from 0 to 159, all different within a row
- panel_index: int32 [1], replicated, may hold values from 0 to 79
- reg_diag: float32 [40960], replicated, may hold values from 0.5 to 4
Outputs:
- solved: float32 [512, 40960], P(None, ('par', 'arc'))
The draws below stay inside these ranges and needn't reach their ends.
Inputs may be any that keep to these rules, and one draw needn't show every extreme that they name: Each cov_factor[a] is lower triangular with a positive diagonal.
All inputs are finite; a program needn't handle non-finite values.
Results may differ from the reference program's by a relative error of at most 0.0032.
Values may be sent and summed in bfloat16 or wider, within the bound.
No kernel may reach another device: no remote copies, remote signals or barrier semaphores. Data moves between devices by JAX's collectives and lax.ppermute only.
A program may use at most 192 MiB of HBM per device.

```python
import math
import jax
import jax.numpy as jnp
from jax import lax

P_SIZE = 40960
OBS = 1024
PANEL = 512
BLK = 256
ACT = 80
ARCS = 4


def draw_cov_factor(key, part):
    first, second = jax.random.split(jax.random.fold_in(key, 7))
    spread = 0.5 / OBS ** 0.5
    diagonal = jax.random.uniform(first, (ARCS, OBS), jnp.float32, 1.0, 2.0)
    lower = jnp.clip(jax.random.normal(second, (ARCS, OBS, OBS), jnp.float32), -6.0, 6.0) * spread
    below = jnp.tril(jnp.ones((OBS, OBS), jnp.float32), -1)
    unit = jnp.eye(OBS, dtype=jnp.float32)
    return lower * below[None] + diagonal[:, :, None] * unit[None]


def shard_levels(stream_key, extent, cuts, low, high):
    level = 1.0
    for position, blocks in cuts:
        draws = jax.random.uniform(jax.random.fold_in(jax.random.fold_in(stream_key, 6), position), (blocks,), jnp.float32, low / len(cuts), high / len(cuts))
        level = level * jnp.repeat(jnp.exp(draws), extent[position] // blocks).reshape((-1,) + (1,) * (len(extent) - 1 - position))
    return level


def distinct(rng, rows, amount, top, lift):
    ranking = jax.random.permutation(jax.random.fold_in(rng, 1), amount)
    favour = ranking
    for power in range(3):
        favour = favour * favour // amount
    favour = favour * lift // amount
    chance = jax.random.randint(jax.random.fold_in(rng, 2), (rows, amount), 0, 4096) + favour
    holders = jax.random.permutation(jax.random.fold_in(rng, 3), rows)[jnp.arange(amount) % rows]
    chance = jnp.where(jnp.arange(rows)[:, None] == holders[None, :], 1 << 14, chance)
    merit = chance * amount + jnp.arange(amount)
    return lax.top_k(merit.astype(jnp.int32), top)[1].astype(jnp.int32)


def scatter_about(rng, extent, deviation, bound, cuts=(), kind=jnp.bfloat16):
    gain = shard_levels(rng, extent, cuts, -0.22, 0.18) if cuts else 1.0
    result = jax.random.normal(rng, extent, jnp.float32) * deviation * gain
    return jnp.minimum(jnp.maximum(result, -bound), bound).astype(kind)


def setup_inputs(seed: int = 0) -> dict:
    seeds = jax.random.split(jax.random.key(seed), 6)
    return {
        "design": scatter_about(seeds[0], (ARCS, OBS, P_SIZE), OBS ** -0.5, 0.1875, ((0, 2), (2, 16))),
        "cov_factor": draw_cov_factor(jax.random.fold_in(seeds[5], 71), 0),
        "active_blocks": distinct(seeds[2], ARCS, P_SIZE // BLK, ACT, 4096),
        "panel_index": jax.random.randint(seeds[3], (1,), 0, P_SIZE // PANEL).astype(jnp.int32),
        "reg_diag": jnp.clip(jnp.exp(jax.random.uniform(seeds[4], (P_SIZE,), jnp.float32, math.log(0.5), math.log(4.0))), 0.5, 4.0),
    }


def whiten(factor, rhs):
    size = factor.shape[0]
    step = min(128, size)
    pieces = []
    for index in range(size // step):
        low = index * step
        accum = rhs[low:low + step]
        if index > 0:
            done = jnp.concatenate(pieces, axis=0)
            accum = accum - jnp.dot(factor[low:low + step, :low].astype(jnp.float32), done.astype(jnp.float32), precision=lax.Precision.HIGHEST, preferred_element_type=jnp.float32)
        pieces.append(lax.linalg.triangular_solve(factor[low:low + step, low:low + step], accum, left_side=True, lower=True))
    return jnp.concatenate(pieces, axis=0)

def reference(design, cov_factor, active_blocks, panel_index, reg_diag):
    nblocks = P_SIZE // BLK
    start = (panel_index[0] * PANEL).astype(jnp.int32)
    block_ids = jnp.arange(nblocks, dtype=jnp.int32)

    def one_arc(normals, inputs):
        rows, factor, active = inputs
        hits = jnp.any(active[:, None] == block_ids[None, :], axis=0)
        col_mask = jnp.repeat(hits, BLK).astype(rows.dtype)
        masked = rows * col_mask[None, :]
        picked = rows.reshape(OBS, nblocks, BLK)[:, active, :].reshape(OBS, ACT * BLK)
        whitened = whiten(factor, picked.astype(jnp.float32)).astype(jnp.bfloat16)
        raw_panel = lax.dynamic_slice_in_dim(masked, start, PANEL, 1).astype(jnp.float32)
        panel = whiten(factor, raw_panel).astype(jnp.bfloat16)
        term = jnp.dot(panel.T.astype(jnp.float32), whitened.astype(jnp.float32), preferred_element_type=jnp.float32)
        grid = normals.reshape(PANEL, nblocks, BLK).at[:, active, :].add(term.reshape(PANEL, ACT, BLK))
        return (grid.reshape(PANEL, P_SIZE), None)
    normals, _ = lax.scan(one_arc, jnp.zeros((PANEL, P_SIZE), jnp.float32), (design, cov_factor, active_blocks))
    reg_panel = lax.dynamic_slice_in_dim(reg_diag, start, PANEL)
    block = lax.dynamic_slice_in_dim(normals, start, PANEL, 1) + jnp.diag(reg_panel)
    lower11 = jnp.linalg.cholesky(block)
    columns = jnp.arange(P_SIZE, dtype=jnp.int32)
    rows_at = start + jnp.arange(PANEL, dtype=jnp.int32)
    shifted = normals + jnp.where(columns[None, :] == rows_at[:, None], reg_panel[:, None], jnp.float32(0.0))
    return whiten(lower11, shifted)
```

```python
import functools

import jax
import jax.numpy as jnp
from jax import lax
from jax.experimental import pallas as pl
from jax.experimental.pallas import tpu as pltpu
from jax.sharding import PartitionSpec as P

PANEL = 512
BLK = 256
F32, BF16 = jnp.float32, jnp.bfloat16
LANE = 128


def split(value):
    high = value.astype(BF16)
    return high, (value - high.astype(F32)).astype(BF16)


def mm(a, b, dims=((1,), (0,))):
    return lax.dot_general(a, b, (dims, ((), ())), preferred_element_type=F32)


def mm3(a, b):
    ah, al = split(a)
    bh, bl = split(b)
    return mm(ah, bh) + (mm(ah, bl) + mm(al, bh))


def level_mask(step):
    rows = lax.broadcasted_iota(jnp.int32, (LANE, LANE), 0)
    cols = lax.broadcasted_iota(jnp.int32, (LANE, LANE), 1)
    return (
        (rows // (2 * step) == cols // (2 * step))
        & ((rows // step) % 2 == 1)
        & ((cols // step) % 2 == 0)
    )


def invert_levels(inverse, lower, first, last):
    step = first
    while step < last:
        below = jnp.where(level_mask(step), lower, 0.0)
        inverse = inverse - mm3(inverse, mm3(below, inverse))
        step *= 2
    return inverse


def diag_kernel(off_ref, strip_ref, out_ref, square):
    arcs, rows, _ = strip_ref.shape
    off = pl.multiple_of(off_ref[0], 8)
    r = lax.broadcasted_iota(jnp.int32, (LANE, LANE), 0)
    c = lax.broadcasted_iota(jnp.int32, (LANE, LANE), 1)
    eye = r == c
    sub = lax.broadcasted_iota(jnp.int32, (rows, LANE), 1)
    own = (sub >= off) & (sub < off + rows)
    for arc in range(arcs):
        square[arc] = eye.astype(F32)
        square[arc, pl.ds(off, rows), :] = jnp.where(own, strip_ref[arc], 0.0)
    lowers = [square[arc] for arc in range(arcs)]
    invs = [jnp.where(eye, 1.0 / jnp.where(eye, low, 1.0), 0.0) for low in lowers]
    step = 1
    while step < rows:
        mask = level_mask(step)
        parts = [mm3(jnp.where(mask, low, 0.0), inv) for low, inv in zip(lowers, invs)]
        invs = [inv - mm3(inv, part) for inv, part in zip(invs, parts)]
        step *= 2
    for arc in range(arcs):
        square[arc] = invs[arc]
        out_ref[arc] = jnp.where(own, square[arc, pl.ds(off, rows), :], strip_ref[arc])


def invert_diag(strip, off):
    arcs, rows, _ = strip.shape
    return pl.pallas_call(
        diag_kernel,
        out_shape=jax.ShapeDtypeStruct(strip.shape, F32),
        in_specs=[pl.BlockSpec(memory_space=pltpu.SMEM), pl.BlockSpec(memory_space=pltpu.VMEM)],
        out_specs=pl.BlockSpec(memory_space=pltpu.VMEM),
        scratch_shapes=[pltpu.VMEM((arcs, LANE, LANE), F32)],
        name="invert_diag",
    )(off, strip)


def invert_factor(lower_ref, high, low, first):
    size = high.shape[0]
    span = max(size // 2, LANE)
    for top in range(0, size, span):
        for ref in (high, low):
            ref[top : top + span, top : top + span] = jnp.zeros((span, span), BF16)
    rows = lax.broadcasted_iota(jnp.int32, (LANE, LANE), 0) // first
    cols = lax.broadcasted_iota(jnp.int32, (LANE, LANE), 1) // first
    blocks = [lower_ref[t : t + LANE, t : t + LANE] for t in range(0, size, LANE)]
    invs = [jnp.where(rows == cols, block, 0.0) for block in blocks]
    step = first
    while step < LANE:
        mask = level_mask(step)
        parts = [mm3(jnp.where(mask, block, 0.0), inv) for block, inv in zip(blocks, invs)]
        invs = [inv - mm3(inv, part) for inv, part in zip(invs, parts)]
        step *= 2
    for index, inv in enumerate(invs):
        at = slice(index * LANE, (index + 1) * LANE)
        high[at, at], low[at, at] = split(inv)
    step = LANE
    while step < size:
        for base in range(0, size, 2 * step):
            left = slice(base, base + step)
            right = slice(base + step, base + 2 * step)
            bh, bl = split(lower_ref[right, left])
            ah, al = high[left, left], low[left, left]
            part = mm(bh, ah) + (mm(bh, al) + mm(bl, ah))
            ph, pL = split(part)
            ch, cl = high[right, right], low[right, right]
            high[right, left], low[right, left] = split(-(mm(ch, ph) + (mm(ch, pL) + mm(cl, ph))))
        step *= 2


VM = pl.BlockSpec(memory_space=pltpu.VMEM)
SM = pl.BlockSpec(memory_space=pltpu.SMEM)


def invert_dense_kernel(first, lower_ref, high, low):
    invert_factor(lower_ref, high, low, first)


def invert_pieces_kernel(first, place_ref, p0, p1, p2, p3, high, low, lower):
    rows = p0.shape[0]
    planes = lower.shape[0] // (4 * rows)
    for k, piece in enumerate((p0, p1, p2, p3)):
        seat = place_ref[k]
        left = 0
        for plane in range(planes):
            width = 4 * rows * (plane + 1)
            at = pl.multiple_of((4 * plane + seat) * rows, 8)
            lower[pl.ds(at, rows), :width] = piece[:, left : left + width]
            left += width
    invert_factor(lower, high, low, first)


def invert_call(kernel, size, count, scratch):
    out = jax.ShapeDtypeStruct((size, size), BF16)
    return pl.pallas_call(
        kernel,
        out_shape=(out, out),
        in_specs=[SM] * (count > 1) + [VM] * count,
        out_specs=(VM, VM),
        scratch_shapes=scratch,
        name="invert_factor",
    )


def apply_panel(raw, high, low, pt_ref, qh_ref, ql_ref):
    size = high.shape[0]
    span = min(256, size)
    nt = ((1,), (1,))
    for top in range(0, size, span):
        end = top + span
        value = mm(raw[:, :end], high[top:end, :end], nt) + mm(raw[:, :end], low[top:end, :end], nt)
        pt_ref[:, top:end] = value.astype(BF16)
    for top in range(0, size, span):
        end = top + span
        part = pt_ref[:, top:]
        value = mm(part, high[top:, top:end]) + mm(part, low[top:, top:end])
        qh_ref[:, top:end], ql_ref[:, top:end] = split(value)


def apply_dense_kernel(panel_ref, high, low, pt_ref, qh_ref, ql_ref):
    apply_panel(panel_ref[...].astype(F32).T.astype(BF16), high, low, pt_ref, qh_ref, ql_ref)


def apply_pieces_kernel(row_ref, p0, p1, p2, p3, high, low, pt_ref, qh_ref, ql_ref, panel):
    count, rows, _ = p0.shape
    for k, piece in enumerate((p0, p1, p2, p3)):
        for z in range(count):
            at = pl.multiple_of(row_ref[k * count + z], 8)
            panel[pl.ds(at, rows), :] = piece[z].astype(F32)
    apply_panel(panel[...].T.astype(BF16), high, low, pt_ref, qh_ref, ql_ref)


def apply_call(kernel, size, width, count, scratch):
    out = jax.ShapeDtypeStruct((width, size), BF16)
    return pl.pallas_call(
        kernel,
        out_shape=(out, out, out),
        in_specs=[SM] * (count > 1) + [VM] * (count + 2),
        out_specs=(VM, VM, VM),
        scratch_shapes=scratch,
        name="apply_panel",
    )


def block_kernel(a_ref, b_ref, out_ref):
    nt = ((1,), (1,))
    out_ref[...] = mm(a_ref[...], a_ref[...], nt) + mm(b_ref[...], b_ref[...], nt)


def normals_kernel(info, own, far, qoh, qol, qfh, qfl, inv_ref, reg_ref, out_ref, acc, invs):
    block, arc = pl.program_id(0), pl.program_id(1)
    arcs = pl.num_programs(1)
    near = qoh.shape[0]
    size, span = acc.shape
    half = size // 2

    @pl.when((block == 0) & (arc == 0))
    def _():
        invs[0], invs[1] = split(inv_ref[...])

    @pl.when(arc == 0)
    def _():
        acc[...] = jnp.zeros_like(acc)

    live = info[2 + block * arcs + arc] > 0

    @pl.when(live & (arc < near))
    def _():
        data = own[0]
        at = jnp.minimum(arc, near - 1)
        acc[...] += mm(qoh[at], data) + mm(qol[at], data)

    @pl.when(live & (arc >= near))
    def _():
        data = far[0]
        at = jnp.maximum(arc - near, 0)
        acc[...] += mm(qfh[at], data) + mm(qfl[at], data)

    @pl.when(arc == arcs - 1)
    def _():
        row = lax.broadcasted_iota(jnp.int32, (size, span), 0)
        col = lax.broadcasted_iota(jnp.int32, (size, span), 1)
        hit = row + info[1] == col + block * span
        total = acc[...] + jnp.where(hit, reg_ref[...], 0.0)
        th, tl = split(total)
        for top, end in ((0, half), (half, size)):
            ih, il = invs[0, top:end, :end], invs[1, top:end, :end]
            out_ref[top:end, :] = mm(ih, th[:end]) + (mm(ih, tl[:end]) + mm(il, th[:end]))


def normals_call(info, own, far, qs, inverse, reg):
    near, size, _ = own.shape
    arcs = 2 * near
    share = far.shape[2]
    width = inverse.shape[0]
    whole = pl.BlockSpec((near, width, size), lambda b, a, s: (0, 0, 0), pipeline_mode=pl.Buffered(1))
    return pl.pallas_call(
        normals_kernel,
        out_shape=jax.ShapeDtypeStruct((width, share), F32),
        grid_spec=pltpu.PrefetchScalarGridSpec(
            num_scalar_prefetch=1,
            grid=(share // BLK, arcs),
            in_specs=[
                pl.BlockSpec((1, size, BLK), lambda b, a, s: (jnp.minimum(a, near - 1), 0, s[0] + b)),
                pl.BlockSpec((1, size, BLK), lambda b, a, s: (jnp.maximum(a - near, 0), 0, b)),
                whole,
                whole,
                whole,
                whole,
                pl.BlockSpec((width, width), lambda b, a, s: (0, 0), pipeline_mode=pl.Buffered(1)),
                pl.BlockSpec((1, BLK), lambda b, a, s: (0, b)),
            ],
            out_specs=pl.BlockSpec((width, BLK), lambda b, a, s: (0, b)),
            scratch_shapes=[pltpu.VMEM((width, BLK), F32), pltpu.VMEM((2, width, width), BF16)],
        ),
        name="normals",
    )(info, own, far, *qs, inverse, reg)

SUB = 8


def three(value):
    high = value.astype(BF16)
    rest = value - high.astype(F32)
    mid = rest.astype(BF16)
    return high, mid, (rest - mid.astype(F32)).astype(BF16)


def factor_diag(work):
    tn = ((0,), (0,))
    wide = work.shape[1]
    for top in range(0, LANE, SUB):
        rows = [work[top + i : top + i + 1, :] for i in range(SUB)]
        e = {}
        for j in range(SUB):
            for i in range(j, SUB):
                at = top + i
                e[j, i] = jnp.broadcast_to(rows[j][:, at : at + 1], (1, LANE))
        for j in range(SUB):
            inv = lax.rsqrt(e[j, j])
            inv2 = jnp.concatenate([inv] * (wide // LANE), axis=1)
            rows[j] = rows[j] * inv2
            for i in range(j + 1, SUB):
                e[j, i] = e[j, i] * inv
            for i in range(j + 1, SUB):
                for k in range(i, SUB):
                    e[i, k] = e[i, k] - e[j, i] * e[j, k]
                coef = jnp.concatenate([e[j, i]] * (wide // LANE), axis=1)
                rows[i] = rows[i] - coef * rows[j]
        part = jnp.concatenate(rows, axis=0)
        work[top : top + SUB, :] = part
        end = top + SUB
        if end < LANE:
            h, m, l = three(part)
            lhs = jnp.concatenate([h, h, m, m, h, l], axis=0)[:, :LANE]
            rhs = jnp.concatenate([h, m, h, m, l, h], axis=0)
            gone = mm(lhs, rhs, tn)
            work[end:, :] = work[end:, :] - gone[end:, :]


def chol_kernel(block_ref, reg_ref, out_ref, full, work, upper):
    size = block_ref.shape[0]
    row = lax.broadcasted_iota(jnp.int32, (size, size), 0)
    col = lax.broadcasted_iota(jnp.int32, (size, size), 1)
    full[...] = block_ref[...] + jnp.where(row == col, reg_ref[...], 0.0)
    r1 = lax.broadcasted_iota(jnp.int32, (LANE, LANE), 0)
    c1 = lax.broadcasted_iota(jnp.int32, (LANE, LANE), 1)
    out_ref[...] = jnp.zeros(out_ref.shape, F32)
    for top in range(0, size, LANE):
        end = top + LANE
        work[:, :LANE] = full[top:end, top:end]
        work[:, LANE:] = (r1 == c1).astype(F32)
        factor_diag(work)
        inverse = jnp.where(r1 >= c1, work[:, LANE:], 0.0)
        out_ref[top:end, top:end] = inverse
        if end < size:
            right = mm3(inverse, full[top:end, end:])
            upper[top:end, end:] = right
            rt = right.T
            full[end:, end:] = full[end:, end:] - mm3(rt, right)
    step = LANE
    while step < size:
        for base in range(0, size, 2 * step):
            left = slice(base, base + step)
            second = slice(base + step, base + 2 * step)
            low = upper[left, second].T
            out_ref[second, left] = -mm3(out_ref[second, second], mm3(low, out_ref[left, left]))
        step *= 2


def chol_inverse(block, reg):
    size = block.shape[0]
    vm = pl.BlockSpec(memory_space=pltpu.VMEM)
    return pl.pallas_call(
        chol_kernel,
        out_shape=jax.ShapeDtypeStruct((size, size), F32),
        in_specs=[vm, vm],
        out_specs=vm,
        scratch_shapes=[
            pltpu.VMEM((size, size), F32),
            pltpu.VMEM((LANE, 2 * LANE), F32),
            pltpu.VMEM((size, size), F32),
        ],
        name="chol_inverse",
    )(block, reg)


def block_hits(active, first, count):
    ids = first + jnp.arange(count, dtype=jnp.int32)
    return jnp.any(active[:, :, None] == ids[None, None, :], axis=1)


def general(design, cov_factor, active_blocks, panel_index, reg_diag):
    arcs, observed, columns = design.shape
    rows = cov_factor.shape[1]
    par_id = lax.axis_index("par")
    arc_id = lax.axis_index("arc")
    strip_at = par_id * rows // LANE * LANE
    strip = lax.dynamic_slice_in_dim(cov_factor, strip_at, LANE, 2)
    strip = invert_diag(strip, (par_id * rows % LANE).astype(jnp.int32)[None])
    lower = lax.dynamic_update_slice_in_dim(cov_factor, strip, strip_at, 2)
    lower = lax.all_gather(lower, "par", axis=1, tiled=True)
    local_blocks = columns // BLK
    hits = block_hits(active_blocks, par_id * local_blocks, local_blocks)
    masked = design * jnp.repeat(hits, BLK, axis=1).astype(BF16)[:, None, :]
    start = panel_index[0] * PANEL
    padded = jnp.pad(masked, ((0, 0), (0, 0), (PANEL, PANEL)))
    window = lax.dynamic_slice_in_dim(
        padded, jnp.clip(start - par_id * columns + PANEL, 0, columns + PANEL), PANEL, 2
    )
    panel = lax.psum(window.astype(F32).astype(BF16), "par")
    gram, block = 0.0, 0.0
    for arc in range(arcs):
        high, low = invert_call(functools.partial(invert_dense_kernel, rows), observed, 1, [])(lower[arc])
        pt, qh, ql = apply_call(apply_dense_kernel, observed, PANEL, 1, [])(panel[arc], high, low)
        gram += jnp.dot(qh, masked[arc], preferred_element_type=F32)
        gram += jnp.dot(ql, masked[arc], preferred_element_type=F32)
        block += lax.dot_general(pt, pt, (((1,), (1,)), ((), ())), preferred_element_type=F32)
    share = columns // lax.axis_size("arc")
    gram, block = lax.psum((gram, block), "arc")
    gram = lax.dynamic_slice_in_dim(gram, arc_id * share, share, 1)
    reg_panel = lax.dynamic_slice_in_dim(reg_diag, start, PANEL)
    inverse = chol_inverse(block, reg_panel[None, :])
    global_cols = par_id * columns + arc_id * share + jnp.arange(share, dtype=jnp.int32)
    rows_at = start + jnp.arange(PANEL, dtype=jnp.int32)
    shifted = gram + jnp.where(global_cols[None, :] == rows_at[:, None], reg_panel[:, None], 0.0)
    return jnp.dot(inverse, shifted, precision=lax.Precision.HIGHEST, preferred_element_type=F32)


def solution(mesh):
    in_specs = (P("arc", None, "par"), P("arc", "par", None), P("arc", None), P(), P())
    out_specs = P(None, ("par", "arc"))
    return jax.shard_map(
        general, mesh=mesh, in_specs=in_specs, out_specs=out_specs, check_vma=False
    )
```

```python
import functools

import jax
import jax.numpy as jnp
from jax import lax
from jax.experimental import pallas as pl
from jax.experimental.pallas import tpu as pltpu
from jax.sharding import PartitionSpec as P

PANEL = 512
BLK = 256
F32, BF16 = jnp.float32, jnp.bfloat16
LANE = 128


def split(value):
    high = value.astype(BF16)
    return high, (value - high.astype(F32)).astype(BF16)


def mm(a, b, dims=((1,), (0,))):
    return lax.dot_general(a, b, (dims, ((), ())), preferred_element_type=F32)


def mm3(a, b):
    ah, al = split(a)
    bh, bl = split(b)
    return mm(ah, bh) + (mm(ah, bl) + mm(al, bh))


def level_mask(step):
    rows = lax.broadcasted_iota(jnp.int32, (LANE, LANE), 0)
    cols = lax.broadcasted_iota(jnp.int32, (LANE, LANE), 1)
    return (
        (rows // (2 * step) == cols // (2 * step))
        & ((rows // step) % 2 == 1)
        & ((cols // step) % 2 == 0)
    )


def invert_levels(inverse, lower, first, last):
    step = first
    while step < last:
        below = jnp.where(level_mask(step), lower, 0.0)
        inverse = inverse - mm3(inverse, mm3(below, inverse))
        step *= 2
    return inverse


def diag_kernel(off_ref, strip_ref, out_ref, square):
    arcs, rows, _ = strip_ref.shape
    off = pl.multiple_of(off_ref[0], 8)
    r = lax.broadcasted_iota(jnp.int32, (LANE, LANE), 0)
    c = lax.broadcasted_iota(jnp.int32, (LANE, LANE), 1)
    eye = r == c
    sub = lax.broadcasted_iota(jnp.int32, (rows, LANE), 1)
    own = (sub >= off) & (sub < off + rows)
    for arc in range(arcs):
        square[arc] = eye.astype(F32)
        square[arc, pl.ds(off, rows), :] = jnp.where(own, strip_ref[arc], 0.0)
    lowers = [square[arc] for arc in range(arcs)]
    invs = [jnp.where(eye, 1.0 / jnp.where(eye, low, 1.0), 0.0) for low in lowers]
    step = 1
    while step < rows:
        mask = level_mask(step)
        parts = [mm3(jnp.where(mask, low, 0.0), inv) for low, inv in zip(lowers, invs)]
        invs = [inv - mm3(inv, part) for inv, part in zip(invs, parts)]
        step *= 2
    for arc in range(arcs):
        square[arc] = invs[arc]
        out_ref[arc] = jnp.where(own, square[arc, pl.ds(off, rows), :], strip_ref[arc])


def invert_diag(strip, off):
    arcs, rows, _ = strip.shape
    return pl.pallas_call(
        diag_kernel,
        out_shape=jax.ShapeDtypeStruct(strip.shape, F32),
        in_specs=[pl.BlockSpec(memory_space=pltpu.SMEM), pl.BlockSpec(memory_space=pltpu.VMEM)],
        out_specs=pl.BlockSpec(memory_space=pltpu.VMEM),
        scratch_shapes=[pltpu.VMEM((arcs, LANE, LANE), F32)],
        name="invert_diag",
    )(off, strip)


def invert_factor(lower_ref, high, low, first):
    size = high.shape[0]
    span = max(size // 2, LANE)
    for top in range(0, size, span):
        for ref in (high, low):
            ref[top : top + span, top : top + span] = jnp.zeros((span, span), BF16)
    rows = lax.broadcasted_iota(jnp.int32, (LANE, LANE), 0) // first
    cols = lax.broadcasted_iota(jnp.int32, (LANE, LANE), 1) // first
    blocks = [lower_ref[t : t + LANE, t : t + LANE] for t in range(0, size, LANE)]
    invs = [jnp.where(rows == cols, block, 0.0) for block in blocks]
    step = first
    while step < LANE:
        mask = level_mask(step)
        parts = [mm3(jnp.where(mask, block, 0.0), inv) for block, inv in zip(blocks, invs)]
        invs = [inv - mm3(inv, part) for inv, part in zip(invs, parts)]
        step *= 2
    for index, inv in enumerate(invs):
        at = slice(index * LANE, (index + 1) * LANE)
        high[at, at], low[at, at] = split(inv)
    step = LANE
    while step < size:
        for base in range(0, size, 2 * step):
            left = slice(base, base + step)
            right = slice(base + step, base + 2 * step)
            bh, bl = split(lower_ref[right, left])
            ah, al = high[left, left], low[left, left]
            part = mm(bh, ah) + (mm(bh, al) + mm(bl, ah))
            ph, pL = split(part)
            ch, cl = high[right, right], low[right, right]
            high[right, left], low[right, left] = split(-(mm(ch, ph) + (mm(ch, pL) + mm(cl, ph))))
        step *= 2


VM = pl.BlockSpec(memory_space=pltpu.VMEM)
SM = pl.BlockSpec(memory_space=pltpu.SMEM)


def invert_dense_kernel(first, lower_ref, high, low):
    invert_factor(lower_ref, high, low, first)


def invert_pieces_kernel(first, place_ref, p0, p1, p2, p3, high, low, lower):
    rows = p0.shape[0]
    planes = lower.shape[0] // (4 * rows)
    for k, piece in enumerate((p0, p1, p2, p3)):
        seat = place_ref[k]
        left = 0
        for plane in range(planes):
            width = 4 * rows * (plane + 1)
            at = pl.multiple_of((4 * plane + seat) * rows, 8)
            lower[pl.ds(at, rows), :width] = piece[:, left : left + width]
            left += width
    invert_factor(lower, high, low, first)


def invert_call(kernel, size, count, scratch):
    out = jax.ShapeDtypeStruct((size, size), BF16)
    return pl.pallas_call(
        kernel,
        out_shape=(out, out),
        in_specs=[SM] * (count > 1) + [VM] * count,
        out_specs=(VM, VM),
        scratch_shapes=scratch,
        name="invert_factor",
    )


def apply_panel(raw, high, low, pt_ref, qh_ref, ql_ref):
    size = high.shape[0]
    span = min(256, size)
    nt = ((1,), (1,))
    for top in range(0, size, span):
        end = top + span
        value = mm(raw[:, :end], high[top:end, :end], nt) + mm(raw[:, :end], low[top:end, :end], nt)
        pt_ref[:, top:end] = value.astype(BF16)
    for top in range(0, size, span):
        end = top + span
        part = pt_ref[:, top:]
        value = mm(part, high[top:, top:end]) + mm(part, low[top:, top:end])
        qh_ref[:, top:end], ql_ref[:, top:end] = split(value)


def apply_dense_kernel(panel_ref, high, low, pt_ref, qh_ref, ql_ref):
    apply_panel(panel_ref[...].astype(F32).T.astype(BF16), high, low, pt_ref, qh_ref, ql_ref)


def apply_pieces_kernel(row_ref, p0, p1, p2, p3, high, low, pt_ref, qh_ref, ql_ref, panel):
    count, rows, _ = p0.shape
    for k, piece in enumerate((p0, p1, p2, p3)):
        for z in range(count):
            at = pl.multiple_of(row_ref[k * count + z], 8)
            panel[pl.ds(at, rows), :] = piece[z].astype(F32)
    apply_panel(panel[...].T.astype(BF16), high, low, pt_ref, qh_ref, ql_ref)


def apply_call(kernel, size, width, count, scratch):
    out = jax.ShapeDtypeStruct((width, size), BF16)
    return pl.pallas_call(
        kernel,
        out_shape=(out, out, out),
        in_specs=[SM] * (count > 1) + [VM] * (count + 2),
        out_specs=(VM, VM, VM),
        scratch_shapes=scratch,
        name="apply_panel",
    )


def block_kernel(a_ref, b_ref, out_ref):
    nt = ((1,), (1,))
    out_ref[...] = mm(a_ref[...], a_ref[...], nt) + mm(b_ref[...], b_ref[...], nt)


def normals_kernel(info, own, far, *refs):
    arcs = pl.num_programs(1)
    count = (len(refs) - 5) // 2
    qs = refs[: 2 * count]
    inv_ref, reg_ref, out_ref, acc, invs = refs[2 * count :]
    block, arc = pl.program_id(0), pl.program_id(1)
    size, span = acc.shape
    half = size // 2

    @pl.when((block == 0) & (arc == 0))
    def _():
        invs[0], invs[1] = split(inv_ref[...])

    @pl.when(arc == 0)
    def _():
        acc[...] = jnp.zeros_like(acc)

    live = info[2 + block * arcs + arc] > 0
    for index in range(count):

        @pl.when(live & (arc == index))
        def _():
            data = own[0] if index < count // 2 else far[0]
            acc[...] += mm(qs[2 * index][...], data) + mm(qs[2 * index + 1][...], data)

    @pl.when(arc == arcs - 1)
    def _():
        row = lax.broadcasted_iota(jnp.int32, (size, span), 0)
        col = lax.broadcasted_iota(jnp.int32, (size, span), 1)
        hit = row + info[1] == col + block * span
        total = acc[...] + jnp.where(hit, reg_ref[...], 0.0)
        th, tl = split(total)
        for top, end in ((0, half), (half, size)):
            ih, il = invs[0, top:end, :end], invs[1, top:end, :end]
            out_ref[top:end, :] = mm(ih, th[:end]) + (mm(ih, tl[:end]) + mm(il, th[:end]))


def normals_call(info, own, far, qs, inverse, reg):
    near, size, _ = own.shape
    arcs = 2 * near
    share = far.shape[2]
    width = inverse.shape[0]

    def fixed(shape):
        return pl.BlockSpec(shape, lambda b, a, s: (0, 0), pipeline_mode=pl.Buffered(1))

    return pl.pallas_call(
        normals_kernel,
        out_shape=jax.ShapeDtypeStruct((width, share), F32),
        grid_spec=pltpu.PrefetchScalarGridSpec(
            num_scalar_prefetch=1,
            grid=(share // BLK, arcs),
            in_specs=[
                pl.BlockSpec((1, size, BLK), lambda b, a, s: (jnp.minimum(a, near - 1), 0, s[0] + b)),
                pl.BlockSpec((1, size, BLK), lambda b, a, s: (jnp.maximum(a - near, 0), 0, b)),
            ]
            + [fixed((width, size))] * len(qs)
            + [fixed((width, width)), pl.BlockSpec((1, BLK), lambda b, a, s: (0, b))],
            out_specs=pl.BlockSpec((width, BLK), lambda b, a, s: (0, b)),
            scratch_shapes=[pltpu.VMEM((width, BLK), F32), pltpu.VMEM((2, width, width), BF16)],
        ),
        name="normals",
    )(info, own, far, *qs, inverse, reg)
SUB = 8


def three(value):
    high = value.astype(BF16)
    rest = value - high.astype(F32)
    mid = rest.astype(BF16)
    return high, mid, (rest - mid.astype(F32)).astype(BF16)


def factor_diag(work):
    tn = ((0,), (0,))
    wide = work.shape[1]
    for top in range(0, LANE, SUB):
        rows = [work[top + i : top + i + 1, :] for i in range(SUB)]
        e = {}
        for j in range(SUB):
            for i in range(j, SUB):
                at = top + i
                e[j, i] = jnp.broadcast_to(rows[j][:, at : at + 1], (1, LANE))
        for j in range(SUB):
            inv = lax.rsqrt(e[j, j])
            inv2 = jnp.concatenate([inv] * (wide // LANE), axis=1)
            rows[j] = rows[j] * inv2
            for i in range(j + 1, SUB):
                e[j, i] = e[j, i] * inv
            for i in range(j + 1, SUB):
                for k in range(i, SUB):
                    e[i, k] = e[i, k] - e[j, i] * e[j, k]
                coef = jnp.concatenate([e[j, i]] * (wide // LANE), axis=1)
                rows[i] = rows[i] - coef * rows[j]
        part = jnp.concatenate(rows, axis=0)
        work[top : top + SUB, :] = part
        end = top + SUB
        if end < LANE:
            h, m, l = three(part)
            lhs = jnp.concatenate([h, h, m, m, h, l], axis=0)[:, :LANE]
            rhs = jnp.concatenate([h, m, h, m, l, h], axis=0)
            gone = mm(lhs, rhs, tn)
            work[end:, :] = work[end:, :] - gone[end:, :]


def chol_kernel(block_ref, reg_ref, out_ref, full, work, upper):
    size = block_ref.shape[0]
    row = lax.broadcasted_iota(jnp.int32, (size, size), 0)
    col = lax.broadcasted_iota(jnp.int32, (size, size), 1)
    full[...] = block_ref[...] + jnp.where(row == col, reg_ref[...], 0.0)
    r1 = lax.broadcasted_iota(jnp.int32, (LANE, LANE), 0)
    c1 = lax.broadcasted_iota(jnp.int32, (LANE, LANE), 1)
    out_ref[...] = jnp.zeros(out_ref.shape, F32)
    for top in range(0, size, LANE):
        end = top + LANE
        work[:, :LANE] = full[top:end, top:end]
        work[:, LANE:] = (r1 == c1).astype(F32)
        factor_diag(work)
        inverse = jnp.where(r1 >= c1, work[:, LANE:], 0.0)
        out_ref[top:end, top:end] = inverse
        if end < size:
            right = mm3(inverse, full[top:end, end:])
            upper[top:end, end:] = right
            rt = right.T
            full[end:, end:] = full[end:, end:] - mm3(rt, right)
    step = LANE
    while step < size:
        for base in range(0, size, 2 * step):
            left = slice(base, base + step)
            second = slice(base + step, base + 2 * step)
            low = upper[left, second].T
            out_ref[second, left] = -mm3(out_ref[second, second], mm3(low, out_ref[left, left]))
        step *= 2


def chol_inverse(block, reg):
    size = block.shape[0]
    vm = pl.BlockSpec(memory_space=pltpu.VMEM)
    return pl.pallas_call(
        chol_kernel,
        out_shape=jax.ShapeDtypeStruct((size, size), F32),
        in_specs=[vm, vm],
        out_specs=vm,
        scratch_shapes=[
            pltpu.VMEM((size, size), F32),
            pltpu.VMEM((LANE, 2 * LANE), F32),
            pltpu.VMEM((size, size), F32),
        ],
        name="chol_inverse",
    )(block, reg)


def block_hits(active, first, count):
    ids = first + jnp.arange(count, dtype=jnp.int32)
    return jnp.any(active[:, :, None] == ids[None, None, :], axis=1)


def general(design, cov_factor, active_blocks, panel_index, reg_diag):
    arcs, observed, columns = design.shape
    rows = cov_factor.shape[1]
    par_id = lax.axis_index("par")
    arc_id = lax.axis_index("arc")
    strip_at = par_id * rows // LANE * LANE
    strip = lax.dynamic_slice_in_dim(cov_factor, strip_at, LANE, 2)
    strip = invert_diag(strip, (par_id * rows % LANE).astype(jnp.int32)[None])
    lower = lax.dynamic_update_slice_in_dim(cov_factor, strip, strip_at, 2)
    lower = lax.all_gather(lower, "par", axis=1, tiled=True)
    local_blocks = columns // BLK
    hits = block_hits(active_blocks, par_id * local_blocks, local_blocks)
    masked = design * jnp.repeat(hits, BLK, axis=1).astype(BF16)[:, None, :]
    start = panel_index[0] * PANEL
    padded = jnp.pad(masked, ((0, 0), (0, 0), (PANEL, PANEL)))
    window = lax.dynamic_slice_in_dim(
        padded, jnp.clip(start - par_id * columns + PANEL, 0, columns + PANEL), PANEL, 2
    )
    panel = lax.psum(window.astype(F32).astype(BF16), "par")
    gram, block = 0.0, 0.0
    for arc in range(arcs):
        high, low = invert_call(functools.partial(invert_dense_kernel, rows), observed, 1, [])(lower[arc])
        pt, qh, ql = apply_call(apply_dense_kernel, observed, PANEL, 1, [])(panel[arc], high, low)
        gram += jnp.dot(qh, masked[arc], preferred_element_type=F32)
        gram += jnp.dot(ql, masked[arc], preferred_element_type=F32)
        block += lax.dot_general(pt, pt, (((1,), (1,)), ((), ())), preferred_element_type=F32)
    share = columns // lax.axis_size("arc")
    gram, block = lax.psum((gram, block), "arc")
    gram = lax.dynamic_slice_in_dim(gram, arc_id * share, share, 1)
    reg_panel = lax.dynamic_slice_in_dim(reg_diag, start, PANEL)
    inverse = chol_inverse(block, reg_panel[None, :])
    global_cols = par_id * columns + arc_id * share + jnp.arange(share, dtype=jnp.int32)
    rows_at = start + jnp.arange(PANEL, dtype=jnp.int32)
    shifted = gram + jnp.where(global_cols[None, :] == rows_at[:, None], reg_panel[:, None], 0.0)
    return jnp.dot(inverse, shifted, precision=lax.Precision.HIGHEST, preferred_element_type=F32)

def paired(design, cov_factor, active_blocks, panel_index, reg_diag):
    arcs, observed, columns = design.shape
    rows = cov_factor.shape[1]
    chips = lax.axis_size("par")
    planes = chips // 4
    me = lax.axis_index("par")
    core = lax.axis_index("arc")
    sides = (me & 1, (me >> 1) & 1)
    plane = me >> 2
    share = columns // 2
    local_blocks = columns // BLK
    start = panel_index[0] * PANEL

    def swap(value):
        return lax.ppermute(value, "arc", [(0, 1), (1, 0)])

    def hop(value, bits):
        return lax.ppermute(value, "par", [(p, p ^ bits) for p in range(chips)])

    def part(value, index, size):
        return lax.dynamic_slice_in_dim(value, index * size, size, 0)

    offset = start - me * columns
    inside = (offset >= 0) & (offset < columns)
    live = block_hits(active_blocks, start // BLK, PANEL // BLK) & inside
    window = lax.dynamic_slice_in_dim(design, jnp.clip(offset, 0, columns - PANEL), PANEL, 2)
    window = jnp.where(jnp.repeat(live, BLK, axis=1)[:, None, :], window, 0)

    seeds = []
    for arc in range(arcs):
        value = window[arc]
        for axis in (arc % 2, 1 - arc % 2):
            half = value.shape[0] // 2
            gone = hop(part(value, 1 - sides[axis], half), 1 << axis)
            value = part(value, sides[axis], half) + gone
        seeds.append(value.reshape(planes, rows, PANEL))
    seeds = jnp.stack(seeds, axis=1)
    chunk = lax.dynamic_index_in_dim(seeds, plane, 0, False)
    for k in range(1, planes):
        chunk += hop(lax.dynamic_index_in_dim(seeds, plane ^ k, 0, False), 4 * k)

    strip_at = me * rows // LANE * LANE
    strip = lax.dynamic_slice_in_dim(cov_factor, strip_at, LANE, 2)
    strip = invert_diag(strip, (me * rows % LANE).astype(jnp.int32)[None])
    lower = lax.dynamic_update_slice_in_dim(cov_factor, strip, strip_at, 2)
    stack = [lower] + [hop(lower, 4 * k) for k in range(1, planes)]
    packed = []
    for index in range(planes):
        width = 4 * rows * (index + 1)
        value = stack[0][:, :, :width]
        for k in range(1, planes):
            value = jnp.where(plane == (index ^ k), stack[k][:, :, :width], value)
        packed.append(value)
    packed = jnp.concatenate(packed, axis=2)

    def spread(value, first):
        second = 3 - first
        direct = hop(value, first)
        return {0: value, first: direct, second: hop(value, second), 3: hop(direct, second)}

    seats = (me & 3) ^ jnp.arange(4, dtype=jnp.int32)
    inverses = []
    for arc in range(arcs):
        pieces = spread(packed[arc], 1 + arc % 2)
        call = invert_call(
            functools.partial(invert_pieces_kernel, rows), observed, 4,
            [pltpu.VMEM((observed, observed), F32)],
        )
        inverses.append(call(seats, *[pieces[k] for k in range(4)]))

    grid = jnp.arange(4, dtype=jnp.int32)[:, None] ^ (4 * jnp.arange(planes, dtype=jnp.int32)[None, :])
    solved = []
    for arc in range(arcs):
        source = me ^ (grid if arc % 2 == 0 else grid.T)
        low_bit, high_bit = source & 1, (source >> 1) & 1
        if arc % 2:
            low_bit, high_bit = high_bit, low_bit
        place = ((low_bit * 2 + high_bit) * planes + (source >> 2)) * rows
        if arc % 2 == 0:
            value = jnp.stack([chunk[arc]] + [hop(chunk[arc], 4 * k) for k in range(1, planes)])
            pieces = spread(value, 1)
        else:
            pieces = spread(chunk[arc], 2)
            value = jnp.stack([pieces[k] for k in range(4)])
            pieces = [value] + [hop(value, 4 * k) for k in range(1, planes)]
        pieces = [pieces[k] for k in range(len(pieces))]
        call = apply_call(
            apply_pieces_kernel, observed, PANEL, len(pieces), [pltpu.VMEM((observed, PANEL), F32)]
        )
        solved.append(call(place.reshape(-1), *pieces, *inverses[arc]))

    block = pl.pallas_call(
        block_kernel,
        out_shape=jax.ShapeDtypeStruct((PANEL, PANEL), F32),
        in_specs=[VM, VM],
        out_specs=VM,
        name="panel_block",
    )(solved[0][0], solved[1][0])
    block = block + swap(block)
    reg_panel = lax.dynamic_slice_in_dim(reg_diag, start, PANEL)
    inverse = chol_inverse(block, reg_panel[None, :])

    far = swap(lax.dynamic_slice_in_dim(design, (1 - core) * share, share, 2))
    near_qs = [q for arc in range(arcs) for q in solved[arc][1:]]
    far_qs = [swap(q) for q in near_qs]
    first = me * columns + core * share
    both = jnp.concatenate([active_blocks, swap(active_blocks)], axis=0)
    lives = block_hits(both, first // BLK, share // BLK).T.reshape(-1).astype(jnp.int32)
    info = jnp.concatenate([jnp.stack([core * (share // BLK), start - first]).astype(jnp.int32), lives])
    reg = lax.dynamic_slice_in_dim(reg_diag, first, share)[None, :]
    return normals_call(info, design, far, near_qs + far_qs, inverse, reg)


def whole(design, cov_factor, *rest):
    chips = lax.axis_size("par")
    columns = design.shape[2]
    fits = (
        lax.axis_size("arc") == 2
        and design.shape[0] == 2
        and chips == 16
        and columns % PANEL == 0
        and columns % (2 * BLK) == 0
        and LANE % cov_factor.shape[1] == 0
    )
    return (paired if fits else general)(design, cov_factor, *rest)


def solution(mesh):
    in_specs = (P("arc", None, "par"), P("arc", "par", None), P("arc", None), P(), P())
    out_specs = P(None, ("par", "arc"))
    return jax.shard_map(
        whole, mesh=mesh, in_specs=in_specs, out_specs=out_specs, check_vma=False
    )
```

```python
import functools

import jax
import jax.numpy as jnp
from jax import lax
from jax.experimental import pallas as pl
from jax.experimental.pallas import tpu as pltpu
from jax.sharding import PartitionSpec as P

PANEL = 512
BLK = 256
F32, BF16 = jnp.float32, jnp.bfloat16
LANE = 128


def split(value):
    high = value.astype(BF16)
    return high, (value - high.astype(F32)).astype(BF16)


def mm(a, b, dims=((1,), (0,))):
    return lax.dot_general(a, b, (dims, ((), ())), preferred_element_type=F32)


def mm3(a, b):
    ah, al = split(a)
    bh, bl = split(b)
    return mm(ah, bh) + (mm(ah, bl) + mm(al, bh))


def level_mask(step):
    rows = lax.broadcasted_iota(jnp.int32, (LANE, LANE), 0)
    cols = lax.broadcasted_iota(jnp.int32, (LANE, LANE), 1)
    return (
        (rows // (2 * step) == cols // (2 * step))
        & ((rows // step) % 2 == 1)
        & ((cols // step) % 2 == 0)
    )


def invert_levels(inverse, lower, first, last):
    step = first
    while step < last:
        below = jnp.where(level_mask(step), lower, 0.0)
        inverse = inverse - mm3(inverse, mm3(below, inverse))
        step *= 2
    return inverse


def diag_kernel(off_ref, strip_ref, high, low, square):
    arcs, rows, _ = strip_ref.shape
    off = pl.multiple_of(off_ref[0], 8)
    r = lax.broadcasted_iota(jnp.int32, (LANE, LANE), 0)
    c = lax.broadcasted_iota(jnp.int32, (LANE, LANE), 1)
    eye = r == c
    sub = lax.broadcasted_iota(jnp.int32, (rows, LANE), 1)
    own = (sub >= off) & (sub < off + rows)
    for arc in range(arcs):
        square[arc] = eye.astype(F32)
        square[arc, pl.ds(off, rows), :] = jnp.where(own, strip_ref[arc], 0.0)
    lowers = [square[arc] for arc in range(arcs)]
    invs = [jnp.where(eye, 1.0 / jnp.where(eye, low, 1.0), 0.0) for low in lowers]
    step = 1
    while step < rows:
        mask = level_mask(step)
        parts = [mm3(jnp.where(mask, low, 0.0), inv) for low, inv in zip(lowers, invs)]
        invs = [inv - mm3(inv, part) for inv, part in zip(invs, parts)]
        step *= 2
    for arc in range(arcs):
        square[arc] = invs[arc]
        value = jnp.where(own, square[arc, pl.ds(off, rows), :], strip_ref[arc])
        high[arc], low[arc] = split(value)


def invert_diag(strip, off):
    arcs = strip.shape[0]
    out = jax.ShapeDtypeStruct(strip.shape, BF16)
    return pl.pallas_call(
        diag_kernel,
        out_shape=(out, out),
        in_specs=[pl.BlockSpec(memory_space=pltpu.SMEM), pl.BlockSpec(memory_space=pltpu.VMEM)],
        out_specs=(pl.BlockSpec(memory_space=pltpu.VMEM), pl.BlockSpec(memory_space=pltpu.VMEM)),
        scratch_shapes=[pltpu.VMEM((arcs, LANE, LANE), F32)],
        name="invert_diag",
    )(off, strip)


def invert_factor(rest, fine, high, low, first):
    size = high.shape[0]
    half = max(size // 2, LANE)
    for top in range(0, size, half):
        for ref in (high, low):
            ref[top : top + half, top : top + half] = jnp.zeros((half, half), BF16)
    rows = lax.broadcasted_iota(jnp.int32, (LANE, LANE), 0) // first
    cols = lax.broadcasted_iota(jnp.int32, (LANE, LANE), 1) // first
    blocks = [
        rest[t : t + LANE, t : t + LANE].astype(F32) + fine[t : t + LANE, :].astype(F32)
        for t in range(0, size, LANE)
    ]
    invs = [jnp.where(rows == cols, block, 0.0) for block in blocks]
    step = first
    while step < LANE:
        mask = level_mask(step)
        parts = [mm3(jnp.where(mask, block, 0.0), inv) for block, inv in zip(blocks, invs)]
        invs = [inv - mm3(inv, part) for inv, part in zip(invs, parts)]
        step *= 2
    for index, inv in enumerate(invs):
        at = slice(index * LANE, (index + 1) * LANE)
        high[at, at], low[at, at] = split(inv)
    step = LANE
    while step < size:
        for base in range(0, size, 2 * step):
            left = slice(base, base + step)
            right = slice(base + step, base + 2 * step)
            below = rest[right, left]
            ph, pl_ = split(mm(below, high[left, left]) + mm(below, low[left, left]))
            ch, cl = high[right, right], low[right, right]
            high[right, left], low[right, left] = split(-(mm(ch, ph) + (mm(ch, pl_) + mm(cl, ph))))
        step *= 2


VM = pl.BlockSpec(memory_space=pltpu.VMEM)
SM = pl.BlockSpec(memory_space=pltpu.SMEM)
MIB = 1 << 20


def grant(mib):
    return pltpu.CompilerParams(vmem_limit_bytes=mib * MIB)


def invert_dense_kernel(first, rows_ref, high, low):
    invert_factor(rows_ref.at[:, LANE:], rows_ref.at[:, :LANE], high, low, first)


def invert_pieces_kernel(first, place_ref, p0, p1, p2, p3, high, low, rest, fine):
    rows = p0.shape[0]
    planes = rest.shape[0] // (4 * rows)
    for k, piece in enumerate((p0, p1, p2, p3)):
        seat = place_ref[k]
        left = 0
        for plane in range(planes):
            width = 4 * rows * (plane + 1)
            at = pl.multiple_of((4 * plane + seat) * rows, 16)
            fine[pl.ds(at, rows), :] = piece[:, left : left + LANE]
            rest[pl.ds(at, rows), :width] = piece[:, left + LANE : left + LANE + width]
            left += LANE + width
    invert_factor(rest, fine, high, low, first)


def invert_call(kernel, size, count, scratch):
    out = jax.ShapeDtypeStruct((size, size), BF16)
    return pl.pallas_call(
        kernel,
        out_shape=(out, out),
        in_specs=[SM] * (count > 1) + [VM] * count,
        out_specs=(VM, VM),
        scratch_shapes=scratch,
        compiler_params=grant(20),
        name="invert_factor",
    )


def apply_panel(raw, high, low, pt, q_ref):
    width, size = pt.shape
    span = min(256, size)
    nt = ((1,), (1,))
    for top in range(0, size, span):
        end = top + span
        value = mm(raw[:, :end], high[top:end, :end], nt) + mm(raw[:, :end], low[top:end, :end], nt)
        pt[:, top:end] = value.astype(BF16)
    for top in range(0, size, span):
        end = top + span
        part = pt[:, top:]
        value = mm(part, high[top:, top:end]) + mm(part, low[top:, top:end])
        q_ref[:width, top:end], q_ref[width:, top:end] = split(value)


def apply_kernel(arcs, place_ref, *refs):
    count = (len(refs) - 4) // arcs - 2
    pieces = refs[: arcs * count]
    factors = refs[arcs * count : arcs * (count + 2)]
    q_ref, block_ref, panel, pt = refs[arcs * (count + 2) :]
    nt = ((1,), (1,))
    for arc in range(arcs):
        index = arc * pieces[0].shape[0] * count
        for piece in pieces[arc * count : (arc + 1) * count]:
            rows = piece.shape[1]
            for z in range(piece.shape[0]):
                at = pl.multiple_of(place_ref[index], 16)
                panel[pl.ds(at, rows), :] = piece[z].astype(F32)
                index += 1
        raw = panel[...].T.astype(BF16)
        apply_panel(raw, factors[2 * arc], factors[2 * arc + 1], pt, q_ref.at[arc])
        part = mm(pt[...], pt[...], nt)
        block_ref[...] = part if arc == 0 else block_ref[...] + part


def apply_call(place, pieces, factors):
    arcs = len(factors) // 2
    size = factors[0].shape[0]
    width = pieces[0].shape[2]
    return pl.pallas_call(
        functools.partial(apply_kernel, arcs),
        out_shape=(
            jax.ShapeDtypeStruct((arcs, 2 * width, size), BF16),
            jax.ShapeDtypeStruct((width, width), F32),
        ),
        in_specs=[SM] + [VM] * (len(pieces) + len(factors)),
        out_specs=(VM, VM),
        scratch_shapes=[pltpu.VMEM((size, width), F32), pltpu.VMEM((width, size), BF16)],
        compiler_params=grant(32),
        name="apply_panel",
    )(place, *pieces, *factors)


def normals_kernel(info, own, far, qown, qfar, inv_ref, reg_ref, out_ref, data, qs, acc, sems):
    near = own.shape[0]
    arcs = 2 * near
    size, share = acc.shape
    blocks = share // BLK
    half = size // 2
    left = pl.multiple_of(info[0] * BLK, BLK)
    copies = []
    for arc in range(arcs):
        if arc < near:
            source, q = own.at[arc, :, pl.ds(left, share)], qown.at[arc]
        else:
            source, q = far.at[arc - near], qfar.at[arc - near]
        pair = (
            pltpu.make_async_copy(q, qs.at[arc], sems.at[2 * arc]),
            pltpu.make_async_copy(source, data.at[arc], sems.at[2 * arc + 1]),
        )
        for copy in pair:
            copy.start()
        copies.append(pair)
    acc[...] = jnp.zeros_like(acc)
    for arc in range(arcs):
        for copy in copies[arc]:
            copy.wait()

        def add(block, _):
            @pl.when(info[2 + block * arcs + arc] > 0)
            def _():
                at = pl.ds(pl.multiple_of(block * BLK, BLK), BLK)
                both = mm(qs[arc], data[arc, :, at])
                acc[:, at] += both[:size] + both[size:]

            return 0

        lax.fori_loop(0, blocks, add, 0)
    ih, il = split(inv_ref[...])
    row = lax.broadcasted_iota(jnp.int32, (size, BLK), 0) + info[1]
    col = lax.broadcasted_iota(jnp.int32, (size, BLK), 1)
    for block in range(blocks):
        at = slice(block * BLK, (block + 1) * BLK)
        hit = row == col + block * BLK
        th, tl = split(acc[:, at] + jnp.where(hit, reg_ref[:, at], 0.0))
        for top, end in ((0, half), (half, size)):
            value = mm(ih[top:end, :end], th[:end]) + mm(ih[top:end, :end], tl[:end])
            out_ref[top:end, at] = value + mm(il[top:end, :end], th[:end])


def normals_call(info, own, far, qown, qfar, inverse, reg):
    near, size, _ = own.shape
    arcs = 2 * near
    share = far.shape[2]
    width = inverse.shape[0]
    hbm = pl.BlockSpec(memory_space=pl.ANY)
    return pl.pallas_call(
        normals_kernel,
        out_shape=jax.ShapeDtypeStruct((width, share), F32),
        in_specs=[SM, hbm, hbm, hbm, hbm, VM, VM],
        out_specs=VM,
        scratch_shapes=[
            pltpu.VMEM((arcs, size, share), BF16),
            pltpu.VMEM((arcs, 2 * width, size), BF16),
            pltpu.VMEM((width, share), F32),
            pltpu.SemaphoreType.DMA((2 * arcs,)),
        ],
        compiler_params=grant(36),
        name="normals",
    )(info, own, far, qown, qfar, inverse, reg)

SUB = 8


def three(value):
    high = value.astype(BF16)
    rest = value - high.astype(F32)
    mid = rest.astype(BF16)
    return high, mid, (rest - mid.astype(F32)).astype(BF16)


def factor_diag(work):
    tn = ((0,), (0,))
    wide = work.shape[1]
    for top in range(0, LANE, SUB):
        rows = [work[top + i : top + i + 1, :] for i in range(SUB)]
        e = {}
        for j in range(SUB):
            for i in range(j, SUB):
                at = top + i
                e[j, i] = jnp.broadcast_to(rows[j][:, at : at + 1], (1, LANE))
        for j in range(SUB):
            inv = lax.rsqrt(e[j, j])
            inv2 = jnp.concatenate([inv] * (wide // LANE), axis=1)
            rows[j] = rows[j] * inv2
            for i in range(j + 1, SUB):
                e[j, i] = e[j, i] * inv
            for i in range(j + 1, SUB):
                for k in range(i, SUB):
                    e[i, k] = e[i, k] - e[j, i] * e[j, k]
                coef = jnp.concatenate([e[j, i]] * (wide // LANE), axis=1)
                rows[i] = rows[i] - coef * rows[j]
        part = jnp.concatenate(rows, axis=0)
        work[top : top + SUB, :] = part
        end = top + SUB
        if end < LANE:
            h, m, l = three(part)
            lhs = jnp.concatenate([h, h, m, m, h, l], axis=0)[:, :LANE]
            rhs = jnp.concatenate([h, m, h, m, l, h], axis=0)
            gone = mm(lhs, rhs, tn)
            work[end:, :] = work[end:, :] - gone[end:, :]


def chol_kernel(block_ref, other_ref, reg_ref, out_ref, full, work, upper):
    size = block_ref.shape[0]
    row = lax.broadcasted_iota(jnp.int32, (size, size), 0)
    col = lax.broadcasted_iota(jnp.int32, (size, size), 1)
    full[...] = (block_ref[...] + other_ref[...]) + jnp.where(row == col, reg_ref[...], 0.0)
    r1 = lax.broadcasted_iota(jnp.int32, (LANE, LANE), 0)
    c1 = lax.broadcasted_iota(jnp.int32, (LANE, LANE), 1)
    out_ref[...] = jnp.zeros(out_ref.shape, F32)
    for top in range(0, size, LANE):
        end = top + LANE
        work[:, :LANE] = full[top:end, top:end]
        work[:, LANE:] = (r1 == c1).astype(F32)
        factor_diag(work)
        inverse = jnp.where(r1 >= c1, work[:, LANE:], 0.0)
        out_ref[top:end, top:end] = inverse
        if end < size:
            right = mm3(inverse, full[top:end, end:])
            upper[top:end, end:] = right
            rt = right.T
            full[end:, end:] = full[end:, end:] - mm3(rt, right)
    step = LANE
    while step < size:
        for base in range(0, size, 2 * step):
            left = slice(base, base + step)
            second = slice(base + step, base + 2 * step)
            low = upper[left, second].T
            out_ref[second, left] = -mm3(out_ref[second, second], mm3(low, out_ref[left, left]))
        step *= 2


def chol_inverse(block, other, reg):
    size = block.shape[0]
    vm = pl.BlockSpec(memory_space=pltpu.VMEM)
    return pl.pallas_call(
        chol_kernel,
        out_shape=jax.ShapeDtypeStruct((size, size), F32),
        in_specs=[vm, vm, vm],
        out_specs=vm,
        scratch_shapes=[
            pltpu.VMEM((size, size), F32),
            pltpu.VMEM((LANE, 2 * LANE), F32),
            pltpu.VMEM((size, size), F32),
        ],
        compiler_params=grant(12),
        name="chol_inverse",
    )(block, other, reg)


def block_hits(active, first, count):
    ids = first + jnp.arange(count, dtype=jnp.int32)
    return jnp.any(active[:, :, None] == ids[None, None, :], axis=1)


def factor_rows(cov_factor, me):
    rows = cov_factor.shape[1]
    at = me * rows // LANE * LANE
    strip = lax.dynamic_slice_in_dim(cov_factor, at, LANE, 2)
    high, low = invert_diag(strip, (me * rows % LANE).astype(jnp.int32)[None])
    rest = lax.dynamic_update_slice_in_dim(cov_factor.astype(BF16), high, at, 2)
    return jnp.concatenate([low, rest], axis=2)


def general(design, cov_factor, active_blocks, panel_index, reg_diag):
    arcs, observed, columns = design.shape
    rows = cov_factor.shape[1]
    par_id = lax.axis_index("par")
    arc_id = lax.axis_index("arc")
    lower = lax.all_gather(factor_rows(cov_factor, par_id), "par", axis=1, tiled=True)
    local_blocks = columns // BLK
    hits = block_hits(active_blocks, par_id * local_blocks, local_blocks)
    masked = design * jnp.repeat(hits, BLK, axis=1).astype(BF16)[:, None, :]
    start = panel_index[0] * PANEL
    padded = jnp.pad(masked, ((0, 0), (0, 0), (PANEL, PANEL)))
    window = lax.dynamic_slice_in_dim(
        padded, jnp.clip(start - par_id * columns + PANEL, 0, columns + PANEL), PANEL, 2
    )
    panel = lax.psum(window.astype(F32).astype(BF16), "par")
    factors = []
    for arc in range(arcs):
        call = invert_call(functools.partial(invert_dense_kernel, rows), observed, 1, [])
        factors += call(lower[arc])
    place = jnp.zeros((arcs,), jnp.int32)
    qs, block = apply_call(place, [panel[arc : arc + 1] for arc in range(arcs)], factors)
    both = jnp.einsum("apo,aoc->pc", qs, masked, preferred_element_type=F32)
    gram = both[:PANEL] + both[PANEL:]
    share = columns // lax.axis_size("arc")
    gram, block = lax.psum((gram, block), "arc")
    gram = lax.dynamic_slice_in_dim(gram, arc_id * share, share, 1)
    reg_panel = lax.dynamic_slice_in_dim(reg_diag, start, PANEL)
    inverse = chol_inverse(block, jnp.zeros_like(block), reg_panel[None, :])
    global_cols = par_id * columns + arc_id * share + jnp.arange(share, dtype=jnp.int32)
    rows_at = start + jnp.arange(PANEL, dtype=jnp.int32)
    shifted = gram + jnp.where(global_cols[None, :] == rows_at[:, None], reg_panel[:, None], 0.0)
    return jnp.dot(inverse, shifted, precision=lax.Precision.HIGHEST, preferred_element_type=F32)


def paired(design, cov_factor, active_blocks, panel_index, reg_diag):
    arcs, observed, columns = design.shape
    rows = cov_factor.shape[1]
    chips = lax.axis_size("par")
    planes = chips // 4
    me = lax.axis_index("par")
    core = lax.axis_index("arc")
    sides = (me & 1, (me >> 1) & 1)
    plane = me >> 2
    share = columns // 2
    start = panel_index[0] * PANEL

    def swap(value):
        return lax.ppermute(value, "arc", [(0, 1), (1, 0)])

    def hop(value, bits):
        return lax.ppermute(value, "par", [(p, p ^ bits) for p in range(chips)])

    def spread(value, first):
        second = 3 - first
        direct = hop(value, first)
        return {0: value, first: direct, second: hop(value, second), 3: hop(direct, second)}

    offset = start - me * columns
    inside = (offset >= 0) & (offset < columns)
    live = jnp.repeat(block_hits(active_blocks, start // BLK, PANEL // BLK) & inside, BLK, axis=1)
    left = jnp.clip(offset, 0, columns - PANEL)
    half, quarter = observed // 2, observed // 4

    def window(arc, top):
        value = lax.dynamic_slice(design, (jnp.int32(arc), top, left), (1, half, PANEL))[0]
        return jnp.where(live[arc][None, :], value, 0)

    sends = [window(arc, (1 - sides[arc % 2]) * half) for arc in range(arcs)]
    sends, cov_factor = lax.optimization_barrier((sends, cov_factor))
    keeps = [window(arc, sides[arc % 2] * half) for arc in range(arcs)]
    seeds = []
    for arc in range(arcs):
        first, second = arc % 2, 1 - arc % 2
        gone = hop(sends[arc], 1 << first)

        def piece(side):
            at = side * quarter
            return lax.dynamic_slice_in_dim(keeps[arc], at, quarter, 0) + lax.dynamic_slice_in_dim(
                gone, at, quarter, 0
            )

        value = piece(sides[second]) + hop(piece(1 - sides[second]), 1 << second)
        seeds.append(value.reshape(planes, rows, PANEL))
    seeds = jnp.stack(seeds, axis=1)
    chunk = lax.dynamic_index_in_dim(seeds, plane, 0, False)
    for k in range(1, planes):
        chunk += hop(lax.dynamic_index_in_dim(seeds, plane ^ k, 0, False), 4 * k)

    lower = factor_rows(cov_factor, me)
    stack = [lower] + [hop(lower, 4 * k) for k in range(1, planes)]
    packed = []
    for index in range(planes):
        width = LANE + 4 * rows * (index + 1)
        value = stack[0][:, :, :width]
        for k in range(1, planes):
            value = jnp.where(plane == (index ^ k), stack[k][:, :, :width], value)
        packed.append(value)
    packed = jnp.concatenate(packed, axis=2)
    seats = (me & 3) ^ jnp.arange(4, dtype=jnp.int32)

    first_column = me * columns + core * share
    both = jnp.concatenate([active_blocks, swap(active_blocks)], axis=0)
    lives = block_hits(both, first_column // BLK, share // BLK).T.reshape(-1).astype(jnp.int32)
    info = jnp.stack([core * (share // BLK), start - first_column]).astype(jnp.int32)
    info = jnp.concatenate([info, lives])
    reg = lax.dynamic_slice_in_dim(reg_diag, first_column, share)[None, :]
    reg_panel = lax.dynamic_slice_in_dim(reg_diag, start, PANEL)[None, :]
    source = me ^ (
        jnp.arange(4, dtype=jnp.int32)[:, None] ^ (4 * jnp.arange(planes, dtype=jnp.int32)[None, :])
    )
    place = []
    for arc in range(arcs):
        bits = (source & 1, (source >> 1) & 1)
        order = (bits[arc % 2] * 2 + bits[1 - arc % 2]) * planes + (source >> 2)
        place.append(order.reshape(-1) * rows)
    place = jnp.concatenate(place)
    far = swap(lax.dynamic_slice_in_dim(design, (1 - core) * share, share, 2))
    chunk, seats, info, reg, reg_panel, place = lax.optimization_barrier(
        (chunk, seats, info, reg, reg_panel, place)
    )

    factors = []
    for arc in range(arcs):
        pieces = spread(packed[arc], 1 + arc % 2)
        call = invert_call(
            functools.partial(invert_pieces_kernel, rows), observed, 4,
            [pltpu.VMEM((observed, observed), BF16), pltpu.VMEM((observed, LANE), BF16)],
        )
        factors += call(seats, *[pieces[k] for k in range(4)])

    stack = jnp.stack([chunk] + [hop(chunk, 4 * k) for k in range(1, planes)], axis=1)
    pieces = []
    for arc in range(arcs):
        found = spread(stack[arc], 1 + arc % 2)
        pieces += [found[k] for k in range(4)]
    qs, block = apply_call(place, pieces, factors)
    inverse = chol_inverse(block, swap(block), reg_panel)
    return normals_call(info, design, far, qs, swap(qs), inverse, reg)


def whole(design, cov_factor, *rest):
    chips = lax.axis_size("par")
    columns = design.shape[2]
    fits = (
        lax.axis_size("arc") == 2
        and design.shape[0] == 2
        and chips == 16
        and columns % PANEL == 0
        and columns % (2 * BLK) == 0
        and LANE % cov_factor.shape[1] == 0
    )
    return (paired if fits else general)(design, cov_factor, *rest)


def solution(mesh):
    in_specs = (P("arc", None, "par"), P("arc", "par", None), P("arc", None), P(), P())
    out_specs = P(None, ("par", "arc"))
    return jax.shard_map(
        whole, mesh=mesh, in_specs=in_specs, out_specs=out_specs, check_vma=False
    )
```

```python
import functools

import jax
import jax.numpy as jnp
from jax import lax
from jax.experimental import pallas as pl
from jax.experimental.pallas import tpu as pltpu
from jax.sharding import PartitionSpec as P


PANEL = 512
BLK = 256
F32, BF16 = jnp.float32, jnp.bfloat16
LANE = 128


def split(value):
    high = value.astype(BF16)
    return high, (value - high.astype(F32)).astype(BF16)


def mm(a, b, dims=((1,), (0,))):
    return lax.dot_general(a, b, (dims, ((), ())), preferred_element_type=F32)


def mm3(a, b):
    ah, al = split(a)
    bh, bl = split(b)
    return mm(ah, bh) + (mm(ah, bl) + mm(al, bh))


def level_mask(step):
    rows = lax.broadcasted_iota(jnp.int32, (LANE, LANE), 0)
    cols = lax.broadcasted_iota(jnp.int32, (LANE, LANE), 1)
    return (
        (rows // (2 * step) == cols // (2 * step))
        & ((rows // step) % 2 == 1)
        & ((cols // step) % 2 == 0)
    )


def diag_kernel(off_ref, strip_ref, high, low, square):
    arcs, rows, _ = strip_ref.shape
    off = pl.multiple_of(off_ref[0], 8)
    r = lax.broadcasted_iota(jnp.int32, (LANE, LANE), 0)
    c = lax.broadcasted_iota(jnp.int32, (LANE, LANE), 1)
    eye = r == c
    sub = lax.broadcasted_iota(jnp.int32, (rows, LANE), 1)
    own = (sub >= off) & (sub < off + rows)
    for arc in range(arcs):
        square[arc] = eye.astype(F32)
        square[arc, pl.ds(off, rows), :] = jnp.where(own, strip_ref[arc], 0.0)
    lowers = [square[arc] for arc in range(arcs)]
    invs = [jnp.where(eye, 1.0 / jnp.where(eye, low, 1.0), 0.0) for low in lowers]
    step = 1
    while step < rows:
        mask = level_mask(step)
        parts = [mm3(jnp.where(mask, low, 0.0), inv) for low, inv in zip(lowers, invs)]
        invs = [inv - mm3(inv, part) for inv, part in zip(invs, parts)]
        step *= 2
    for arc in range(arcs):
        square[arc] = invs[arc]
        value = jnp.where(own, square[arc, pl.ds(off, rows), :], strip_ref[arc])
        high[arc], low[arc] = split(value)


def invert_diag(strip, off):
    arcs = strip.shape[0]
    out = jax.ShapeDtypeStruct(strip.shape, BF16)
    return pl.pallas_call(
        diag_kernel,
        out_shape=(out, out),
        in_specs=[pl.BlockSpec(memory_space=pltpu.SMEM), pl.BlockSpec(memory_space=pltpu.VMEM)],
        out_specs=(pl.BlockSpec(memory_space=pltpu.VMEM), pl.BlockSpec(memory_space=pltpu.VMEM)),
        scratch_shapes=[pltpu.VMEM((arcs, LANE, LANE), F32)],
        name="invert_diag",
    )(off, strip)


def invert_factor(rest, fine, high, low, first):
    size = high.shape[0]
    half = max(size // 2, LANE)
    for top in range(0, size, half):
        for ref in (high, low):
            ref[top : top + half, top : top + half] = jnp.zeros((half, half), BF16)
    rows = lax.broadcasted_iota(jnp.int32, (LANE, LANE), 0) // first
    cols = lax.broadcasted_iota(jnp.int32, (LANE, LANE), 1) // first
    blocks = [
        rest[t : t + LANE, t : t + LANE].astype(F32) + fine[t : t + LANE, :].astype(F32)
        for t in range(0, size, LANE)
    ]
    invs = [jnp.where(rows == cols, block, 0.0) for block in blocks]
    step = first
    while step < LANE:
        mask = level_mask(step)
        parts = [mm3(jnp.where(mask, block, 0.0), inv) for block, inv in zip(blocks, invs)]
        invs = [inv - mm3(inv, part) for inv, part in zip(invs, parts)]
        step *= 2
    for index, inv in enumerate(invs):
        at = slice(index * LANE, (index + 1) * LANE)
        high[at, at], low[at, at] = split(inv)
    step = LANE
    while step < size:
        for base in range(0, size, 2 * step):
            left = slice(base, base + step)
            right = slice(base + step, base + 2 * step)
            below = rest[right, left]
            ph, pl_ = split(mm(below, high[left, left]) + mm(below, low[left, left]))
            ch, cl = high[right, right], low[right, right]
            high[right, left], low[right, left] = split(-(mm(ch, ph) + (mm(ch, pl_) + mm(cl, ph))))
        step *= 2


VM = pl.BlockSpec(memory_space=pltpu.VMEM)
SM = pl.BlockSpec(memory_space=pltpu.SMEM)
MIB = 1 << 20


def grant(mib):
    return pltpu.CompilerParams(vmem_limit_bytes=mib * MIB)


def invert_dense_kernel(first, rows_ref, high, low):
    invert_factor(rows_ref.at[:, LANE:], rows_ref.at[:, :LANE], high, low, first)


def invert_pieces_kernel(first, place_ref, p0, p1, p2, p3, high, low, rest, fine):
    rows = p0.shape[0]
    planes = rest.shape[0] // (4 * rows)
    for k, piece in enumerate((p0, p1, p2, p3)):
        seat = place_ref[k]
        left = 0
        for plane in range(planes):
            width = 4 * rows * (plane + 1)
            at = pl.multiple_of((4 * plane + seat) * rows, 16)
            fine[pl.ds(at, rows), :] = piece[:, left : left + LANE]
            rest[pl.ds(at, rows), :width] = piece[:, left + LANE : left + LANE + width]
            left += LANE + width
    invert_factor(rest, fine, high, low, first)


def invert_call(kernel, size, count, scratch):
    out = jax.ShapeDtypeStruct((size, size), BF16)
    return pl.pallas_call(
        kernel,
        out_shape=(out, out),
        in_specs=[SM] * (count > 1) + [VM] * count,
        out_specs=(VM, VM),
        scratch_shapes=scratch,
        compiler_params=grant(20),
        name="invert_factor",
    )


def panel_kernel(arcs, place_ref, *refs):
    count = (len(refs) - 3) // arcs - 2
    pieces = refs[: arcs * count]
    factors = refs[arcs * count : arcs * (count + 2)]
    pt, block_ref, panel = refs[arcs * (count + 2) :]
    size = panel.shape[0]
    span = min(256, size)
    nt = ((1,), (1,))
    for arc in range(arcs):
        index = arc * pieces[0].shape[0] * count
        for piece in pieces[arc * count : (arc + 1) * count]:
            rows = piece.shape[1]
            for z in range(piece.shape[0]):
                at = pl.multiple_of(place_ref[index], 16)
                panel[pl.ds(at, rows), :] = piece[z].astype(F32)
                index += 1
        raw = panel[...].T.astype(BF16)
        high, low = factors[2 * arc], factors[2 * arc + 1]
        for top in range(0, size, span):
            end = top + span
            value = mm(raw[:, :end], high[top:end, :end], nt) + mm(raw[:, :end], low[top:end, :end], nt)
            pt[arc, :, top:end] = value.astype(BF16)
        part = mm(pt[arc], pt[arc], nt)
        block_ref[...] = part if arc == 0 else block_ref[...] + part


def back_kernel(arcs, pt, *refs):
    factors, q_ref = refs[: 2 * arcs], refs[2 * arcs]
    _, width, size = pt.shape
    span = min(256, size)
    for arc in range(arcs):
        high, low = factors[2 * arc], factors[2 * arc + 1]
        for top in range(0, size, span):
            end = top + span
            part = pt[arc, :, top:]
            value = mm(part, high[top:, top:end]) + mm(part, low[top:, top:end])
            q_ref[arc, :width, top:end], q_ref[arc, width:, top:end] = split(value)


def panel_call(place, pieces, factors):
    arcs = len(factors) // 2
    size = factors[0].shape[0]
    width = pieces[0].shape[2]
    return pl.pallas_call(
        functools.partial(panel_kernel, arcs),
        out_shape=(
            jax.ShapeDtypeStruct((arcs, width, size), BF16),
            jax.ShapeDtypeStruct((width, width), F32),
        ),
        in_specs=[SM] + [VM] * (len(pieces) + len(factors)),
        out_specs=(VM, VM),
        scratch_shapes=[pltpu.VMEM((size, width), F32)],
        compiler_params=grant(26),
        name="panel_block",
    )(place, *pieces, *factors)


def back_call(pt, factors):
    arcs, width, size = pt.shape
    return pl.pallas_call(
        functools.partial(back_kernel, arcs),
        out_shape=jax.ShapeDtypeStruct((arcs, 2 * width, size), BF16),
        in_specs=[VM] * (1 + len(factors)),
        out_specs=VM,
        compiler_params=grant(26),
        name="back_solve",
    )(pt, *factors)


def normals_kernel(info, own, far, qown, qfar, inv_ref, reg_ref, out_ref, data, qs, acc, sems):
    near = own.shape[0]
    arcs = 2 * near
    size, share = acc.shape
    blocks = share // BLK
    half = size // 2
    left = pl.multiple_of(info[0] * BLK, BLK)
    copies = []
    for arc in range(arcs):
        if arc < near:
            source, q = own.at[arc, :, pl.ds(left, share)], qown.at[arc]
        else:
            source, q = far.at[arc - near], qfar.at[arc - near]
        pair = (
            pltpu.make_async_copy(q, qs.at[arc], sems.at[2 * arc]),
            pltpu.make_async_copy(source, data.at[arc], sems.at[2 * arc + 1]),
        )
        for copy in pair:
            copy.start()
        copies.append(pair)
    acc[...] = jnp.zeros_like(acc)
    for arc in range(arcs):
        for copy in copies[arc]:
            copy.wait()

        def add(block, _):
            @pl.when(info[2 + block * arcs + arc] > 0)
            def _():
                at = pl.ds(pl.multiple_of(block * BLK, BLK), BLK)
                both = mm(qs[arc], data[arc, :, at])
                acc[:, at] += both[:size] + both[size:]

            return 0

        lax.fori_loop(0, blocks, add, 0)
    ih, il = split(inv_ref[...])
    row = lax.broadcasted_iota(jnp.int32, (size, BLK), 0) + info[1]
    col = lax.broadcasted_iota(jnp.int32, (size, BLK), 1)
    for block in range(blocks):
        at = slice(block * BLK, (block + 1) * BLK)
        hit = row == col + block * BLK
        th, tl = split(acc[:, at] + jnp.where(hit, reg_ref[:, at], 0.0))
        for top, end in ((0, half), (half, size)):
            value = mm(ih[top:end, :end], th[:end]) + mm(ih[top:end, :end], tl[:end])
            out_ref[top:end, at] = value + mm(il[top:end, :end], th[:end])


def normals_call(info, own, far, qown, qfar, inverse, reg):
    near, size, _ = own.shape
    arcs = 2 * near
    share = far.shape[2]
    width = inverse.shape[0]
    hbm = pl.BlockSpec(memory_space=pl.ANY)
    return pl.pallas_call(
        normals_kernel,
        out_shape=jax.ShapeDtypeStruct((width, share), F32),
        in_specs=[SM, hbm, hbm, hbm, hbm, VM, VM],
        out_specs=VM,
        scratch_shapes=[
            pltpu.VMEM((arcs, size, share), BF16),
            pltpu.VMEM((arcs, 2 * width, size), BF16),
            pltpu.VMEM((width, share), F32),
            pltpu.SemaphoreType.DMA((2 * arcs,)),
        ],
        compiler_params=grant(36),
        name="normals",
    )(info, own, far, qown, qfar, inverse, reg)


SUB = 8


def three(value):
    high = value.astype(BF16)
    rest = value - high.astype(F32)
    mid = rest.astype(BF16)
    return high, mid, (rest - mid.astype(F32)).astype(BF16)


def factor_diag(work):
    tn = ((0,), (0,))
    wide = work.shape[1]
    for top in range(0, LANE, SUB):
        rows = [work[top + i : top + i + 1, :] for i in range(SUB)]
        e = {}
        for j in range(SUB):
            for i in range(j, SUB):
                at = top + i
                e[j, i] = jnp.broadcast_to(rows[j][:, at : at + 1], (1, LANE))
        for j in range(SUB):
            inv = lax.rsqrt(e[j, j])
            inv2 = jnp.concatenate([inv] * (wide // LANE), axis=1)
            rows[j] = rows[j] * inv2
            for i in range(j + 1, SUB):
                e[j, i] = e[j, i] * inv
            for i in range(j + 1, SUB):
                for k in range(i, SUB):
                    e[i, k] = e[i, k] - e[j, i] * e[j, k]
                coef = jnp.concatenate([e[j, i]] * (wide // LANE), axis=1)
                rows[i] = rows[i] - coef * rows[j]
        part = jnp.concatenate(rows, axis=0)
        work[top : top + SUB, :] = part
        end = top + SUB
        if end < LANE:
            h, m, l = three(part)
            lhs = jnp.concatenate([h, h, m, m, h, l], axis=0)[:, :LANE]
            rhs = jnp.concatenate([h, m, h, m, l, h], axis=0)
            gone = mm(lhs, rhs, tn)
            work[end:, :] = work[end:, :] - gone[end:, :]


def chol_kernel(block_ref, other_ref, reg_ref, out_ref, full, work, upper):
    size = block_ref.shape[0]
    row = lax.broadcasted_iota(jnp.int32, (size, size), 0)
    col = lax.broadcasted_iota(jnp.int32, (size, size), 1)
    full[...] = (block_ref[...] + other_ref[...]) + jnp.where(row == col, reg_ref[...], 0.0)
    r1 = lax.broadcasted_iota(jnp.int32, (LANE, LANE), 0)
    c1 = lax.broadcasted_iota(jnp.int32, (LANE, LANE), 1)
    out_ref[...] = jnp.zeros(out_ref.shape, F32)
    for top in range(0, size, LANE):
        end = top + LANE
        work[:, :LANE] = full[top:end, top:end]
        work[:, LANE:] = (r1 == c1).astype(F32)
        factor_diag(work)
        inverse = jnp.where(r1 >= c1, work[:, LANE:], 0.0)
        out_ref[top:end, top:end] = inverse
        if end < size:
            right = mm3(inverse, full[top:end, end:])
            upper[top:end, end:] = right
            rt = right.T
            full[end:, end:] = full[end:, end:] - mm3(rt, right)
    step = LANE
    while step < size:
        for base in range(0, size, 2 * step):
            left = slice(base, base + step)
            second = slice(base + step, base + 2 * step)
            low = upper[left, second].T
            out_ref[second, left] = -mm3(out_ref[second, second], mm3(low, out_ref[left, left]))
        step *= 2


def chol_inverse(block, other, reg):
    size = block.shape[0]
    vm = pl.BlockSpec(memory_space=pltpu.VMEM)
    return pl.pallas_call(
        chol_kernel,
        out_shape=jax.ShapeDtypeStruct((size, size), F32),
        in_specs=[vm, vm, vm],
        out_specs=vm,
        scratch_shapes=[
            pltpu.VMEM((size, size), F32),
            pltpu.VMEM((LANE, 2 * LANE), F32),
            pltpu.VMEM((size, size), F32),
        ],
        compiler_params=grant(12),
        name="chol_inverse",
    )(block, other, reg)


def block_hits(active, first, count):
    ids = first + jnp.arange(count, dtype=jnp.int32)
    return jnp.any(active[:, :, None] == ids[None, None, :], axis=1)


def factor_rows(cov_factor, me):
    rows = cov_factor.shape[1]
    at = me * rows // LANE * LANE
    strip = lax.dynamic_slice_in_dim(cov_factor, at, LANE, 2)
    high, low = invert_diag(strip, (me * rows % LANE).astype(jnp.int32)[None])
    rest = lax.dynamic_update_slice_in_dim(cov_factor.astype(BF16), high, at, 2)
    return jnp.concatenate([low, rest], axis=2)


def general(design, cov_factor, active_blocks, panel_index, reg_diag):
    arcs, observed, columns = design.shape
    rows = cov_factor.shape[1]
    par_id = lax.axis_index("par")
    arc_id = lax.axis_index("arc")
    lower = lax.all_gather(factor_rows(cov_factor, par_id), "par", axis=1, tiled=True)
    local_blocks = columns // BLK
    hits = block_hits(active_blocks, par_id * local_blocks, local_blocks)
    masked = design * jnp.repeat(hits, BLK, axis=1).astype(BF16)[:, None, :]
    start = panel_index[0] * PANEL
    padded = jnp.pad(masked, ((0, 0), (0, 0), (PANEL, PANEL)))
    window = lax.dynamic_slice_in_dim(
        padded, jnp.clip(start - par_id * columns + PANEL, 0, columns + PANEL), PANEL, 2
    )
    panel = lax.psum(window.astype(F32).astype(BF16), "par")
    factors = []
    for arc in range(arcs):
        call = invert_call(functools.partial(invert_dense_kernel, rows), observed, 1, [])
        factors += call(lower[arc])
    place = jnp.zeros((arcs,), jnp.int32)
    pt, block = panel_call(place, [panel[arc : arc + 1] for arc in range(arcs)], factors)
    qs = back_call(pt, factors)
    both = jnp.einsum("apo,aoc->pc", qs, masked, preferred_element_type=F32)
    gram = both[:PANEL] + both[PANEL:]
    share = columns // lax.axis_size("arc")
    gram, block = lax.psum((gram, block), "arc")
    gram = lax.dynamic_slice_in_dim(gram, arc_id * share, share, 1)
    reg_panel = lax.dynamic_slice_in_dim(reg_diag, start, PANEL)
    inverse = chol_inverse(block, jnp.zeros_like(block), reg_panel[None, :])
    global_cols = par_id * columns + arc_id * share + jnp.arange(share, dtype=jnp.int32)
    rows_at = start + jnp.arange(PANEL, dtype=jnp.int32)
    shifted = gram + jnp.where(global_cols[None, :] == rows_at[:, None], reg_panel[:, None], 0.0)
    return jnp.dot(inverse, shifted, precision=lax.Precision.HIGHEST, preferred_element_type=F32)


def paired(design, cov_factor, active_blocks, panel_index, reg_diag):
    arcs, observed, columns = design.shape
    rows = cov_factor.shape[1]
    chips = lax.axis_size("par")
    planes = chips // 4
    me = lax.axis_index("par")
    core = lax.axis_index("arc")
    sides = (me & 1, (me >> 1) & 1)
    plane = me >> 2
    share = columns // 2
    start = panel_index[0] * PANEL

    def swap(value):
        return lax.ppermute(value, "arc", [(0, 1), (1, 0)])

    def hop(value, bits):
        return lax.ppermute(value, "par", [(p, p ^ bits) for p in range(chips)])

    def spread(value, first):
        second = 3 - first
        direct = hop(value, first)
        return {0: value, first: direct, second: hop(value, second), 3: hop(direct, second)}

    offset = start - me * columns
    inside = (offset >= 0) & (offset < columns)
    live = jnp.repeat(block_hits(active_blocks, start // BLK, PANEL // BLK) & inside, BLK, axis=1)
    left = jnp.clip(offset, 0, columns - PANEL)
    half, quarter = observed // 2, observed // 4

    def window(arc, top):
        value = lax.dynamic_slice(design, (jnp.int32(arc), top, left), (1, half, PANEL))[0]
        return jnp.where(live[arc][None, :], value, 0)

    sends = [window(arc, (1 - sides[arc % 2]) * half) for arc in range(arcs)]
    sends, cov_factor = lax.optimization_barrier((sends, cov_factor))
    keeps = [window(arc, sides[arc % 2] * half) for arc in range(arcs)]
    seeds = []
    for arc in range(arcs):
        first, second = arc % 2, 1 - arc % 2
        gone = hop(sends[arc], 1 << first)

        def piece(side):
            at = side * quarter
            return lax.dynamic_slice_in_dim(keeps[arc], at, quarter, 0) + lax.dynamic_slice_in_dim(
                gone, at, quarter, 0
            )

        again = piece(1 - sides[second])
        again = hop(again, 1 << second)
        value = piece(sides[second]) + again
        seeds.append(value.reshape(planes, rows, PANEL))
    seeds = jnp.stack(seeds, axis=1)
    chunk = lax.dynamic_index_in_dim(seeds, plane, 0, False)
    for k in range(1, planes):
        chunk += hop(lax.dynamic_index_in_dim(seeds, plane ^ k, 0, False), 4 * k)

    lower = factor_rows(cov_factor, me)
    stack = [lower]
    for k in range(1, planes):
        stack.append(hop(lower, 4 * k))
    packed = []
    for index in range(planes):
        width = LANE + 4 * rows * (index + 1)
        value = stack[0][:, :, :width]
        for k in range(1, planes):
            value = jnp.where(plane == (index ^ k), stack[k][:, :, :width], value)
        packed.append(value)
    packed = jnp.concatenate(packed, axis=2)
    seats = (me & 3) ^ jnp.arange(4, dtype=jnp.int32)

    first_column = me * columns + core * share
    both = jnp.concatenate([active_blocks, swap(active_blocks)], axis=0)
    lives = block_hits(both, first_column // BLK, share // BLK).T.reshape(-1).astype(jnp.int32)
    info = jnp.stack([core * (share // BLK), start - first_column]).astype(jnp.int32)
    info = jnp.concatenate([info, lives])
    reg = lax.dynamic_slice_in_dim(reg_diag, first_column, share)[None, :]
    reg_panel = lax.dynamic_slice_in_dim(reg_diag, start, PANEL)[None, :]
    source = me ^ (
        jnp.arange(4, dtype=jnp.int32)[:, None] ^ (4 * jnp.arange(planes, dtype=jnp.int32)[None, :])
    )
    place = []
    for arc in range(arcs):
        bits = (source & 1, (source >> 1) & 1)
        order = (bits[arc % 2] * 2 + bits[1 - arc % 2]) * planes + (source >> 2)
        place.append(order.reshape(-1) * rows)
    place = jnp.concatenate(place)
    far = lax.dynamic_slice_in_dim(design, (1 - core) * share, share, 2)
    far = swap(far)
    chunk, seats, info, reg, reg_panel, place = lax.optimization_barrier(
        (chunk, seats, info, reg, reg_panel, place)
    )

    factors = []
    for arc in range(arcs):
        pieces = spread(packed[arc], 1 + arc % 2)
        call = invert_call(
            functools.partial(invert_pieces_kernel, rows), observed, 4,
            [pltpu.VMEM((observed, observed), BF16), pltpu.VMEM((observed, LANE), BF16)],
        )
        factors += call(seats, *[pieces[k] for k in range(4)])

    stack = jnp.stack([chunk] + [hop(chunk, 4 * k) for k in range(1, planes)], axis=1)
    pieces = []
    for arc in range(arcs):
        found = spread(stack[arc], 1 + arc % 2)
        pieces += [found[k] for k in range(4)]
    pt, block = panel_call(place, pieces, factors)
    other = swap(block)
    qs = back_call(pt, factors)
    qs, other = lax.optimization_barrier((qs, other))
    inverse = chol_inverse(block, other, reg_panel)
    return normals_call(info, design, far, qs, swap(qs), inverse, reg)


def whole(design, cov_factor, *rest):
    chips = lax.axis_size("par")
    columns = design.shape[2]
    fits = (
        lax.axis_size("arc") == 2
        and design.shape[0] == 2
        and chips == 16
        and columns % PANEL == 0
        and columns % (2 * BLK) == 0
        and LANE % cov_factor.shape[1] == 0
    )
    return (paired if fits else general)(design, cov_factor, *rest)


def solution(mesh):
    in_specs = (P("arc", None, "par"), P("arc", "par", None), P("arc", None), P(), P())
    out_specs = P(None, ("par", "arc"))
    return jax.shard_map(
        whole, mesh=mesh, in_specs=in_specs, out_specs=out_specs, check_vma=False
    )
```

```python
import functools

import jax
import jax.numpy as jnp
from jax import lax
from jax.experimental import pallas as pl
from jax.experimental.pallas import tpu as pltpu
from jax.sharding import PartitionSpec as P


PANEL = 512
BLK = 256
F32, BF16 = jnp.float32, jnp.bfloat16
LANE = 128


def split(value):
    high = value.astype(BF16)
    return high, (value - high.astype(F32)).astype(BF16)


def mm(a, b, dims=((1,), (0,))):
    return lax.dot_general(a, b, (dims, ((), ())), preferred_element_type=F32)


def mm3(a, b):
    ah, al = split(a)
    bh, bl = split(b)
    return mm(ah, bh) + (mm(ah, bl) + mm(al, bh))


def level_mask(step):
    rows = lax.broadcasted_iota(jnp.int32, (LANE, LANE), 0)
    cols = lax.broadcasted_iota(jnp.int32, (LANE, LANE), 1)
    return (
        (rows // (2 * step) == cols // (2 * step))
        & ((rows // step) % 2 == 1)
        & ((cols // step) % 2 == 0)
    )


def diag_kernel(off_ref, strip_ref, high, low, square):
    arcs, rows, _ = strip_ref.shape
    off = pl.multiple_of(off_ref[0], 8)
    r = lax.broadcasted_iota(jnp.int32, (LANE, LANE), 0)
    c = lax.broadcasted_iota(jnp.int32, (LANE, LANE), 1)
    eye = r == c
    sub = lax.broadcasted_iota(jnp.int32, (rows, LANE), 1)
    own = (sub >= off) & (sub < off + rows)
    for arc in range(arcs):
        square[arc] = eye.astype(F32)
        square[arc, pl.ds(off, rows), :] = jnp.where(own, strip_ref[arc], 0.0)
    lowers = [square[arc] for arc in range(arcs)]
    invs = [jnp.where(eye, 1.0 / jnp.where(eye, low, 1.0), 0.0) for low in lowers]
    step = 1
    while step < rows:
        mask = level_mask(step)
        parts = [mm3(jnp.where(mask, low, 0.0), inv) for low, inv in zip(lowers, invs)]
        invs = [inv - mm3(inv, part) for inv, part in zip(invs, parts)]
        step *= 2
    for arc in range(arcs):
        square[arc] = invs[arc]
        value = jnp.where(own, square[arc, pl.ds(off, rows), :], strip_ref[arc])
        high[arc], low[arc] = split(value)


def invert_diag(strip, off):
    arcs = strip.shape[0]
    out = jax.ShapeDtypeStruct(strip.shape, BF16)
    return pl.pallas_call(
        diag_kernel,
        out_shape=(out, out),
        in_specs=[pl.BlockSpec(memory_space=pltpu.SMEM), pl.BlockSpec(memory_space=pltpu.VMEM)],
        out_specs=(pl.BlockSpec(memory_space=pltpu.VMEM), pl.BlockSpec(memory_space=pltpu.VMEM)),
        scratch_shapes=[pltpu.VMEM((arcs, LANE, LANE), F32)],
        name="invert_diag",
    )(off, strip)


def invert_factor(rest, fine, high, low, first):
    size = high.shape[0]
    half = max(size // 2, LANE)
    for top in range(0, size, half):
        for ref in (high, low):
            ref[top : top + half, top : top + half] = jnp.zeros((half, half), BF16)
    rows = lax.broadcasted_iota(jnp.int32, (LANE, LANE), 0) // first
    cols = lax.broadcasted_iota(jnp.int32, (LANE, LANE), 1) // first
    blocks = [
        rest[t : t + LANE, t : t + LANE].astype(F32) + fine[t : t + LANE, :].astype(F32)
        for t in range(0, size, LANE)
    ]
    invs = [jnp.where(rows == cols, block, 0.0) for block in blocks]
    step = first
    while step < LANE:
        mask = level_mask(step)
        parts = [mm3(jnp.where(mask, block, 0.0), inv) for block, inv in zip(blocks, invs)]
        invs = [inv - mm3(inv, part) for inv, part in zip(invs, parts)]
        step *= 2
    for index, inv in enumerate(invs):
        at = slice(index * LANE, (index + 1) * LANE)
        high[at, at], low[at, at] = split(inv)
    step = LANE
    while step < size:
        for base in range(0, size, 2 * step):
            left = slice(base, base + step)
            right = slice(base + step, base + 2 * step)
            below = rest[right, left]
            ph, pl_ = split(mm(below, high[left, left]) + mm(below, low[left, left]))
            ch, cl = high[right, right], low[right, right]
            high[right, left], low[right, left] = split(-(mm(ch, ph) + (mm(ch, pl_) + mm(cl, ph))))
        step *= 2


VM = pl.BlockSpec(memory_space=pltpu.VMEM)
SM = pl.BlockSpec(memory_space=pltpu.SMEM)
MIB = 1 << 20


def grant(mib):
    return pltpu.CompilerParams(vmem_limit_bytes=mib * MIB)


def invert_dense_kernel(first, rows_ref, high, low):
    invert_factor(rows_ref.at[:, LANE:], rows_ref.at[:, :LANE], high, low, first)


def invert_pieces_kernel(first, place_ref, p0, p1, p2, p3, high, low, rest, fine):
    rows = p0.shape[0]
    planes = rest.shape[0] // (4 * rows)
    for k, piece in enumerate((p0, p1, p2, p3)):
        seat = place_ref[k]
        left = 0
        for plane in range(planes):
            width = 4 * rows * (plane + 1)
            at = pl.multiple_of((4 * plane + seat) * rows, 16)
            fine[pl.ds(at, rows), :] = piece[:, left : left + LANE]
            rest[pl.ds(at, rows), :width] = piece[:, left + LANE : left + LANE + width]
            left += LANE + width
    invert_factor(rest, fine, high, low, first)


def invert_call(kernel, size, count, scratch):
    out = jax.ShapeDtypeStruct((size, size), BF16)
    return pl.pallas_call(
        kernel,
        out_shape=(out, out),
        in_specs=[SM] * (count > 1) + [VM] * count,
        out_specs=(VM, VM),
        scratch_shapes=scratch,
        compiler_params=grant(20),
        name="invert_factor",
    )


def panel_kernel(arcs, place_ref, *refs):
    count = (len(refs) - 3) // arcs - 2
    pieces = refs[: arcs * count]
    factors = refs[arcs * count : arcs * (count + 2)]
    pt, block_ref, panel = refs[arcs * (count + 2) :]
    size = panel.shape[0]
    span = min(256, size)
    nt = ((1,), (1,))
    for arc in range(arcs):
        index = arc * pieces[0].shape[0] * count
        for piece in pieces[arc * count : (arc + 1) * count]:
            rows = piece.shape[1]
            for z in range(piece.shape[0]):
                at = pl.multiple_of(place_ref[index], 16)
                panel[pl.ds(at, rows), :] = piece[z].astype(F32)
                index += 1
        raw = panel[...].T.astype(BF16)
        high, low = factors[2 * arc], factors[2 * arc + 1]
        for top in range(0, size, span):
            end = top + span
            value = mm(raw[:, :end], high[top:end, :end], nt) + mm(raw[:, :end], low[top:end, :end], nt)
            pt[arc, :, top:end] = value.astype(BF16)
        part = mm(pt[arc], pt[arc], nt)
        block_ref[...] = part if arc == 0 else block_ref[...] + part


def back_kernel(arcs, pt, *refs):
    factors, q_ref = refs[: 2 * arcs], refs[2 * arcs]
    _, width, size = pt.shape
    span = min(256, size)
    for arc in range(arcs):
        high, low = factors[2 * arc], factors[2 * arc + 1]
        for top in range(0, size, span):
            end = top + span
            part = pt[arc, :, top:]
            value = mm(part, high[top:, top:end]) + mm(part, low[top:, top:end])
            q_ref[arc, :width, top:end], q_ref[arc, width:, top:end] = split(value)


def panel_call(place, pieces, factors):
    arcs = len(factors) // 2
    size = factors[0].shape[0]
    width = pieces[0].shape[2]
    return pl.pallas_call(
        functools.partial(panel_kernel, arcs),
        out_shape=(
            jax.ShapeDtypeStruct((arcs, width, size), BF16),
            jax.ShapeDtypeStruct((width, width), F32),
        ),
        in_specs=[SM] + [VM] * (len(pieces) + len(factors)),
        out_specs=(VM, VM),
        scratch_shapes=[pltpu.VMEM((size, width), F32)],
        compiler_params=grant(26),
        name="panel_block",
    )(place, *pieces, *factors)


def back_call(pt, factors):
    arcs, width, size = pt.shape
    return pl.pallas_call(
        functools.partial(back_kernel, arcs),
        out_shape=jax.ShapeDtypeStruct((arcs, 2 * width, size), BF16),
        in_specs=[VM] * (1 + len(factors)),
        out_specs=VM,
        compiler_params=grant(26),
        name="back_solve",
    )(pt, *factors)


def normals_kernel(info, own, far, qown, qfar, inv_ref, reg_ref, out_ref, data, qs, acc, sems):
    near = own.shape[0]
    arcs = 2 * near
    size, share = acc.shape
    blocks = share // BLK
    half = size // 2
    left = pl.multiple_of(info[0] * BLK, BLK)
    copies = []
    for arc in range(arcs):
        if arc < near:
            source, q = own.at[arc, :, pl.ds(left, share)], qown.at[arc]
        else:
            source, q = far.at[arc - near], qfar.at[arc - near]
        pair = (
            pltpu.make_async_copy(q, qs.at[arc], sems.at[2 * arc]),
            pltpu.make_async_copy(source, data.at[arc], sems.at[2 * arc + 1]),
        )
        for copy in pair:
            copy.start()
        copies.append(pair)
    acc[...] = jnp.zeros_like(acc)
    for arc in range(arcs):
        for copy in copies[arc]:
            copy.wait()

        def add(block, _):
            @pl.when(info[2 + block * arcs + arc] > 0)
            def _():
                at = pl.ds(pl.multiple_of(block * BLK, BLK), BLK)
                both = mm(qs[arc], data[arc, :, at])
                acc[:, at] += both[:size] + both[size:]

            return 0

        lax.fori_loop(0, blocks, add, 0)
    ih, il = split(inv_ref[...])
    row = lax.broadcasted_iota(jnp.int32, (size, BLK), 0) + info[1]
    col = lax.broadcasted_iota(jnp.int32, (size, BLK), 1)
    for block in range(blocks):
        at = slice(block * BLK, (block + 1) * BLK)
        hit = row == col + block * BLK
        th, tl = split(acc[:, at] + jnp.where(hit, reg_ref[:, at], 0.0))
        for top, end in ((0, half), (half, size)):
            value = mm(ih[top:end, :end], th[:end]) + mm(ih[top:end, :end], tl[:end])
            out_ref[top:end, at] = value + mm(il[top:end, :end], th[:end])


def normals_call(info, own, far, qown, qfar, inverse, reg):
    near, size, _ = own.shape
    arcs = 2 * near
    share = far.shape[2]
    width = inverse.shape[0]
    hbm = pl.BlockSpec(memory_space=pl.ANY)
    return pl.pallas_call(
        normals_kernel,
        out_shape=jax.ShapeDtypeStruct((width, share), F32),
        in_specs=[SM, hbm, hbm, hbm, hbm, VM, VM],
        out_specs=VM,
        scratch_shapes=[
            pltpu.VMEM((arcs, size, share), BF16),
            pltpu.VMEM((arcs, 2 * width, size), BF16),
            pltpu.VMEM((width, share), F32),
            pltpu.SemaphoreType.DMA((2 * arcs,)),
        ],
        compiler_params=grant(36),
        name="normals",
    )(info, own, far, qown, qfar, inverse, reg)


SUB = 8


def three(value):
    high = value.astype(BF16)
    rest = value - high.astype(F32)
    mid = rest.astype(BF16)
    return high, mid, (rest - mid.astype(F32)).astype(BF16)


def factor_diag(work):
    tn = ((0,), (0,))
    wide = work.shape[1]
    for top in range(0, LANE, SUB):
        rows = [work[top + i : top + i + 1, :] for i in range(SUB)]
        e = {}
        for j in range(SUB):
            for i in range(j, SUB):
                at = top + i
                e[j, i] = jnp.broadcast_to(rows[j][:, at : at + 1], (1, LANE))
        for j in range(SUB):
            inv = lax.rsqrt(e[j, j])
            inv2 = jnp.concatenate([inv] * (wide // LANE), axis=1)
            rows[j] = rows[j] * inv2
            for i in range(j + 1, SUB):
                e[j, i] = e[j, i] * inv
            for i in range(j + 1, SUB):
                for k in range(i, SUB):
                    e[i, k] = e[i, k] - e[j, i] * e[j, k]
                coef = jnp.concatenate([e[j, i]] * (wide // LANE), axis=1)
                rows[i] = rows[i] - coef * rows[j]
        part = jnp.concatenate(rows, axis=0)
        work[top : top + SUB, :] = part
        end = top + SUB
        if end < LANE:
            h, m, l = three(part)
            lhs = jnp.concatenate([h, h, m, m, h, l], axis=0)[:, :LANE]
            rhs = jnp.concatenate([h, m, h, m, l, h], axis=0)
            gone = mm(lhs, rhs, tn)
            work[end:, :] = work[end:, :] - gone[end:, :]


def chol_kernel(block_ref, other_ref, reg_ref, out_ref, full, work, upper):
    size = block_ref.shape[0]
    row = lax.broadcasted_iota(jnp.int32, (size, size), 0)
    col = lax.broadcasted_iota(jnp.int32, (size, size), 1)
    full[...] = (block_ref[...] + other_ref[...]) + jnp.where(row == col, reg_ref[...], 0.0)
    r1 = lax.broadcasted_iota(jnp.int32, (LANE, LANE), 0)
    c1 = lax.broadcasted_iota(jnp.int32, (LANE, LANE), 1)
    out_ref[...] = jnp.zeros(out_ref.shape, F32)
    for top in range(0, size, LANE):
        end = top + LANE
        work[:, :LANE] = full[top:end, top:end]
        work[:, LANE:] = (r1 == c1).astype(F32)
        factor_diag(work)
        inverse = jnp.where(r1 >= c1, work[:, LANE:], 0.0)
        out_ref[top:end, top:end] = inverse
        if end < size:
            right = mm3(inverse, full[top:end, end:])
            upper[top:end, end:] = right
            rt = right.T
            full[end:, end:] = full[end:, end:] - mm3(rt, right)
    step = LANE
    while step < size:
        for base in range(0, size, 2 * step):
            left = slice(base, base + step)
            second = slice(base + step, base + 2 * step)
            low = upper[left, second].T
            out_ref[second, left] = -mm3(out_ref[second, second], mm3(low, out_ref[left, left]))
        step *= 2


def chol_inverse(block, other, reg):
    size = block.shape[0]
    vm = pl.BlockSpec(memory_space=pltpu.VMEM)
    return pl.pallas_call(
        chol_kernel,
        out_shape=jax.ShapeDtypeStruct((size, size), F32),
        in_specs=[vm, vm, vm],
        out_specs=vm,
        scratch_shapes=[
            pltpu.VMEM((size, size), F32),
            pltpu.VMEM((LANE, 2 * LANE), F32),
            pltpu.VMEM((size, size), F32),
        ],
        compiler_params=grant(12),
        name="chol_inverse",
    )(block, other, reg)


def block_hits(active, first, count):
    ids = first + jnp.arange(count, dtype=jnp.int32)
    return jnp.any(active[:, :, None] == ids[None, None, :], axis=1)


def factor_rows(cov_factor, me):
    rows = cov_factor.shape[1]
    at = me * rows // LANE * LANE
    strip = lax.dynamic_slice_in_dim(cov_factor, at, LANE, 2)
    high, low = invert_diag(strip, (me * rows % LANE).astype(jnp.int32)[None])
    rest = lax.dynamic_update_slice_in_dim(cov_factor.astype(BF16), high, at, 2)
    return jnp.concatenate([low, rest], axis=2)


def general(design, cov_factor, active_blocks, panel_index, reg_diag):
    arcs, observed, columns = design.shape
    rows = cov_factor.shape[1]
    par_id = lax.axis_index("par")
    arc_id = lax.axis_index("arc")
    lower = lax.all_gather(factor_rows(cov_factor, par_id), "par", axis=1, tiled=True)
    local_blocks = columns // BLK
    hits = block_hits(active_blocks, par_id * local_blocks, local_blocks)
    masked = design * jnp.repeat(hits, BLK, axis=1).astype(BF16)[:, None, :]
    start = panel_index[0] * PANEL
    padded = jnp.pad(masked, ((0, 0), (0, 0), (PANEL, PANEL)))
    window = lax.dynamic_slice_in_dim(
        padded, jnp.clip(start - par_id * columns + PANEL, 0, columns + PANEL), PANEL, 2
    )
    panel = lax.psum(window.astype(F32).astype(BF16), "par")
    factors = []
    for arc in range(arcs):
        call = invert_call(functools.partial(invert_dense_kernel, rows), observed, 1, [])
        factors += call(lower[arc])
    place = jnp.zeros((arcs,), jnp.int32)
    pt, block = panel_call(place, [panel[arc : arc + 1] for arc in range(arcs)], factors)
    qs = back_call(pt, factors)
    both = jnp.einsum("apo,aoc->pc", qs, masked, preferred_element_type=F32)
    gram = both[:PANEL] + both[PANEL:]
    share = columns // lax.axis_size("arc")
    gram, block = lax.psum((gram, block), "arc")
    gram = lax.dynamic_slice_in_dim(gram, arc_id * share, share, 1)
    reg_panel = lax.dynamic_slice_in_dim(reg_diag, start, PANEL)
    inverse = chol_inverse(block, jnp.zeros_like(block), reg_panel[None, :])
    global_cols = par_id * columns + arc_id * share + jnp.arange(share, dtype=jnp.int32)
    rows_at = start + jnp.arange(PANEL, dtype=jnp.int32)
    shifted = gram + jnp.where(global_cols[None, :] == rows_at[:, None], reg_panel[:, None], 0.0)
    return jnp.dot(inverse, shifted, precision=lax.Precision.HIGHEST, preferred_element_type=F32)


def paired(design, cov_factor, active_blocks, panel_index, reg_diag):
    arcs, observed, columns = design.shape
    rows = cov_factor.shape[1]
    chips = lax.axis_size("par")
    planes = chips // 4
    me = lax.axis_index("par")
    core = lax.axis_index("arc")
    sides = (me & 1, (me >> 1) & 1)
    plane = me >> 2
    share = columns // 2
    start = panel_index[0] * PANEL

    def swap(value):
        return lax.ppermute(value, "arc", [(0, 1), (1, 0)])

    def hop(value, bits):
        return lax.ppermute(value, "par", [(p, p ^ bits) for p in range(chips)])

    def spread(value, first):
        second = 3 - first
        direct, other = hop(value, first), hop(value, second)
        corner = hop(direct, second)
        return {0: value, first: direct, second: other, 3: corner}

    offset = start - me * columns
    inside = (offset >= 0) & (offset < columns)
    live = jnp.repeat(block_hits(active_blocks, start // BLK, PANEL // BLK) & inside, BLK, axis=1)
    left = jnp.clip(offset, 0, columns - PANEL)
    half, quarter = observed // 2, observed // 4

    def window(arc, top):
        value = lax.dynamic_slice(design, (jnp.int32(arc), top, left), (1, half, PANEL))[0]
        return jnp.where(live[arc][None, :], value, 0)

    sends = [window(arc, (1 - sides[arc % 2]) * half) for arc in range(arcs)]
    sends, cov_factor = lax.optimization_barrier((sends, cov_factor))
    keeps = [window(arc, sides[arc % 2] * half) for arc in range(arcs)]
    seeds = []
    for arc in range(arcs):
        first, second = arc % 2, 1 - arc % 2
        gone = hop(sends[arc], 1 << first)

        def piece(side):
            at = side * quarter
            return lax.dynamic_slice_in_dim(keeps[arc], at, quarter, 0) + lax.dynamic_slice_in_dim(
                gone, at, quarter, 0
            )

        again = piece(1 - sides[second])
        again = hop(again, 1 << second)
        value = piece(sides[second]) + again
        seeds.append(value.reshape(planes, rows, PANEL))
    seeds = jnp.stack(seeds, axis=1)
    chunk = lax.dynamic_index_in_dim(seeds, plane, 0, False)
    for k in range(1, planes):
        gone = hop(lax.dynamic_index_in_dim(seeds, plane ^ k, 0, False), 4 * k)
        chunk += gone

    lower = factor_rows(cov_factor, me)
    stack = [lower]
    for k in range(1, planes):
        stack.append(hop(lower, 4 * k))
    packed = []
    for index in range(planes):
        width = LANE + 4 * rows * (index + 1)
        value = stack[0][:, :, :width]
        for k in range(1, planes):
            value = jnp.where(plane == (index ^ k), stack[k][:, :, :width], value)
        packed.append(value)
    packed = jnp.concatenate(packed, axis=2)
    seats = (me & 3) ^ jnp.arange(4, dtype=jnp.int32)

    first_column = me * columns + core * share
    both = jnp.concatenate([active_blocks, swap(active_blocks)], axis=0)
    lives = block_hits(both, first_column // BLK, share // BLK).T.reshape(-1).astype(jnp.int32)
    info = jnp.stack([core * (share // BLK), start - first_column]).astype(jnp.int32)
    info = jnp.concatenate([info, lives])
    reg = lax.dynamic_slice_in_dim(reg_diag, first_column, share)[None, :]
    reg_panel = lax.dynamic_slice_in_dim(reg_diag, start, PANEL)[None, :]
    source = me ^ (
        jnp.arange(4, dtype=jnp.int32)[:, None] ^ (4 * jnp.arange(planes, dtype=jnp.int32)[None, :])
    )
    place = []
    for arc in range(arcs):
        bits = (source & 1, (source >> 1) & 1)
        order = (bits[arc % 2] * 2 + bits[1 - arc % 2]) * planes + (source >> 2)
        place.append(order.reshape(-1) * rows)
    place = jnp.concatenate(place)
    far = lax.dynamic_slice_in_dim(design, (1 - core) * share, share, 2)
    far = swap(far)
    chunk, seats, info, reg, reg_panel, place = lax.optimization_barrier(
        (chunk, seats, info, reg, reg_panel, place)
    )

    factors = []
    for arc in range(arcs):
        pieces = spread(packed[arc], 1 + arc % 2)
        call = invert_call(
            functools.partial(invert_pieces_kernel, rows), observed, 4,
            [pltpu.VMEM((observed, observed), BF16), pltpu.VMEM((observed, LANE), BF16)],
        )
        factors += call(seats, *[pieces[k] for k in range(4)])

    stack = [chunk] + [hop(chunk, 4 * k) for k in range(1, planes)]
    stack = jnp.stack(stack, axis=1)
    pieces = []
    for arc in range(arcs):
        found = spread(stack[arc], 1 + arc % 2)
        pieces += [found[k] for k in range(4)]
    pt, block = panel_call(place, pieces, factors)
    other = swap(block)
    qs = back_call(pt, factors)
    qs, other = lax.optimization_barrier((qs, other))
    inverse = chol_inverse(block, other, reg_panel)
    return normals_call(info, design, far, qs, swap(qs), inverse, reg)


def whole(design, cov_factor, *rest):
    chips = lax.axis_size("par")
    columns = design.shape[2]
    fits = (
        lax.axis_size("arc") == 2
        and design.shape[0] == 2
        and chips == 16
        and columns % PANEL == 0
        and columns % (2 * BLK) == 0
        and LANE % cov_factor.shape[1] == 0
    )
    return (paired if fits else general)(design, cov_factor, *rest)


def solution(mesh):
    in_specs = (P("arc", None, "par"), P("arc", "par", None), P("arc", None), P(), P())
    out_specs = P(None, ("par", "arc"))
    return jax.shard_map(
        whole, mesh=mesh, in_specs=in_specs, out_specs=out_specs, check_vma=False
    )
```

```python
import functools

import jax
import jax.numpy as jnp
from jax import lax
from jax.experimental import pallas as pl
from jax.experimental.pallas import tpu as pltpu
from jax.sharding import PartitionSpec as P


PANEL = 512
BLK = 256
F32, BF16 = jnp.float32, jnp.bfloat16
LANE = 128


def split(value):
    high = value.astype(BF16)
    return high, (value - high.astype(F32)).astype(BF16)


def mm(a, b, dims=((1,), (0,))):
    return lax.dot_general(a, b, (dims, ((), ())), preferred_element_type=F32)


def mm3(a, b):
    ah, al = split(a)
    bh, bl = split(b)
    return mm(ah, bh) + (mm(ah, bl) + mm(al, bh))


def level_mask(step):
    rows = lax.broadcasted_iota(jnp.int32, (LANE, LANE), 0)
    cols = lax.broadcasted_iota(jnp.int32, (LANE, LANE), 1)
    return (
        (rows // (2 * step) == cols // (2 * step))
        & ((rows // step) % 2 == 1)
        & ((cols // step) % 2 == 0)
    )


def diag_kernel(off_ref, strip_ref, high, low, square):
    arcs, rows, _ = strip_ref.shape
    off = pl.multiple_of(off_ref[0], 8)
    r = lax.broadcasted_iota(jnp.int32, (LANE, LANE), 0)
    c = lax.broadcasted_iota(jnp.int32, (LANE, LANE), 1)
    eye = r == c
    sub = lax.broadcasted_iota(jnp.int32, (rows, LANE), 1)
    own = (sub >= off) & (sub < off + rows)
    for arc in range(arcs):
        square[arc] = eye.astype(F32)
        square[arc, pl.ds(off, rows), :] = jnp.where(own, strip_ref[arc], 0.0)
    lowers = [square[arc] for arc in range(arcs)]
    invs = [jnp.where(eye, 1.0 / jnp.where(eye, low, 1.0), 0.0) for low in lowers]
    step = 1
    while step < rows:
        mask = level_mask(step)
        parts = [mm3(jnp.where(mask, low, 0.0), inv) for low, inv in zip(lowers, invs)]
        invs = [inv - mm3(inv, part) for inv, part in zip(invs, parts)]
        step *= 2
    for arc in range(arcs):
        square[arc] = invs[arc]
        value = jnp.where(own, square[arc, pl.ds(off, rows), :], strip_ref[arc])
        high[arc], low[arc] = split(value)


def invert_diag(strip, off):
    arcs = strip.shape[0]
    out = jax.ShapeDtypeStruct(strip.shape, BF16)
    return pl.pallas_call(
        diag_kernel,
        out_shape=(out, out),
        in_specs=[pl.BlockSpec(memory_space=pltpu.SMEM), pl.BlockSpec(memory_space=pltpu.VMEM)],
        out_specs=(pl.BlockSpec(memory_space=pltpu.VMEM), pl.BlockSpec(memory_space=pltpu.VMEM)),
        scratch_shapes=[pltpu.VMEM((arcs, LANE, LANE), F32)],
        name="invert_diag",
    )(off, strip)


def invert_factor(rest, fine, high, low, first):
    size = high.shape[0]
    half = max(size // 2, LANE)
    for top in range(0, size, half):
        for ref in (high, low):
            ref[top : top + half, top : top + half] = jnp.zeros((half, half), BF16)
    rows = lax.broadcasted_iota(jnp.int32, (LANE, LANE), 0) // first
    cols = lax.broadcasted_iota(jnp.int32, (LANE, LANE), 1) // first
    blocks = [
        rest[t : t + LANE, t : t + LANE].astype(F32) + fine[t : t + LANE, :].astype(F32)
        for t in range(0, size, LANE)
    ]
    invs = [jnp.where(rows == cols, block, 0.0) for block in blocks]
    step = first
    while step < LANE:
        mask = level_mask(step)
        parts = [mm3(jnp.where(mask, block, 0.0), inv) for block, inv in zip(blocks, invs)]
        invs = [inv - mm3(inv, part) for inv, part in zip(invs, parts)]
        step *= 2
    for index, inv in enumerate(invs):
        at = slice(index * LANE, (index + 1) * LANE)
        high[at, at], low[at, at] = split(inv)
    step = LANE
    while step < size:
        for base in range(0, size, 2 * step):
            left = slice(base, base + step)
            right = slice(base + step, base + 2 * step)
            below = rest[right, left]
            ph, pl_ = split(mm(below, high[left, left]) + mm(below, low[left, left]))
            ch, cl = high[right, right], low[right, right]
            high[right, left], low[right, left] = split(-(mm(ch, ph) + (mm(ch, pl_) + mm(cl, ph))))
        step *= 2


VM = pl.BlockSpec(memory_space=pltpu.VMEM)
SM = pl.BlockSpec(memory_space=pltpu.SMEM)
MIB = 1 << 20


def grant(mib):
    return pltpu.CompilerParams(vmem_limit_bytes=mib * MIB)


def invert_pieces_kernel(first, place_ref, *refs):
    pieces, (high, low, rest, fine) = refs[:-4], refs[-4:]
    arcs, size, _ = high.shape
    rows = pieces[0].shape[0]
    planes = size // (4 * rows)
    for index, piece in enumerate(pieces):
        arc, seat = index // 4, place_ref[index % 4]
        left = 0
        for plane in range(planes):
            width = 4 * rows * (plane + 1)
            at = pl.multiple_of((4 * plane + seat) * rows, 16)
            fine[arc, pl.ds(at, rows), :] = piece[:, left : left + LANE]
            rest[arc, pl.ds(at, rows), :width] = piece[:, left + LANE : left + LANE + width]
            left += LANE + width

    def one(arc, _):
        invert_factor(rest.at[arc], fine.at[arc], high.at[arc], low.at[arc], first)
        return 0

    lax.fori_loop(0, arcs, one, 0)


def invert_dense_kernel(first, rows_ref, high, low):
    def one(arc, _):
        both = rows_ref.at[arc]
        invert_factor(both.at[:, LANE:], both.at[:, :LANE], high.at[arc], low.at[arc], first)
        return 0

    lax.fori_loop(0, rows_ref.shape[0], one, 0)


def invert_call(kernel, arcs, size, operands, scratch):
    out = jax.ShapeDtypeStruct((arcs, size, size), BF16)
    return pl.pallas_call(
        kernel,
        out_shape=(out, out),
        in_specs=[SM if value.dtype == jnp.int32 else VM for value in operands],
        out_specs=(VM, VM),
        scratch_shapes=scratch,
        compiler_params=grant(28),
        name="invert_factor",
    )(*operands)


def panel_kernel(arcs, place_ref, *refs):
    pieces, (high, low, pt, block_ref, panel) = refs[:-5], refs[-5:]
    count = len(pieces) // arcs
    size = panel.shape[1]
    span = min(256, size)
    nt = ((1,), (1,))
    for arc in range(arcs):
        index = arc * pieces[0].shape[0] * count
        for piece in pieces[arc * count : (arc + 1) * count]:
            rows = piece.shape[1]
            for z in range(piece.shape[0]):
                at = pl.multiple_of(place_ref[index], 16)
                panel[arc, pl.ds(at, rows), :] = piece[z].astype(F32)
                index += 1
    block_ref[...] = jnp.zeros_like(block_ref)

    def one(arc, _):
        raw = panel[arc].T.astype(BF16)
        for top in range(0, size, span):
            end = top + span
            value = mm(raw[:, :end], high[arc, top:end, :end], nt)
            value += mm(raw[:, :end], low[arc, top:end, :end], nt)
            pt[arc, :, top:end] = value.astype(BF16)
        block_ref[...] += mm(pt[arc], pt[arc], nt)
        return 0

    lax.fori_loop(0, arcs, one, 0)


def back_kernel(pt, high, low, q_ref):
    arcs, width, size = pt.shape
    span = min(256, size)

    def one(arc, _):
        for top in range(0, size, span):
            end = top + span
            part = pt[arc, :, top:]
            value = mm(part, high[arc, top:, top:end]) + mm(part, low[arc, top:, top:end])
            q_ref[arc, :width, top:end], q_ref[arc, width:, top:end] = split(value)
        return 0

    lax.fori_loop(0, arcs, one, 0)


def panel_call(place, pieces, factors):
    arcs, size, _ = factors[0].shape
    width = pieces[0].shape[2]
    return pl.pallas_call(
        functools.partial(panel_kernel, arcs),
        out_shape=(
            jax.ShapeDtypeStruct((arcs, width, size), BF16),
            jax.ShapeDtypeStruct((width, width), F32),
        ),
        in_specs=[SM] + [VM] * (len(pieces) + len(factors)),
        out_specs=(VM, VM),
        scratch_shapes=[pltpu.VMEM((arcs, size, width), F32)],
        compiler_params=grant(26),
        name="panel_block",
    )(place, *pieces, *factors)


def back_call(pt, factors):
    arcs, width, size = pt.shape
    return pl.pallas_call(
        back_kernel,
        out_shape=jax.ShapeDtypeStruct((arcs, 2 * width, size), BF16),
        in_specs=[VM] * (1 + len(factors)),
        out_specs=VM,
        compiler_params=grant(26),
        name="back_solve",
    )(pt, *factors)


def normals_kernel(info, far, qs, sums, inv_ref, reg_ref, out_ref, data, acc, sems):
    arcs, _, share = far.shape
    width = inv_ref.shape[0]
    blocks = share // BLK
    half = width // 2
    copies = []
    for arc in range(arcs):
        copies.append(pltpu.make_async_copy(far.at[arc], data.at[arc], sems.at[arc]))
        copies[arc].start()
    for block in range(blocks):
        acc[block] = sums[block]
    for arc in range(arcs):
        copies[arc].wait()

        def add(block, _):
            @pl.when(info[2 + block * 2 * arcs + arcs + arc] > 0)
            def _():
                at = pl.ds(pl.multiple_of(block * BLK, BLK), BLK)
                both = mm(qs[arc], data[arc, :, at])
                acc[block] += both[:width] + both[width:]

            return 0

        lax.fori_loop(0, blocks, add, 0)
    ih, il = split(inv_ref[...])
    row = lax.broadcasted_iota(jnp.int32, (width, BLK), 0) + info[1]
    col = lax.broadcasted_iota(jnp.int32, (width, BLK), 1)
    for block in range(blocks):
        at = slice(block * BLK, (block + 1) * BLK)
        hit = row == col + block * BLK
        th, tl = split(acc[block] + jnp.where(hit, reg_ref[:, at], 0.0))
        for top, end in ((0, half), (half, width)):
            value = mm(ih[top:end, :end], th[:end]) + mm(ih[top:end, :end], tl[:end])
            out_ref[top:end, at] = value + mm(il[top:end, :end], th[:end])


def normals_call(info, far, qfar, sums, inverse, reg):
    arcs, size, share = far.shape
    width = inverse.shape[0]
    hbm = pl.BlockSpec(memory_space=pltpu.HBM)
    return pl.pallas_call(
        normals_kernel,
        out_shape=jax.ShapeDtypeStruct((width, share), F32),
        in_specs=[SM, hbm, VM, VM, VM, VM],
        out_specs=VM,
        scratch_shapes=[
            pltpu.VMEM((arcs, size, share), BF16),
            pltpu.VMEM((share // BLK, width, BLK), F32),
            pltpu.SemaphoreType.DMA((arcs,)),
        ],
        compiler_params=grant(28),
        name="normals",
    )(info, far, qfar, sums, inverse, reg)


SUB = 8


def three(value):
    high = value.astype(BF16)
    rest = value - high.astype(F32)
    mid = rest.astype(BF16)
    return high, mid, (rest - mid.astype(F32)).astype(BF16)


def factor_diag(work, between):
    tn = ((0,), (0,))
    wide = work.shape[1]
    for top in range(0, LANE, SUB):
        rows = [work[top + i : top + i + 1, :] for i in range(SUB)]
        e = {}
        for j in range(SUB):
            for i in range(j, SUB):
                at = top + i
                e[j, i] = jnp.broadcast_to(rows[j][:, at : at + 1], (1, LANE))
        for j in range(SUB):
            inv = lax.rsqrt(e[j, j])
            inv2 = jnp.concatenate([inv] * (wide // LANE), axis=1)
            rows[j] = rows[j] * inv2
            for i in range(j + 1, SUB):
                e[j, i] = e[j, i] * inv
            for i in range(j + 1, SUB):
                for k in range(i, SUB):
                    e[i, k] = e[i, k] - e[j, i] * e[j, k]
                coef = jnp.concatenate([e[j, i]] * (wide // LANE), axis=1)
                rows[i] = rows[i] - coef * rows[j]
        part = jnp.concatenate(rows, axis=0)
        work[top : top + SUB, :] = part
        end = top + SUB
        if end < LANE:
            h, m, l = three(part)
            lhs = jnp.concatenate([h, h, m, m, h, l], axis=0)[:, :LANE]
            rhs = jnp.concatenate([h, m, h, m, l, h], axis=0)
            gone = mm(lhs, rhs, tn)
            work[end:, :] = work[end:, :] - gone[end:, :]
        between()


def chol_body(block_ref, other_ref, reg_ref, out_ref, full, work, upper, between):
    size = block_ref.shape[0]
    row = lax.broadcasted_iota(jnp.int32, (size, size), 0)
    col = lax.broadcasted_iota(jnp.int32, (size, size), 1)
    full[...] = (block_ref[...] + other_ref[...]) + jnp.where(row == col, reg_ref[...], 0.0)
    r1 = lax.broadcasted_iota(jnp.int32, (LANE, LANE), 0)
    c1 = lax.broadcasted_iota(jnp.int32, (LANE, LANE), 1)
    out_ref[...] = jnp.zeros(out_ref.shape, F32)
    for top in range(0, size, LANE):
        end = top + LANE
        work[:, :LANE] = full[top:end, top:end]
        work[:, LANE:] = (r1 == c1).astype(F32)
        factor_diag(work, between)
        inverse = jnp.where(r1 >= c1, work[:, LANE:], 0.0)
        out_ref[top:end, top:end] = inverse
        if end < size:
            right = mm3(inverse, full[top:end, end:])
            upper[top:end, end:] = right
            rt = right.T
            full[end:, end:] = full[end:, end:] - mm3(rt, right)
    step = LANE
    while step < size:
        for base in range(0, size, 2 * step):
            left = slice(base, base + step)
            second = slice(base + step, base + 2 * step)
            low = upper[left, second].T
            out_ref[second, left] = -mm3(out_ref[second, second], mm3(low, out_ref[left, left]))
        step *= 2


def chol_kernel(*refs):
    chol_body(*refs, lambda: None)


def chol_normals_kernel(info, block_ref, other_ref, reg_ref, own, qs, out_ref, sums, full, work, upper, data, sems):
    arcs, size, share = data.shape
    width = block_ref.shape[0]
    blocks = share // BLK
    left = pl.multiple_of(info[0] * BLK, BLK)
    copies = []
    for arc in range(arcs):
        source = own.at[arc, :, pl.ds(left, share)]
        copies.append(pltpu.make_async_copy(source, data.at[arc], sems.at[arc]))
    for copy in copies:
        copy.start()
    for block in range(blocks + 1):
        sums[block] = jnp.zeros((width, BLK), F32)
    span = min(256, size)
    slices = [(arc, block, top) for arc in range(arcs) for block in range(blocks) for top in range(0, size, span)]
    panels = width // SUB
    delay = panels // 4
    state = [0, 0]

    def between():
        state[0] += 1
        if state[0] == delay:
            for copy in copies:
                copy.wait()
        goal = len(slices) * max(state[0] - delay, 0) // (panels - delay)
        while state[1] < goal:
            arc, block, top = slices[state[1]]
            state[1] += 1
            target = jnp.where(info[2 + block * 2 * arcs + arc] > 0, block, blocks)
            at = slice(block * BLK, (block + 1) * BLK)
            rows = slice(top, top + span)
            value = mm(qs[arc, :, rows], data[arc, rows, at])
            sums[target] += value[:width] + value[width:]

    chol_body(block_ref, other_ref, reg_ref, out_ref, full, work, upper, between)


def chol_normals(info, block, other, reg, own, qown):
    arcs, observed, _ = own.shape
    size = block.shape[0]
    share = own.shape[2] // 2
    hbm = pl.BlockSpec(memory_space=pltpu.HBM)
    return pl.pallas_call(
        chol_normals_kernel,
        out_shape=(
            jax.ShapeDtypeStruct((size, size), F32),
            jax.ShapeDtypeStruct((share // BLK + 1, size, BLK), F32),
        ),
        in_specs=[SM, VM, VM, VM, hbm, VM],
        out_specs=(VM, VM),
        scratch_shapes=[
            pltpu.VMEM((size, size), F32),
            pltpu.VMEM((LANE, 2 * LANE), F32),
            pltpu.VMEM((size, size), F32),
            pltpu.VMEM((arcs, observed, share), BF16),
            pltpu.SemaphoreType.DMA((arcs,)),
        ],
        compiler_params=grant(28),
        name="chol_normals",
    )(info, block, other, reg, own, qown)


def chol_inverse(block, other, reg):
    size = block.shape[0]
    vm = pl.BlockSpec(memory_space=pltpu.VMEM)
    return pl.pallas_call(
        chol_kernel,
        out_shape=jax.ShapeDtypeStruct((size, size), F32),
        in_specs=[vm, vm, vm],
        out_specs=vm,
        scratch_shapes=[
            pltpu.VMEM((size, size), F32),
            pltpu.VMEM((LANE, 2 * LANE), F32),
            pltpu.VMEM((size, size), F32),
        ],
        compiler_params=grant(12),
        name="chol_inverse",
    )(block, other, reg)


def block_hits(active, first, count):
    ids = first + jnp.arange(count, dtype=jnp.int32)
    return jnp.any(active[:, :, None] == ids[None, None, :], axis=1)


def factor_rows(cov_factor, me):
    rows = cov_factor.shape[1]
    at = me * rows // LANE * LANE
    strip = lax.dynamic_slice_in_dim(cov_factor, at, LANE, 2)
    high, low = invert_diag(strip, (me * rows % LANE).astype(jnp.int32)[None])
    rest = lax.dynamic_update_slice_in_dim(cov_factor.astype(BF16), high, at, 2)
    return jnp.concatenate([low, rest], axis=2)


def general(design, cov_factor, active_blocks, panel_index, reg_diag):
    arcs, observed, columns = design.shape
    rows = cov_factor.shape[1]
    par_id = lax.axis_index("par")
    arc_id = lax.axis_index("arc")
    lower = lax.all_gather(factor_rows(cov_factor, par_id), "par", axis=1, tiled=True)
    local_blocks = columns // BLK
    hits = block_hits(active_blocks, par_id * local_blocks, local_blocks)
    masked = design * jnp.repeat(hits, BLK, axis=1).astype(BF16)[:, None, :]
    start = panel_index[0] * PANEL
    padded = jnp.pad(masked, ((0, 0), (0, 0), (PANEL, PANEL)))
    window = lax.dynamic_slice_in_dim(
        padded, jnp.clip(start - par_id * columns + PANEL, 0, columns + PANEL), PANEL, 2
    )
    panel = lax.psum(window.astype(F32).astype(BF16), "par")
    factors = invert_call(functools.partial(invert_dense_kernel, rows), arcs, observed, [lower], [])
    place = jnp.zeros((arcs,), jnp.int32)
    pt, block = panel_call(place, [panel[arc : arc + 1] for arc in range(arcs)], factors)
    qs = back_call(pt, factors)
    both = jnp.einsum("apo,aoc->pc", qs, masked, preferred_element_type=F32)
    gram = both[:PANEL] + both[PANEL:]
    share = columns // lax.axis_size("arc")
    gram, block = lax.psum((gram, block), "arc")
    gram = lax.dynamic_slice_in_dim(gram, arc_id * share, share, 1)
    reg_panel = lax.dynamic_slice_in_dim(reg_diag, start, PANEL)
    inverse = chol_inverse(block, jnp.zeros_like(block), reg_panel[None, :])
    global_cols = par_id * columns + arc_id * share + jnp.arange(share, dtype=jnp.int32)
    rows_at = start + jnp.arange(PANEL, dtype=jnp.int32)
    shifted = gram + jnp.where(global_cols[None, :] == rows_at[:, None], reg_panel[:, None], 0.0)
    return jnp.dot(inverse, shifted, precision=lax.Precision.HIGHEST, preferred_element_type=F32)


def paired(design, cov_factor, active_blocks, panel_index, reg_diag):
    arcs, observed, columns = design.shape
    rows = cov_factor.shape[1]
    chips = lax.axis_size("par")
    planes = chips // 4
    me = lax.axis_index("par")
    core = lax.axis_index("arc")
    sides = (me & 1, (me >> 1) & 1)
    plane = me >> 2
    share = columns // 2
    start = panel_index[0] * PANEL

    def swap(value):
        return lax.ppermute(value, "arc", [(0, 1), (1, 0)])

    def hop(value, bits):
        return lax.ppermute(value, "par", [(p, p ^ bits) for p in range(chips)])

    def spread(value, first):
        second = 3 - first
        direct, other = hop(value, first), hop(value, second)
        corner = hop(direct, second)
        return {0: value, first: direct, second: other, 3: corner}

    offset = start - me * columns
    inside = (offset >= 0) & (offset < columns)
    live = jnp.repeat(block_hits(active_blocks, start // BLK, PANEL // BLK) & inside, BLK, axis=1)
    left = jnp.clip(offset, 0, columns - PANEL)
    half, quarter = observed // 2, observed // 4

    def window(arc, top):
        value = lax.dynamic_slice(design, (jnp.int32(arc), top, left), (1, half, PANEL))[0]
        return jnp.where(live[arc][None, :], value, 0)

    sends = [window(arc, (1 - sides[arc % 2]) * half) for arc in range(arcs)]
    sends, cov_factor = lax.optimization_barrier((sends, cov_factor))
    keeps = [window(arc, sides[arc % 2] * half) for arc in range(arcs)]
    seeds = []
    for arc in range(arcs):
        first, second = arc % 2, 1 - arc % 2
        gone = hop(sends[arc], 1 << first)

        def piece(side):
            at = side * quarter
            return lax.dynamic_slice_in_dim(keeps[arc], at, quarter, 0) + lax.dynamic_slice_in_dim(
                gone, at, quarter, 0
            )

        again = piece(1 - sides[second])
        again = hop(again, 1 << second)
        value = piece(sides[second]) + again
        seeds.append(value.reshape(planes, rows, PANEL))
    seeds = jnp.stack(seeds, axis=1)
    chunk = lax.dynamic_index_in_dim(seeds, plane, 0, False)
    for k in range(1, planes):
        gone = hop(lax.dynamic_index_in_dim(seeds, plane ^ k, 0, False), 4 * k)
        chunk += gone

    lower = factor_rows(cov_factor, me)
    stack = [lower]
    for k in range(1, planes):
        stack.append(hop(lower, 4 * k))
    packed = []
    for index in range(planes):
        width = LANE + 4 * rows * (index + 1)
        value = stack[0][:, :, :width]
        for k in range(1, planes):
            value = jnp.where(plane == (index ^ k), stack[k][:, :, :width], value)
        packed.append(value)
    packed = jnp.concatenate(packed, axis=2)
    seats = (me & 3) ^ jnp.arange(4, dtype=jnp.int32)

    first_column = me * columns + core * share
    both = jnp.concatenate([active_blocks, swap(active_blocks)], axis=0)
    lives = block_hits(both, first_column // BLK, share // BLK).T.reshape(-1).astype(jnp.int32)
    info = jnp.stack([core * (share // BLK), start - first_column]).astype(jnp.int32)
    info = jnp.concatenate([info, lives])
    reg = lax.dynamic_slice_in_dim(reg_diag, first_column, share)[None, :]
    reg_panel = lax.dynamic_slice_in_dim(reg_diag, start, PANEL)[None, :]
    source = me ^ (
        jnp.arange(4, dtype=jnp.int32)[:, None] ^ (4 * jnp.arange(planes, dtype=jnp.int32)[None, :])
    )
    place = []
    for arc in range(arcs):
        bits = (source & 1, (source >> 1) & 1)
        order = (bits[arc % 2] * 2 + bits[1 - arc % 2]) * planes + (source >> 2)
        place.append(order.reshape(-1) * rows)
    place = jnp.concatenate(place)
    far = lax.dynamic_slice_in_dim(design, (1 - core) * share, share, 2)
    far = swap(far)
    chunk, seats, info, reg, reg_panel, place = lax.optimization_barrier(
        (chunk, seats, info, reg, reg_panel, place)
    )

    shares = [seats]
    for arc in range(arcs):
        pieces = spread(packed[arc], 1 + arc % 2)
        shares += [pieces[k] for k in range(4)]
    factors = invert_call(
        functools.partial(invert_pieces_kernel, rows), arcs, observed, shares,
        [pltpu.VMEM((arcs, observed, observed), BF16), pltpu.VMEM((arcs, observed, LANE), BF16)],
    )

    stack = [chunk] + [hop(chunk, 4 * k) for k in range(1, planes)]
    stack = jnp.stack(stack, axis=1)
    pieces = []
    for arc in range(arcs):
        found = spread(stack[arc], 1 + arc % 2)
        pieces += [found[k] for k in range(4)]
    pt, block = panel_call(place, pieces, factors)
    other = swap(block)
    qs = back_call(pt, factors)
    qs, other = lax.optimization_barrier((qs, other))
    inverse, sums = chol_normals(info, block, other, reg_panel, design, qs)
    return normals_call(info, far, swap(qs), sums, inverse, reg)


def whole(design, cov_factor, *rest):
    chips = lax.axis_size("par")
    columns = design.shape[2]
    fits = (
        lax.axis_size("arc") == 2
        and design.shape[0] == 2
        and chips == 16
        and columns % PANEL == 0
        and columns % (2 * BLK) == 0
        and LANE % cov_factor.shape[1] == 0
    )
    return (paired if fits else general)(design, cov_factor, *rest)


def solution(mesh):
    in_specs = (P("arc", None, "par"), P("arc", "par", None), P("arc", None), P(), P())
    out_specs = P(None, ("par", "arc"))
    return jax.shard_map(
        whole, mesh=mesh, in_specs=in_specs, out_specs=out_specs, check_vma=False
    )
```

```python
import functools

import jax
import jax.numpy as jnp
from jax import lax
from jax.experimental import pallas as pl
from jax.experimental.pallas import tpu as pltpu
from jax.sharding import PartitionSpec as P


PANEL = 512
BLK = 256
F32, BF16 = jnp.float32, jnp.bfloat16
LANE = 128


def split(value):
    high = value.astype(BF16)
    return high, (value - high.astype(F32)).astype(BF16)


def mm(a, b, dims=((1,), (0,))):
    return lax.dot_general(a, b, (dims, ((), ())), preferred_element_type=F32)


def mm3(a, b):
    ah, al = split(a)
    bh, bl = split(b)
    return mm(ah, bh) + (mm(ah, bl) + mm(al, bh))


def level_mask(step):
    rows = lax.broadcasted_iota(jnp.int32, (LANE, LANE), 0)
    cols = lax.broadcasted_iota(jnp.int32, (LANE, LANE), 1)
    return (
        (rows // (2 * step) == cols // (2 * step))
        & ((rows // step) % 2 == 1)
        & ((cols // step) % 2 == 0)
    )


def rows_kernel(place_ref, rows_ref, out_ref, square):
    arcs, rows, _ = rows_ref.shape
    at = pl.multiple_of(place_ref[0], LANE)
    off = pl.multiple_of(place_ref[1], 16)
    r = lax.broadcasted_iota(jnp.int32, (LANE, LANE), 0)
    c = lax.broadcasted_iota(jnp.int32, (LANE, LANE), 1)
    eye = r == c
    sub = lax.broadcasted_iota(jnp.int32, (rows, LANE), 1)
    own = (sub >= off) & (sub < off + rows)
    strips = [rows_ref[arc, :, pl.ds(at, LANE)] for arc in range(arcs)]
    for arc in range(arcs):
        out_ref[arc, :, LANE:] = rows_ref[arc].astype(BF16)
        square[arc] = eye.astype(F32)
        square[arc, pl.ds(off, rows), :] = jnp.where(own, strips[arc], 0.0)
    lowers = [square[arc] for arc in range(arcs)]
    invs = [jnp.where(eye, 1.0 / jnp.where(eye, low, 1.0), 0.0) for low in lowers]
    step = 1
    while step < rows:
        mask = level_mask(step)
        parts = [mm3(jnp.where(mask, low, 0.0), inv) for low, inv in zip(lowers, invs)]
        invs = [inv - mm3(inv, part) for inv, part in zip(invs, parts)]
        step *= 2
    for arc in range(arcs):
        square[arc] = invs[arc]
        value = jnp.where(own, square[arc, pl.ds(off, rows), :], strips[arc])
        high, low = split(value)
        out_ref[arc, :, pl.ds(at + LANE, LANE)] = high
        out_ref[arc, :, :LANE] = low


def factor_rows(cov_factor, me):
    arcs, rows, size = cov_factor.shape
    at = me * rows // LANE * LANE
    place = jnp.stack([at, me * rows - at]).astype(jnp.int32)
    return pl.pallas_call(
        rows_kernel,
        out_shape=jax.ShapeDtypeStruct((arcs, rows, LANE + size), BF16),
        in_specs=[pl.BlockSpec(memory_space=pltpu.SMEM), pl.BlockSpec(memory_space=pltpu.VMEM)],
        out_specs=pl.BlockSpec(memory_space=pltpu.VMEM),
        scratch_shapes=[pltpu.VMEM((arcs, LANE, LANE), F32)],
        compiler_params=pltpu.CompilerParams(vmem_limit_bytes=8 << 20),
        name="factor_rows",
    )(place, cov_factor)


def invert_factor(rest, fine, high, low, first):
    size = high.shape[0]
    half = max(size // 2, LANE)
    for top in range(0, size, half):
        for ref in (high, low):
            ref[top : top + half, top : top + half] = jnp.zeros((half, half), BF16)
    rows = lax.broadcasted_iota(jnp.int32, (LANE, LANE), 0) // first
    cols = lax.broadcasted_iota(jnp.int32, (LANE, LANE), 1) // first
    blocks = [
        rest[t : t + LANE, t : t + LANE].astype(F32) + fine[t : t + LANE, :].astype(F32)
        for t in range(0, size, LANE)
    ]
    invs = [jnp.where(rows == cols, block, 0.0) for block in blocks]
    step = first
    while step < LANE:
        mask = level_mask(step)
        parts = [mm3(jnp.where(mask, block, 0.0), inv) for block, inv in zip(blocks, invs)]
        invs = [inv - mm3(inv, part) for inv, part in zip(invs, parts)]
        step *= 2
    for index, inv in enumerate(invs):
        at = slice(index * LANE, (index + 1) * LANE)
        high[at, at], low[at, at] = split(inv)
    step = LANE
    while step < size:
        for base in range(0, size, 2 * step):
            left = slice(base, base + step)
            right = slice(base + step, base + 2 * step)
            below = rest[right, left]
            ph, pl_ = split(mm(below, high[left, left]) + mm(below, low[left, left]))
            ch, cl = high[right, right], low[right, right]
            high[right, left], low[right, left] = split(-(mm(ch, ph) + (mm(ch, pl_) + mm(cl, ph))))
        step *= 2


VM = pl.BlockSpec(memory_space=pltpu.VMEM)
SM = pl.BlockSpec(memory_space=pltpu.SMEM)
MIB = 1 << 20


def grant(mib):
    return pltpu.CompilerParams(vmem_limit_bytes=mib * MIB)


def invert_pieces_kernel(first, place_ref, *refs):
    pieces, (high, low, rest, fine) = refs[:-4], refs[-4:]
    arcs, size, _ = high.shape
    rows = pieces[0].shape[0]
    planes = size // (4 * rows)
    for index, piece in enumerate(pieces):
        arc, seat = index // 4, place_ref[index % 4]
        left = 0
        for plane in range(planes):
            width = 4 * rows * (plane + 1)
            at = pl.multiple_of((4 * plane + seat) * rows, 16)
            fine[arc, pl.ds(at, rows), :] = piece[:, left : left + LANE]
            rest[arc, pl.ds(at, rows), :width] = piece[:, left + LANE : left + LANE + width]
            left += LANE + width

    def one(arc, _):
        invert_factor(rest.at[arc], fine.at[arc], high.at[arc], low.at[arc], first)
        return 0

    lax.fori_loop(0, arcs, one, 0)


def invert_dense_kernel(first, rows_ref, high, low):
    def one(arc, _):
        both = rows_ref.at[arc]
        invert_factor(both.at[:, LANE:], both.at[:, :LANE], high.at[arc], low.at[arc], first)
        return 0

    lax.fori_loop(0, rows_ref.shape[0], one, 0)


def invert_call(kernel, arcs, size, operands, scratch):
    out = jax.ShapeDtypeStruct((arcs, size, size), BF16)
    return pl.pallas_call(
        kernel,
        out_shape=(out, out),
        in_specs=[SM if value.dtype == jnp.int32 else VM for value in operands],
        out_specs=(VM, VM),
        scratch_shapes=scratch,
        compiler_params=grant(28),
        name="invert_factor",
    )(*operands)


def panel_kernel(arcs, place_ref, *refs):
    pieces, (high, low, pt, block_ref, panel) = refs[:-5], refs[-5:]
    count = len(pieces) // arcs
    size = panel.shape[1]
    span = min(256, size)
    nt = ((1,), (1,))
    for arc in range(arcs):
        index = arc * pieces[0].shape[0] * count
        for piece in pieces[arc * count : (arc + 1) * count]:
            rows = piece.shape[1]
            for z in range(piece.shape[0]):
                at = pl.multiple_of(place_ref[index], 16)
                panel[arc, pl.ds(at, rows), :] = piece[z].astype(F32)
                index += 1
    block_ref[...] = jnp.zeros_like(block_ref)

    def one(arc, _):
        raw = panel[arc].T.astype(BF16)
        for top in range(0, size, span):
            end = top + span
            value = mm(raw[:, :end], high[arc, top:end, :end], nt)
            value += mm(raw[:, :end], low[arc, top:end, :end], nt)
            pt[arc, :, top:end] = value.astype(BF16)
        block_ref[...] += mm(pt[arc], pt[arc], nt)
        return 0

    lax.fori_loop(0, arcs, one, 0)


def back_kernel(pt, high, low, q_ref):
    arcs, width, size = pt.shape
    span = min(256, size)

    def one(arc, _):
        for top in range(0, size, span):
            end = top + span
            part = pt[arc, :, top:]
            value = mm(part, high[arc, top:, top:end]) + mm(part, low[arc, top:, top:end])
            q_ref[arc, :width, top:end], q_ref[arc, width:, top:end] = split(value)
        return 0

    lax.fori_loop(0, arcs, one, 0)


def panel_call(place, pieces, factors):
    arcs, size, _ = factors[0].shape
    width = pieces[0].shape[2]
    return pl.pallas_call(
        functools.partial(panel_kernel, arcs),
        out_shape=(
            jax.ShapeDtypeStruct((arcs, width, size), BF16),
            jax.ShapeDtypeStruct((width, width), F32),
        ),
        in_specs=[SM] + [VM] * (len(pieces) + len(factors)),
        out_specs=(VM, VM),
        scratch_shapes=[pltpu.VMEM((arcs, size, width), F32)],
        compiler_params=grant(26),
        name="panel_block",
    )(place, *pieces, *factors)


def back_call(pt, factors):
    arcs, width, size = pt.shape
    return pl.pallas_call(
        back_kernel,
        out_shape=jax.ShapeDtypeStruct((arcs, 2 * width, size), BF16),
        in_specs=[VM] * (1 + len(factors)),
        out_specs=VM,
        compiler_params=grant(26),
        name="back_solve",
    )(pt, *factors)


def normals_kernel(info, far, qs, sums, inv_ref, reg_ref, out_ref, data, acc, sems):
    arcs, _, share = far.shape
    width = inv_ref.shape[0]
    blocks = share // BLK
    half = width // 2
    copies = []
    for arc in range(arcs):
        copies.append(pltpu.make_async_copy(far.at[arc], data.at[arc], sems.at[arc]))
        copies[arc].start()
    for block in range(blocks):
        acc[block] = sums[block]
    for arc in range(arcs):
        copies[arc].wait()

        def add(block, _):
            @pl.when(info[2 + block * 2 * arcs + arcs + arc] > 0)
            def _():
                at = pl.ds(pl.multiple_of(block * BLK, BLK), BLK)
                both = mm(qs[arc], data[arc, :, at])
                acc[block] += both[:width] + both[width:]

            return 0

        lax.fori_loop(0, blocks, add, 0)
    ih, il = split(inv_ref[...])
    row = lax.broadcasted_iota(jnp.int32, (width, BLK), 0) + info[1]
    col = lax.broadcasted_iota(jnp.int32, (width, BLK), 1)
    for block in range(blocks):
        at = slice(block * BLK, (block + 1) * BLK)
        hit = row == col + block * BLK
        th, tl = split(acc[block] + jnp.where(hit, reg_ref[:, at], 0.0))
        for top, end in ((0, half), (half, width)):
            value = mm(ih[top:end, :end], th[:end]) + mm(ih[top:end, :end], tl[:end])
            out_ref[top:end, at] = value + mm(il[top:end, :end], th[:end])


def normals_call(info, far, qfar, sums, inverse, reg):
    arcs, size, share = far.shape
    width = inverse.shape[0]
    hbm = pl.BlockSpec(memory_space=pltpu.HBM)
    return pl.pallas_call(
        normals_kernel,
        out_shape=jax.ShapeDtypeStruct((width, share), F32),
        in_specs=[SM, hbm, VM, VM, VM, VM],
        out_specs=VM,
        scratch_shapes=[
            pltpu.VMEM((arcs, size, share), BF16),
            pltpu.VMEM((share // BLK, width, BLK), F32),
            pltpu.SemaphoreType.DMA((arcs,)),
        ],
        compiler_params=grant(28),
        name="normals",
    )(info, far, qfar, sums, inverse, reg)


SUB = 8


def three(value):
    high = value.astype(BF16)
    rest = value - high.astype(F32)
    mid = rest.astype(BF16)
    return high, mid, (rest - mid.astype(F32)).astype(BF16)


def factor_diag(work, between):
    tn = ((0,), (0,))
    wide = work.shape[1]
    for top in range(0, LANE, SUB):
        rows = [work[top + i : top + i + 1, :] for i in range(SUB)]
        e = {}
        for j in range(SUB):
            for i in range(j, SUB):
                at = top + i
                e[j, i] = jnp.broadcast_to(rows[j][:, at : at + 1], (1, LANE))
        for j in range(SUB):
            inv = lax.rsqrt(e[j, j])
            inv2 = jnp.concatenate([inv] * (wide // LANE), axis=1)
            rows[j] = rows[j] * inv2
            for i in range(j + 1, SUB):
                e[j, i] = e[j, i] * inv
            for i in range(j + 1, SUB):
                for k in range(i, SUB):
                    e[i, k] = e[i, k] - e[j, i] * e[j, k]
                coef = jnp.concatenate([e[j, i]] * (wide // LANE), axis=1)
                rows[i] = rows[i] - coef * rows[j]
        part = jnp.concatenate(rows, axis=0)
        work[top : top + SUB, :] = part
        end = top + SUB
        if end < LANE:
            h, m, l = three(part)
            lhs = jnp.concatenate([h, h, m, m, h, l], axis=0)[:, :LANE]
            rhs = jnp.concatenate([h, m, h, m, l, h], axis=0)
            gone = mm(lhs, rhs, tn)
            work[end:, :] = work[end:, :] - gone[end:, :]
        between()


def chol_body(block_ref, other_ref, reg_ref, out_ref, full, work, upper, between):
    size = block_ref.shape[0]
    row = lax.broadcasted_iota(jnp.int32, (size, size), 0)
    col = lax.broadcasted_iota(jnp.int32, (size, size), 1)
    full[...] = (block_ref[...] + other_ref[...]) + jnp.where(row == col, reg_ref[...], 0.0)
    r1 = lax.broadcasted_iota(jnp.int32, (LANE, LANE), 0)
    c1 = lax.broadcasted_iota(jnp.int32, (LANE, LANE), 1)
    out_ref[...] = jnp.zeros(out_ref.shape, F32)
    for top in range(0, size, LANE):
        end = top + LANE
        work[:, :LANE] = full[top:end, top:end]
        work[:, LANE:] = (r1 == c1).astype(F32)
        factor_diag(work, between)
        inverse = jnp.where(r1 >= c1, work[:, LANE:], 0.0)
        out_ref[top:end, top:end] = inverse
        if end < size:
            right = mm3(inverse, full[top:end, end:])
            upper[top:end, end:] = right
            rt = right.T
            full[end:, end:] = full[end:, end:] - mm3(rt, right)
    step = LANE
    while step < size:
        for base in range(0, size, 2 * step):
            left = slice(base, base + step)
            second = slice(base + step, base + 2 * step)
            low = upper[left, second].T
            out_ref[second, left] = -mm3(out_ref[second, second], mm3(low, out_ref[left, left]))
        step *= 2


def chol_kernel(*refs):
    chol_body(*refs, lambda: None)


def chol_normals_kernel(info, block_ref, other_ref, reg_ref, own, qs, out_ref, sums, full, work, upper, data, sems):
    arcs, size, share = data.shape
    width = block_ref.shape[0]
    blocks = share // BLK
    left = pl.multiple_of(info[0] * BLK, BLK)
    copies = []
    for arc in range(arcs):
        source = own.at[arc, :, pl.ds(left, share)]
        copies.append(pltpu.make_async_copy(source, data.at[arc], sems.at[arc]))
    for copy in copies:
        copy.start()
    for block in range(blocks + 1):
        sums[block] = jnp.zeros((width, BLK), F32)
    span = min(256, size)
    slices = [(arc, block, top) for arc in range(arcs) for block in range(blocks) for top in range(0, size, span)]
    panels = width // SUB
    delay = panels // 4
    state = [0, 0]

    def between():
        state[0] += 1
        if state[0] == delay:
            for copy in copies:
                copy.wait()
        goal = len(slices) * max(state[0] - delay, 0) // (panels - delay)
        while state[1] < goal:
            arc, block, top = slices[state[1]]
            state[1] += 1
            target = jnp.where(info[2 + block * 2 * arcs + arc] > 0, block, blocks)
            at = slice(block * BLK, (block + 1) * BLK)
            rows = slice(top, top + span)
            value = mm(qs[arc, :, rows], data[arc, rows, at])
            sums[target] += value[:width] + value[width:]

    chol_body(block_ref, other_ref, reg_ref, out_ref, full, work, upper, between)


def chol_normals(info, block, other, reg, own, qown):
    arcs, observed, _ = own.shape
    size = block.shape[0]
    share = own.shape[2] // 2
    hbm = pl.BlockSpec(memory_space=pltpu.HBM)
    return pl.pallas_call(
        chol_normals_kernel,
        out_shape=(
            jax.ShapeDtypeStruct((size, size), F32),
            jax.ShapeDtypeStruct((share // BLK + 1, size, BLK), F32),
        ),
        in_specs=[SM, VM, VM, VM, hbm, VM],
        out_specs=(VM, VM),
        scratch_shapes=[
            pltpu.VMEM((size, size), F32),
            pltpu.VMEM((LANE, 2 * LANE), F32),
            pltpu.VMEM((size, size), F32),
            pltpu.VMEM((arcs, observed, share), BF16),
            pltpu.SemaphoreType.DMA((arcs,)),
        ],
        compiler_params=grant(28),
        name="chol_normals",
    )(info, block, other, reg, own, qown)


def chol_inverse(block, other, reg):
    size = block.shape[0]
    vm = pl.BlockSpec(memory_space=pltpu.VMEM)
    return pl.pallas_call(
        chol_kernel,
        out_shape=jax.ShapeDtypeStruct((size, size), F32),
        in_specs=[vm, vm, vm],
        out_specs=vm,
        scratch_shapes=[
            pltpu.VMEM((size, size), F32),
            pltpu.VMEM((LANE, 2 * LANE), F32),
            pltpu.VMEM((size, size), F32),
        ],
        compiler_params=grant(12),
        name="chol_inverse",
    )(block, other, reg)


def block_hits(active, first, count):
    ids = first + jnp.arange(count, dtype=jnp.int32)
    return jnp.any(active[:, :, None] == ids[None, None, :], axis=1)


def general(design, cov_factor, active_blocks, panel_index, reg_diag):
    arcs, observed, columns = design.shape
    rows = cov_factor.shape[1]
    par_id = lax.axis_index("par")
    arc_id = lax.axis_index("arc")
    lower = lax.all_gather(factor_rows(cov_factor, par_id), "par", axis=1, tiled=True)
    local_blocks = columns // BLK
    hits = block_hits(active_blocks, par_id * local_blocks, local_blocks)
    masked = design * jnp.repeat(hits, BLK, axis=1).astype(BF16)[:, None, :]
    start = panel_index[0] * PANEL
    padded = jnp.pad(masked, ((0, 0), (0, 0), (PANEL, PANEL)))
    window = lax.dynamic_slice_in_dim(
        padded, jnp.clip(start - par_id * columns + PANEL, 0, columns + PANEL), PANEL, 2
    )
    panel = lax.psum(window.astype(F32).astype(BF16), "par")
    factors = invert_call(functools.partial(invert_dense_kernel, rows), arcs, observed, [lower], [])
    place = jnp.zeros((arcs,), jnp.int32)
    pt, block = panel_call(place, [panel[arc : arc + 1] for arc in range(arcs)], factors)
    qs = back_call(pt, factors)
    both = jnp.einsum("apo,aoc->pc", qs, masked, preferred_element_type=F32)
    gram = both[:PANEL] + both[PANEL:]
    share = columns // lax.axis_size("arc")
    gram, block = lax.psum((gram, block), "arc")
    gram = lax.dynamic_slice_in_dim(gram, arc_id * share, share, 1)
    reg_panel = lax.dynamic_slice_in_dim(reg_diag, start, PANEL)
    inverse = chol_inverse(block, jnp.zeros_like(block), reg_panel[None, :])
    global_cols = par_id * columns + arc_id * share + jnp.arange(share, dtype=jnp.int32)
    rows_at = start + jnp.arange(PANEL, dtype=jnp.int32)
    shifted = gram + jnp.where(global_cols[None, :] == rows_at[:, None], reg_panel[:, None], 0.0)
    return jnp.dot(inverse, shifted, precision=lax.Precision.HIGHEST, preferred_element_type=F32)


def paired(design, cov_factor, active_blocks, panel_index, reg_diag):
    arcs, observed, columns = design.shape
    rows = cov_factor.shape[1]
    chips = lax.axis_size("par")
    planes = chips // 4
    me = lax.axis_index("par")
    core = lax.axis_index("arc")
    sides = (me & 1, (me >> 1) & 1)
    plane = me >> 2
    share = columns // 2
    start = panel_index[0] * PANEL

    def swap(value):
        return lax.ppermute(value, "arc", [(0, 1), (1, 0)])

    def hop(value, bits):
        return lax.ppermute(value, "par", [(p, p ^ bits) for p in range(chips)])

    def spread(value, first):
        second = 3 - first
        direct, other = hop(value, first), hop(value, second)
        corner = hop(direct, second)
        return {0: value, first: direct, second: other, 3: corner}

    offset = start - me * columns
    inside = (offset >= 0) & (offset < columns)
    live = jnp.repeat(block_hits(active_blocks, start // BLK, PANEL // BLK) & inside, BLK, axis=1)
    left = jnp.clip(offset, 0, columns - PANEL)
    half, quarter = observed // 2, observed // 4

    def window(arc, top):
        value = lax.dynamic_slice(design, (jnp.int32(arc), top, left), (1, half, PANEL))[0]
        return jnp.where(live[arc][None, :], value, 0)

    sends = [window(arc, (1 - sides[arc % 2]) * half) for arc in range(arcs)]
    sends, cov_factor = lax.optimization_barrier((sends, cov_factor))
    keeps = [window(arc, sides[arc % 2] * half) for arc in range(arcs)]
    seeds = []
    for arc in range(arcs):
        first, second = arc % 2, 1 - arc % 2
        gone = hop(sends[arc], 1 << first)

        def piece(side):
            at = side * quarter
            return lax.dynamic_slice_in_dim(keeps[arc], at, quarter, 0) + lax.dynamic_slice_in_dim(
                gone, at, quarter, 0
            )

        again = piece(1 - sides[second])
        again = hop(again, 1 << second)
        value = piece(sides[second]) + again
        seeds.append(value.reshape(planes, rows, PANEL))
    seeds = jnp.stack(seeds, axis=1)
    chunk = lax.dynamic_index_in_dim(seeds, plane, 0, False)
    for k in range(1, planes):
        gone = hop(lax.dynamic_index_in_dim(seeds, plane ^ k, 0, False), 4 * k)
        chunk += gone

    lower = factor_rows(cov_factor, me)
    near = {0: lower}
    for sign in (1, -1):
        value = lower
        for k in range(1, planes):
            low, top = (k - 1, planes - 1) if sign > 0 else (1, planes - k + 1)
            pairs = [(p, p + 4 * sign) for p in range(4 * low, 4 * top)]
            value = lax.ppermute(value, "par", pairs)
            near[sign * k] = value
    packed = []
    for index in range(planes):
        width = LANE + 4 * rows * (index + 1)
        value = lower[:, :, :width]
        for source in range(planes):
            if source != index:
                value = jnp.where(plane == source, near[source - index][:, :, :width], value)
        packed.append(value)
    packed = jnp.concatenate(packed, axis=2)
    seats = (me & 3) ^ jnp.arange(4, dtype=jnp.int32)

    first_column = me * columns + core * share
    both = jnp.concatenate([active_blocks, swap(active_blocks)], axis=0)
    lives = block_hits(both, first_column // BLK, share // BLK).T.reshape(-1).astype(jnp.int32)
    info = jnp.stack([core * (share // BLK), start - first_column]).astype(jnp.int32)
    info = jnp.concatenate([info, lives])
    reg = lax.dynamic_slice_in_dim(reg_diag, first_column, share)[None, :]
    reg_panel = lax.dynamic_slice_in_dim(reg_diag, start, PANEL)[None, :]
    source = me ^ (
        jnp.arange(4, dtype=jnp.int32)[:, None] ^ (4 * jnp.arange(planes, dtype=jnp.int32)[None, :])
    )
    place = []
    for arc in range(arcs):
        bits = (source & 1, (source >> 1) & 1)
        order = (bits[arc % 2] * 2 + bits[1 - arc % 2]) * planes + (source >> 2)
        place.append(order.reshape(-1) * rows)
    place = jnp.concatenate(place)
    far = lax.dynamic_slice_in_dim(design, (1 - core) * share, share, 2)
    far = swap(far)
    chunk, seats, info, reg, reg_panel, place = lax.optimization_barrier(
        (chunk, seats, info, reg, reg_panel, place)
    )

    shares = [seats]
    for arc in range(arcs):
        pieces = spread(packed[arc], 1 + arc % 2)
        shares += [pieces[k] for k in range(4)]
    factors = invert_call(
        functools.partial(invert_pieces_kernel, rows), arcs, observed, shares,
        [pltpu.VMEM((arcs, observed, observed), BF16), pltpu.VMEM((arcs, observed, LANE), BF16)],
    )

    stack = [chunk] + [hop(chunk, 4 * k) for k in range(1, planes)]
    stack = jnp.stack(stack, axis=1)
    pieces = []
    for arc in range(arcs):
        found = spread(stack[arc], 1 + arc % 2)
        pieces += [found[k] for k in range(4)]
    pt, block = panel_call(place, pieces, factors)
    other = swap(block)
    qs = back_call(pt, factors)
    qs, other = lax.optimization_barrier((qs, other))
    inverse, sums = chol_normals(info, block, other, reg_panel, design, qs)
    return normals_call(info, far, swap(qs), sums, inverse, reg)


def whole(design, cov_factor, *rest):
    chips = lax.axis_size("par")
    columns = design.shape[2]
    fits = (
        lax.axis_size("arc") == 2
        and design.shape[0] == 2
        and chips == 16
        and columns % PANEL == 0
        and columns % (2 * BLK) == 0
        and LANE % cov_factor.shape[1] == 0
    )
    return (paired if fits else general)(design, cov_factor, *rest)


def solution(mesh):
    in_specs = (P("arc", None, "par"), P("arc", "par", None), P("arc", None), P(), P())
    out_specs = P(None, ("par", "arc"))
    return jax.shard_map(
        whole, mesh=mesh, in_specs=in_specs, out_specs=out_specs, check_vma=False
    )
```

```python
import functools

import jax
import jax.numpy as jnp
from jax import lax
from jax.experimental import pallas as pl
from jax.experimental.pallas import tpu as pltpu
from jax.sharding import PartitionSpec as P


PANEL = 512
BLK = 256
F32, BF16 = jnp.float32, jnp.bfloat16
LANE = 128


def split(value):
    high = value.astype(BF16)
    return high, (value - high.astype(F32)).astype(BF16)


def mm(a, b, dims=((1,), (0,))):
    return lax.dot_general(a, b, (dims, ((), ())), preferred_element_type=F32)


def mm3(a, b):
    ah, al = split(a)
    bh, bl = split(b)
    return mm(ah, bh) + (mm(ah, bl) + mm(al, bh))


def level_mask(step):
    rows = lax.broadcasted_iota(jnp.int32, (LANE, LANE), 0)
    cols = lax.broadcasted_iota(jnp.int32, (LANE, LANE), 1)
    return (
        (rows // (2 * step) == cols // (2 * step))
        & ((rows // step) % 2 == 1)
        & ((cols // step) % 2 == 0)
    )


def rows_kernel(place_ref, rows_ref, out_ref, square):
    arcs, rows, _ = rows_ref.shape
    at = pl.multiple_of(place_ref[0], LANE)
    off = pl.multiple_of(place_ref[1], 16)
    r = lax.broadcasted_iota(jnp.int32, (LANE, LANE), 0)
    c = lax.broadcasted_iota(jnp.int32, (LANE, LANE), 1)
    eye = r == c
    sub = lax.broadcasted_iota(jnp.int32, (rows, LANE), 1)
    own = (sub >= off) & (sub < off + rows)
    strips = [rows_ref[arc, :, pl.ds(at, LANE)] for arc in range(arcs)]
    for arc in range(arcs):
        out_ref[arc, :, LANE:] = rows_ref[arc].astype(BF16)
        square[arc] = eye.astype(F32)
        square[arc, pl.ds(off, rows), :] = jnp.where(own, strips[arc], 0.0)
    lowers = [square[arc] for arc in range(arcs)]
    invs = [jnp.where(eye, 1.0 / jnp.where(eye, low, 1.0), 0.0) for low in lowers]
    step = 1
    while step < rows:
        mask = level_mask(step)
        parts = [mm3(jnp.where(mask, low, 0.0), inv) for low, inv in zip(lowers, invs)]
        invs = [inv - mm3(inv, part) for inv, part in zip(invs, parts)]
        step *= 2
    for arc in range(arcs):
        square[arc] = invs[arc]
        value = jnp.where(own, square[arc, pl.ds(off, rows), :], strips[arc])
        high, low = split(value)
        out_ref[arc, :, pl.ds(at + LANE, LANE)] = high
        out_ref[arc, :, :LANE] = low


def factor_rows(cov_factor, me):
    arcs, rows, size = cov_factor.shape
    at = me * rows // LANE * LANE
    place = jnp.stack([at, me * rows - at]).astype(jnp.int32)
    return pl.pallas_call(
        rows_kernel,
        out_shape=jax.ShapeDtypeStruct((arcs, rows, LANE + size), BF16),
        in_specs=[pl.BlockSpec(memory_space=pltpu.SMEM), pl.BlockSpec(memory_space=pltpu.VMEM)],
        out_specs=pl.BlockSpec(memory_space=pltpu.VMEM),
        scratch_shapes=[pltpu.VMEM((arcs, LANE, LANE), F32)],
        compiler_params=pltpu.CompilerParams(vmem_limit_bytes=8 << 20),
        name="factor_rows",
    )(place, cov_factor)


def invert_factor(rest, fine, high, low, first):
    size = high.shape[0]
    half = max(size // 2, LANE)
    for top in range(0, size, half):
        for ref in (high, low):
            ref[top : top + half, top : top + half] = jnp.zeros((half, half), BF16)
    rows = lax.broadcasted_iota(jnp.int32, (LANE, LANE), 0) // first
    cols = lax.broadcasted_iota(jnp.int32, (LANE, LANE), 1) // first
    blocks = [
        rest[t : t + LANE, t : t + LANE].astype(F32) + fine[t : t + LANE, :].astype(F32)
        for t in range(0, size, LANE)
    ]
    invs = [jnp.where(rows == cols, block, 0.0) for block in blocks]
    step = first
    while step < LANE:
        mask = level_mask(step)
        parts = [mm3(jnp.where(mask, block, 0.0), inv) for block, inv in zip(blocks, invs)]
        invs = [inv - mm3(inv, part) for inv, part in zip(invs, parts)]
        step *= 2
    for index, inv in enumerate(invs):
        at = slice(index * LANE, (index + 1) * LANE)
        high[at, at], low[at, at] = split(inv)
    step = LANE
    while step < size:
        for base in range(0, size, 2 * step):
            left = slice(base, base + step)
            right = slice(base + step, base + 2 * step)
            below = rest[right, left]
            ph, pl_ = split(mm(below, high[left, left]) + mm(below, low[left, left]))
            ch, cl = high[right, right], low[right, right]
            high[right, left], low[right, left] = split(-(mm(ch, ph) + (mm(ch, pl_) + mm(cl, ph))))
        step *= 2


VM = pl.BlockSpec(memory_space=pltpu.VMEM)
SM = pl.BlockSpec(memory_space=pltpu.SMEM)
MIB = 1 << 20


def grant(mib):
    return pltpu.CompilerParams(vmem_limit_bytes=mib * MIB)


def invert_pieces_kernel(first, place_ref, *refs):
    pieces, (high, low, rest, fine) = refs[:-4], refs[-4:]
    arcs, _, _ = high.shape
    rows = pieces[0].shape[0]

    def unpack(outer):
        for index, piece in enumerate(pieces):
            arc, seat = index // 8, place_ref[index % 4]
            left = 0
            for plane in (0, 3) if (index // 4 % 2 == 0) == outer else (1, 2):
                width = 4 * rows * (plane + 1)
                at = pl.multiple_of((4 * plane + seat) * rows, 16)
                fine[arc, pl.ds(at, rows), :] = piece[:, left : left + LANE]
                rest[arc, pl.ds(at, rows), :width] = piece[:, left + LANE : left + LANE + width]
                left += LANE + width

    @pl.when(place_ref[4] > 0)
    def _():
        unpack(True)

    @pl.when(place_ref[4] == 0)
    def _():
        unpack(False)

    def one(arc, _):
        invert_factor(rest.at[arc], fine.at[arc], high.at[arc], low.at[arc], first)
        return 0

    lax.fori_loop(0, arcs, one, 0)


def invert_dense_kernel(first, rows_ref, high, low):
    def one(arc, _):
        both = rows_ref.at[arc]
        invert_factor(both.at[:, LANE:], both.at[:, :LANE], high.at[arc], low.at[arc], first)
        return 0

    lax.fori_loop(0, rows_ref.shape[0], one, 0)


def invert_call(kernel, arcs, size, operands, scratch):
    out = jax.ShapeDtypeStruct((arcs, size, size), BF16)
    return pl.pallas_call(
        kernel,
        out_shape=(out, out),
        in_specs=[SM if value.dtype == jnp.int32 else VM for value in operands],
        out_specs=(VM, VM),
        scratch_shapes=scratch,
        compiler_params=grant(28),
        name="invert_factor",
    )(*operands)


def panel_kernel(arcs, place_ref, *refs):
    pieces, (high, low, pt, block_ref, panel) = refs[:-5], refs[-5:]
    count = len(pieces) // arcs
    size = panel.shape[1]
    span = min(256, size)
    nt = ((1,), (1,))
    for arc in range(arcs):
        index = arc * pieces[0].shape[0] * count
        for piece in pieces[arc * count : (arc + 1) * count]:
            rows = piece.shape[1]
            for z in range(piece.shape[0]):
                at = pl.multiple_of(place_ref[index], 16)
                panel[arc, pl.ds(at, rows), :] = piece[z].astype(F32)
                index += 1
    block_ref[...] = jnp.zeros_like(block_ref)

    def one(arc, _):
        raw = panel[arc].T.astype(BF16)
        for top in range(0, size, span):
            end = top + span
            value = mm(raw[:, :end], high[arc, top:end, :end], nt)
            value += mm(raw[:, :end], low[arc, top:end, :end], nt)
            pt[arc, :, top:end] = value.astype(BF16)
        block_ref[...] += mm(pt[arc], pt[arc], nt)
        return 0

    lax.fori_loop(0, arcs, one, 0)


def back_kernel(pt, high, low, q_ref):
    arcs, width, size = pt.shape
    span = min(256, size)

    def one(arc, _):
        for top in range(0, size, span):
            end = top + span
            part = pt[arc, :, top:]
            value = mm(part, high[arc, top:, top:end]) + mm(part, low[arc, top:, top:end])
            q_ref[arc, :width, top:end], q_ref[arc, width:, top:end] = split(value)
        return 0

    lax.fori_loop(0, arcs, one, 0)


def panel_call(place, pieces, factors):
    arcs, size, _ = factors[0].shape
    width = pieces[0].shape[2]
    return pl.pallas_call(
        functools.partial(panel_kernel, arcs),
        out_shape=(
            jax.ShapeDtypeStruct((arcs, width, size), BF16),
            jax.ShapeDtypeStruct((width, width), F32),
        ),
        in_specs=[SM] + [VM] * (len(pieces) + len(factors)),
        out_specs=(VM, VM),
        scratch_shapes=[pltpu.VMEM((arcs, size, width), F32)],
        compiler_params=grant(26),
        name="panel_block",
    )(place, *pieces, *factors)


def back_call(pt, factors):
    arcs, width, size = pt.shape
    return pl.pallas_call(
        back_kernel,
        out_shape=jax.ShapeDtypeStruct((arcs, 2 * width, size), BF16),
        in_specs=[VM] * (1 + len(factors)),
        out_specs=VM,
        compiler_params=grant(26),
        name="back_solve",
    )(pt, *factors)


def normals_kernel(info, far, qs, sums, inv_ref, reg_ref, out_ref, data, acc, sems):
    arcs, _, share = far.shape
    width = inv_ref.shape[0]
    blocks = share // BLK
    half = width // 2
    copies = []
    for arc in range(arcs):
        copies.append(pltpu.make_async_copy(far.at[arc], data.at[arc], sems.at[arc]))
        copies[arc].start()
    for block in range(blocks):
        acc[block] = sums[block]
    for arc in range(arcs):
        copies[arc].wait()

        def add(block, _):
            @pl.when(info[2 + block * 2 * arcs + arcs + arc] > 0)
            def _():
                at = pl.ds(pl.multiple_of(block * BLK, BLK), BLK)
                both = mm(qs[arc], data[arc, :, at])
                acc[block] += both[:width] + both[width:]

            return 0

        lax.fori_loop(0, blocks, add, 0)
    ih, il = split(inv_ref[...])
    row = lax.broadcasted_iota(jnp.int32, (width, BLK), 0) + info[1]
    col = lax.broadcasted_iota(jnp.int32, (width, BLK), 1)
    for block in range(blocks):
        at = slice(block * BLK, (block + 1) * BLK)
        hit = row == col + block * BLK
        th, tl = split(acc[block] + jnp.where(hit, reg_ref[:, at], 0.0))
        for top, end in ((0, half), (half, width)):
            value = mm(ih[top:end, :end], th[:end]) + mm(ih[top:end, :end], tl[:end])
            out_ref[top:end, at] = value + mm(il[top:end, :end], th[:end])


def normals_call(info, far, qfar, sums, inverse, reg):
    arcs, size, share = far.shape
    width = inverse.shape[0]
    hbm = pl.BlockSpec(memory_space=pltpu.HBM)
    return pl.pallas_call(
        normals_kernel,
        out_shape=jax.ShapeDtypeStruct((width, share), F32),
        in_specs=[SM, hbm, VM, VM, VM, VM],
        out_specs=VM,
        scratch_shapes=[
            pltpu.VMEM((arcs, size, share), BF16),
            pltpu.VMEM((share // BLK, width, BLK), F32),
            pltpu.SemaphoreType.DMA((arcs,)),
        ],
        compiler_params=grant(28),
        name="normals",
    )(info, far, qfar, sums, inverse, reg)


SUB = 8


def three(value):
    high = value.astype(BF16)
    rest = value - high.astype(F32)
    mid = rest.astype(BF16)
    return high, mid, (rest - mid.astype(F32)).astype(BF16)


def factor_diag(work, between):
    tn = ((0,), (0,))
    wide = work.shape[1]
    for top in range(0, LANE, SUB):
        rows = [work[top + i : top + i + 1, :] for i in range(SUB)]
        e = {}
        for j in range(SUB):
            for i in range(j, SUB):
                at = top + i
                e[j, i] = jnp.broadcast_to(rows[j][:, at : at + 1], (1, LANE))
        for j in range(SUB):
            inv = lax.rsqrt(e[j, j])
            inv2 = jnp.concatenate([inv] * (wide // LANE), axis=1)
            rows[j] = rows[j] * inv2
            for i in range(j + 1, SUB):
                e[j, i] = e[j, i] * inv
            for i in range(j + 1, SUB):
                for k in range(i, SUB):
                    e[i, k] = e[i, k] - e[j, i] * e[j, k]
                coef = jnp.concatenate([e[j, i]] * (wide // LANE), axis=1)
                rows[i] = rows[i] - coef * rows[j]
        part = jnp.concatenate(rows, axis=0)
        work[top : top + SUB, :] = part
        end = top + SUB
        if end < LANE:
            h, m, l = three(part)
            lhs = jnp.concatenate([h, h, m, m, h, l], axis=0)[:, :LANE]
            rhs = jnp.concatenate([h, m, h, m, l, h], axis=0)
            gone = mm(lhs, rhs, tn)
            work[end:, :] = work[end:, :] - gone[end:, :]
        between()


def chol_body(block_ref, other_ref, reg_ref, out_ref, full, work, upper, between):
    size = block_ref.shape[0]
    row = lax.broadcasted_iota(jnp.int32, (size, size), 0)
    col = lax.broadcasted_iota(jnp.int32, (size, size), 1)
    full[...] = (block_ref[...] + other_ref[...]) + jnp.where(row == col, reg_ref[...], 0.0)
    r1 = lax.broadcasted_iota(jnp.int32, (LANE, LANE), 0)
    c1 = lax.broadcasted_iota(jnp.int32, (LANE, LANE), 1)
    out_ref[...] = jnp.zeros(out_ref.shape, F32)
    for top in range(0, size, LANE):
        end = top + LANE
        work[:, :LANE] = full[top:end, top:end]
        work[:, LANE:] = (r1 == c1).astype(F32)
        factor_diag(work, between)
        inverse = jnp.where(r1 >= c1, work[:, LANE:], 0.0)
        out_ref[top:end, top:end] = inverse
        if end < size:
            right = mm3(inverse, full[top:end, end:])
            upper[top:end, end:] = right
            rt = right.T
            full[end:, end:] = full[end:, end:] - mm3(rt, right)
    step = LANE
    while step < size:
        for base in range(0, size, 2 * step):
            left = slice(base, base + step)
            second = slice(base + step, base + 2 * step)
            low = upper[left, second].T
            out_ref[second, left] = -mm3(out_ref[second, second], mm3(low, out_ref[left, left]))
        step *= 2


def chol_kernel(*refs):
    chol_body(*refs, lambda: None)


def chol_normals_kernel(info, block_ref, other_ref, reg_ref, own, qs, out_ref, sums, full, work, upper, data, sems):
    arcs, size, share = data.shape
    width = block_ref.shape[0]
    blocks = share // BLK
    left = pl.multiple_of(info[0] * BLK, BLK)
    copies = []
    for arc in range(arcs):
        source = own.at[arc, :, pl.ds(left, share)]
        copies.append(pltpu.make_async_copy(source, data.at[arc], sems.at[arc]))
    for copy in copies:
        copy.start()
    for block in range(blocks + 1):
        sums[block] = jnp.zeros((width, BLK), F32)
    span = min(256, size)
    slices = [(arc, block, top) for arc in range(arcs) for block in range(blocks) for top in range(0, size, span)]
    panels = width // SUB
    delay = panels // 4
    state = [0, 0]

    def between():
        state[0] += 1
        if state[0] == delay:
            for copy in copies:
                copy.wait()
        goal = len(slices) * max(state[0] - delay, 0) // (panels - delay)
        while state[1] < goal:
            arc, block, top = slices[state[1]]
            state[1] += 1
            target = jnp.where(info[2 + block * 2 * arcs + arc] > 0, block, blocks)
            at = slice(block * BLK, (block + 1) * BLK)
            rows = slice(top, top + span)
            value = mm(qs[arc, :, rows], data[arc, rows, at])
            sums[target] += value[:width] + value[width:]

    chol_body(block_ref, other_ref, reg_ref, out_ref, full, work, upper, between)


def chol_normals(info, block, other, reg, own, qown):
    arcs, observed, _ = own.shape
    size = block.shape[0]
    share = own.shape[2] // 2
    hbm = pl.BlockSpec(memory_space=pltpu.HBM)
    return pl.pallas_call(
        chol_normals_kernel,
        out_shape=(
            jax.ShapeDtypeStruct((size, size), F32),
            jax.ShapeDtypeStruct((share // BLK + 1, size, BLK), F32),
        ),
        in_specs=[SM, VM, VM, VM, hbm, VM],
        out_specs=(VM, VM),
        scratch_shapes=[
            pltpu.VMEM((size, size), F32),
            pltpu.VMEM((LANE, 2 * LANE), F32),
            pltpu.VMEM((size, size), F32),
            pltpu.VMEM((arcs, observed, share), BF16),
            pltpu.SemaphoreType.DMA((arcs,)),
        ],
        compiler_params=grant(28),
        name="chol_normals",
    )(info, block, other, reg, own, qown)


def chol_inverse(block, other, reg):
    size = block.shape[0]
    vm = pl.BlockSpec(memory_space=pltpu.VMEM)
    return pl.pallas_call(
        chol_kernel,
        out_shape=jax.ShapeDtypeStruct((size, size), F32),
        in_specs=[vm, vm, vm],
        out_specs=vm,
        scratch_shapes=[
            pltpu.VMEM((size, size), F32),
            pltpu.VMEM((LANE, 2 * LANE), F32),
            pltpu.VMEM((size, size), F32),
        ],
        compiler_params=grant(12),
        name="chol_inverse",
    )(block, other, reg)


def block_hits(active, first, count):
    ids = first + jnp.arange(count, dtype=jnp.int32)
    return jnp.any(active[:, :, None] == ids[None, None, :], axis=1)


def general(design, cov_factor, active_blocks, panel_index, reg_diag):
    arcs, observed, columns = design.shape
    rows = cov_factor.shape[1]
    par_id = lax.axis_index("par")
    arc_id = lax.axis_index("arc")
    lower = lax.all_gather(factor_rows(cov_factor, par_id), "par", axis=1, tiled=True)
    local_blocks = columns // BLK
    hits = block_hits(active_blocks, par_id * local_blocks, local_blocks)
    masked = design * jnp.repeat(hits, BLK, axis=1).astype(BF16)[:, None, :]
    start = panel_index[0] * PANEL
    padded = jnp.pad(masked, ((0, 0), (0, 0), (PANEL, PANEL)))
    window = lax.dynamic_slice_in_dim(
        padded, jnp.clip(start - par_id * columns + PANEL, 0, columns + PANEL), PANEL, 2
    )
    panel = lax.psum(window.astype(F32).astype(BF16), "par")
    factors = invert_call(functools.partial(invert_dense_kernel, rows), arcs, observed, [lower], [])
    place = jnp.zeros((arcs,), jnp.int32)
    pt, block = panel_call(place, [panel[arc : arc + 1] for arc in range(arcs)], factors)
    qs = back_call(pt, factors)
    both = jnp.einsum("apo,aoc->pc", qs, masked, preferred_element_type=F32)
    gram = both[:PANEL] + both[PANEL:]
    share = columns // lax.axis_size("arc")
    gram, block = lax.psum((gram, block), "arc")
    gram = lax.dynamic_slice_in_dim(gram, arc_id * share, share, 1)
    reg_panel = lax.dynamic_slice_in_dim(reg_diag, start, PANEL)
    inverse = chol_inverse(block, jnp.zeros_like(block), reg_panel[None, :])
    global_cols = par_id * columns + arc_id * share + jnp.arange(share, dtype=jnp.int32)
    rows_at = start + jnp.arange(PANEL, dtype=jnp.int32)
    shifted = gram + jnp.where(global_cols[None, :] == rows_at[:, None], reg_panel[:, None], 0.0)
    return jnp.dot(inverse, shifted, precision=lax.Precision.HIGHEST, preferred_element_type=F32)


def paired(design, cov_factor, active_blocks, panel_index, reg_diag):
    arcs, observed, columns = design.shape
    rows = cov_factor.shape[1]
    chips = lax.axis_size("par")
    planes = chips // 4
    me = lax.axis_index("par")
    core = lax.axis_index("arc")
    sides = (me & 1, (me >> 1) & 1)
    plane = me >> 2
    share = columns // 2
    start = panel_index[0] * PANEL

    def swap(value):
        return lax.ppermute(value, "arc", [(0, 1), (1, 0)])

    def hop(value, bits):
        return lax.ppermute(value, "par", [(p, p ^ bits) for p in range(chips)])

    def spread(value, first):
        second = 3 - first
        direct, other = hop(value, first), hop(value, second)
        corner = hop(direct, second)
        return {0: value, first: direct, second: other, 3: corner}

    offset = start - me * columns
    inside = (offset >= 0) & (offset < columns)
    live = jnp.repeat(block_hits(active_blocks, start // BLK, PANEL // BLK) & inside, BLK, axis=1)
    left = jnp.clip(offset, 0, columns - PANEL)
    half, quarter = observed // 2, observed // 4

    def window(arc, top):
        value = lax.dynamic_slice(design, (jnp.int32(arc), top, left), (1, half, PANEL))[0]
        return jnp.where(live[arc][None, :], value, 0)

    sends = [window(arc, (1 - sides[arc % 2]) * half) for arc in range(arcs)]
    sends, cov_factor = lax.optimization_barrier((sends, cov_factor))
    keeps = [window(arc, sides[arc % 2] * half) for arc in range(arcs)]
    seeds = []
    for arc in range(arcs):
        first, second = arc % 2, 1 - arc % 2
        gone = hop(sends[arc], 1 << first)

        def piece(side):
            at = side * quarter
            return lax.dynamic_slice_in_dim(keeps[arc], at, quarter, 0) + lax.dynamic_slice_in_dim(
                gone, at, quarter, 0
            )

        again = piece(1 - sides[second])
        again = hop(again, 1 << second)
        value = piece(sides[second]) + again
        seeds.append(value.reshape(planes, rows, PANEL))
    seeds = jnp.stack(seeds, axis=1)
    chunk = lax.dynamic_index_in_dim(seeds, plane, 0, False)
    for k in range(1, planes):
        gone = hop(lax.dynamic_index_in_dim(seeds, plane ^ k, 0, False), 4 * k)
        chunk += gone

    lower = factor_rows(cov_factor, me)
    paired_rows = hop(lower, 12)
    ends = (plane == 0) | (plane == 3)
    above = jnp.where(plane < 2, lower, paired_rows)
    below = jnp.where(plane < 2, paired_rows, lower)

    def pack(top, bottom):
        widths = [LANE + 4 * rows * (index + 1) for index in (top, bottom)]
        return jnp.concatenate([above[:, :, : widths[0]], below[:, :, : widths[1]]], axis=2)

    packed = jnp.where(ends, pack(0, 3), pack(1, 2))
    others = hop(packed, 4)
    seats = (me & 3) ^ jnp.arange(4, dtype=jnp.int32)
    seats = jnp.concatenate([seats, ends.astype(jnp.int32)[None]])

    first_column = me * columns + core * share
    both = jnp.concatenate([active_blocks, swap(active_blocks)], axis=0)
    lives = block_hits(both, first_column // BLK, share // BLK).T.reshape(-1).astype(jnp.int32)
    info = jnp.stack([core * (share // BLK), start - first_column]).astype(jnp.int32)
    info = jnp.concatenate([info, lives])
    reg = lax.dynamic_slice_in_dim(reg_diag, first_column, share)[None, :]
    reg_panel = lax.dynamic_slice_in_dim(reg_diag, start, PANEL)[None, :]
    source = me ^ (
        jnp.arange(4, dtype=jnp.int32)[:, None] ^ (4 * jnp.arange(planes, dtype=jnp.int32)[None, :])
    )
    place = []
    for arc in range(arcs):
        bits = (source & 1, (source >> 1) & 1)
        order = (bits[arc % 2] * 2 + bits[1 - arc % 2]) * planes + (source >> 2)
        place.append(order.reshape(-1) * rows)
    place = jnp.concatenate(place)
    far = lax.dynamic_slice_in_dim(design, (1 - core) * share, share, 2)
    far = swap(far)
    chunk, seats, info, reg, reg_panel, place = lax.optimization_barrier(
        (chunk, seats, info, reg, reg_panel, place)
    )

    shares = [seats]
    for arc in range(arcs):
        for value in (packed, others):
            pieces = spread(value[arc], 1 + arc % 2)
            shares += [pieces[k] for k in range(4)]
    factors = invert_call(
        functools.partial(invert_pieces_kernel, rows), arcs, observed, shares,
        [pltpu.VMEM((arcs, observed, observed), BF16), pltpu.VMEM((arcs, observed, LANE), BF16)],
    )

    stack = [chunk] + [hop(chunk, 4 * k) for k in range(1, planes)]
    stack = jnp.stack(stack, axis=1)
    pieces = []
    for arc in range(arcs):
        found = spread(stack[arc], 1 + arc % 2)
        pieces += [found[k] for k in range(4)]
    pt, block = panel_call(place, pieces, factors)
    other = swap(block)
    qs = back_call(pt, factors)
    qs, other = lax.optimization_barrier((qs, other))
    inverse, sums = chol_normals(info, block, other, reg_panel, design, qs)
    return normals_call(info, far, swap(qs), sums, inverse, reg)


def whole(design, cov_factor, *rest):
    chips = lax.axis_size("par")
    columns = design.shape[2]
    fits = (
        lax.axis_size("arc") == 2
        and design.shape[0] == 2
        and chips == 16
        and 16 * cov_factor.shape[1] == cov_factor.shape[2]
        and columns % PANEL == 0
        and columns % (2 * BLK) == 0
        and LANE % cov_factor.shape[1] == 0
    )
    return (paired if fits else general)(design, cov_factor, *rest)


def solution(mesh):
    in_specs = (P("arc", None, "par"), P("arc", "par", None), P("arc", None), P(), P())
    out_specs = P(None, ("par", "arc"))
    return jax.shard_map(
        whole, mesh=mesh, in_specs=in_specs, out_specs=out_specs, check_vma=False
    )
```

```python
import functools

import jax
import jax.numpy as jnp
from jax import lax
from jax.experimental import pallas as pl
from jax.experimental.pallas import tpu as pltpu
from jax.sharding import PartitionSpec as P


PANEL = 512
BLK = 256
F32, BF16 = jnp.float32, jnp.bfloat16
LANE = 128


def split(value):
    high = value.astype(BF16)
    return high, (value - high.astype(F32)).astype(BF16)


def mm(a, b, dims=((1,), (0,))):
    return lax.dot_general(a, b, (dims, ((), ())), preferred_element_type=F32)


def mm3(a, b):
    ah, al = split(a)
    bh, bl = split(b)
    return mm(ah, bh) + (mm(ah, bl) + mm(al, bh))


def level_mask(step):
    rows = lax.broadcasted_iota(jnp.int32, (LANE, LANE), 0)
    cols = lax.broadcasted_iota(jnp.int32, (LANE, LANE), 1)
    return (
        (rows // (2 * step) == cols // (2 * step))
        & ((rows // step) % 2 == 1)
        & ((cols // step) % 2 == 0)
    )


def rows_kernel(place_ref, rows_ref, out_ref, square):
    arcs, rows, _ = rows_ref.shape
    at = pl.multiple_of(place_ref[0], LANE)
    off = pl.multiple_of(place_ref[1], 16)
    r = lax.broadcasted_iota(jnp.int32, (LANE, LANE), 0)
    c = lax.broadcasted_iota(jnp.int32, (LANE, LANE), 1)
    eye = r == c
    sub = lax.broadcasted_iota(jnp.int32, (rows, LANE), 1)
    own = (sub >= off) & (sub < off + rows)
    strips = [rows_ref[arc, :, pl.ds(at, LANE)] for arc in range(arcs)]
    for arc in range(arcs):
        out_ref[arc, :, LANE:] = rows_ref[arc].astype(BF16)
        square[arc] = eye.astype(F32)
        square[arc, pl.ds(off, rows), :] = jnp.where(own, strips[arc], 0.0)
    lowers = [square[arc] for arc in range(arcs)]
    invs = [jnp.where(eye, 1.0 / jnp.where(eye, low, 1.0), 0.0) for low in lowers]
    step = 1
    while step < rows:
        mask = level_mask(step)
        parts = [mm3(jnp.where(mask, low, 0.0), inv) for low, inv in zip(lowers, invs)]
        invs = [inv - mm3(inv, part) for inv, part in zip(invs, parts)]
        step *= 2
    for arc in range(arcs):
        square[arc] = invs[arc]
        value = jnp.where(own, square[arc, pl.ds(off, rows), :], strips[arc])
        high, low = split(value)
        out_ref[arc, :, pl.ds(at + LANE, LANE)] = high
        out_ref[arc, :, :LANE] = low


def factor_rows(cov_factor, me):
    arcs, rows, size = cov_factor.shape
    at = me * rows // LANE * LANE
    place = jnp.stack([at, me * rows - at]).astype(jnp.int32)
    return pl.pallas_call(
        rows_kernel,
        out_shape=jax.ShapeDtypeStruct((arcs, rows, LANE + size), BF16),
        in_specs=[pl.BlockSpec(memory_space=pltpu.SMEM), pl.BlockSpec(memory_space=pltpu.VMEM)],
        out_specs=pl.BlockSpec(memory_space=pltpu.VMEM),
        scratch_shapes=[pltpu.VMEM((arcs, LANE, LANE), F32)],
        compiler_params=pltpu.CompilerParams(vmem_limit_bytes=8 << 20),
        name="factor_rows",
    )(place, cov_factor)


def invert_factor(rest, fine, high, low, first):
    size = high.shape[0]
    half = max(size // 2, LANE)
    for top in range(0, size, half):
        for ref in (high, low):
            ref[top : top + half, top : top + half] = jnp.zeros((half, half), BF16)
    rows = lax.broadcasted_iota(jnp.int32, (LANE, LANE), 0) // first
    cols = lax.broadcasted_iota(jnp.int32, (LANE, LANE), 1) // first
    blocks = [
        rest[t : t + LANE, t : t + LANE].astype(F32) + fine[t : t + LANE, :].astype(F32)
        for t in range(0, size, LANE)
    ]
    invs = [jnp.where(rows == cols, block, 0.0) for block in blocks]
    step = first
    while step < LANE:
        mask = level_mask(step)
        parts = [mm3(jnp.where(mask, block, 0.0), inv) for block, inv in zip(blocks, invs)]
        invs = [inv - mm3(inv, part) for inv, part in zip(invs, parts)]
        step *= 2
    for index, inv in enumerate(invs):
        at = slice(index * LANE, (index + 1) * LANE)
        high[at, at], low[at, at] = split(inv)
    step = LANE
    while step < size:
        for base in range(0, size, 2 * step):
            left = slice(base, base + step)
            right = slice(base + step, base + 2 * step)
            below = rest[right, left]
            ph, pl_ = split(mm(below, high[left, left]) + mm(below, low[left, left]))
            ch, cl = high[right, right], low[right, right]
            high[right, left], low[right, left] = split(-(mm(ch, ph) + (mm(ch, pl_) + mm(cl, ph))))
        step *= 2


VM = pl.BlockSpec(memory_space=pltpu.VMEM)
SM = pl.BlockSpec(memory_space=pltpu.SMEM)
MIB = 1 << 20


def grant(mib):
    return pltpu.CompilerParams(vmem_limit_bytes=mib * MIB)


def invert_pieces_kernel(first, place_ref, *refs):
    pieces, (high, low, rest, fine) = refs[:-4], refs[-4:]
    arcs, _, _ = high.shape
    rows = pieces[0].shape[0]

    def unpack(outer):
        for index, piece in enumerate(pieces):
            arc, seat = index // 8, place_ref[index % 4]
            left = 0
            for plane in (0, 3) if (index // 4 % 2 == 0) == outer else (1, 2):
                width = 4 * rows * (plane + 1)
                at = pl.multiple_of((4 * plane + seat) * rows, 16)
                fine[arc, pl.ds(at, rows), :] = piece[:, left : left + LANE]
                rest[arc, pl.ds(at, rows), :width] = piece[:, left + LANE : left + LANE + width]
                left += LANE + width

    @pl.when(place_ref[4] > 0)
    def _():
        unpack(True)

    @pl.when(place_ref[4] == 0)
    def _():
        unpack(False)

    def one(arc, _):
        invert_factor(rest.at[arc], fine.at[arc], high.at[arc], low.at[arc], first)
        return 0

    lax.fori_loop(0, arcs, one, 0)


def invert_dense_kernel(first, rows_ref, high, low):
    def one(arc, _):
        both = rows_ref.at[arc]
        invert_factor(both.at[:, LANE:], both.at[:, :LANE], high.at[arc], low.at[arc], first)
        return 0

    lax.fori_loop(0, rows_ref.shape[0], one, 0)


def invert_call(kernel, arcs, size, operands, scratch):
    out = jax.ShapeDtypeStruct((arcs, size, size), BF16)
    return pl.pallas_call(
        kernel,
        out_shape=(out, out),
        in_specs=[SM if value.dtype == jnp.int32 else VM for value in operands],
        out_specs=(VM, VM),
        scratch_shapes=scratch,
        compiler_params=grant(28),
        name="invert_factor",
    )(*operands)


def panel_kernel(arcs, place_ref, *refs):
    pieces, (high, low, pt, block_ref, panel) = refs[:-5], refs[-5:]
    count = len(pieces) // arcs
    size = panel.shape[1]
    span = min(256, size)
    nt = ((1,), (1,))
    for arc in range(arcs):
        index = arc * pieces[0].shape[0] * count
        for piece in pieces[arc * count : (arc + 1) * count]:
            rows = piece.shape[1]
            for z in range(piece.shape[0]):
                at = pl.multiple_of(place_ref[index], 16)
                panel[arc, pl.ds(at, rows), :] = piece[z].astype(F32)
                index += 1
    block_ref[...] = jnp.zeros_like(block_ref)

    def one(arc, _):
        raw = panel[arc].T.astype(BF16)
        for top in range(0, size, span):
            end = top + span
            value = mm(raw[:, :end], high[arc, top:end, :end], nt)
            value += mm(raw[:, :end], low[arc, top:end, :end], nt)
            pt[arc, :, top:end] = value.astype(BF16)
        block_ref[...] += mm(pt[arc], pt[arc], nt)
        return 0

    lax.fori_loop(0, arcs, one, 0)


def back_kernel(pt, high, low, q_ref):
    arcs, width, size = pt.shape
    span = min(256, size)

    def one(arc, _):
        for top in range(0, size, span):
            end = top + span
            part = pt[arc, :, top:]
            value = mm(part, high[arc, top:, top:end]) + mm(part, low[arc, top:, top:end])
            q_ref[arc, :width, top:end], q_ref[arc, width:, top:end] = split(value)
        return 0

    lax.fori_loop(0, arcs, one, 0)


def panel_call(place, pieces, factors):
    arcs, size, _ = factors[0].shape
    width = pieces[0].shape[2]
    return pl.pallas_call(
        functools.partial(panel_kernel, arcs),
        out_shape=(
            jax.ShapeDtypeStruct((arcs, width, size), BF16),
            jax.ShapeDtypeStruct((width, width), F32),
        ),
        in_specs=[SM] + [VM] * (len(pieces) + len(factors)),
        out_specs=(VM, VM),
        scratch_shapes=[pltpu.VMEM((arcs, size, width), F32)],
        compiler_params=grant(26),
        name="panel_block",
    )(place, *pieces, *factors)


def back_call(pt, factors):
    arcs, width, size = pt.shape
    return pl.pallas_call(
        back_kernel,
        out_shape=jax.ShapeDtypeStruct((arcs, 2 * width, size), BF16),
        in_specs=[VM] * (1 + len(factors)),
        out_specs=VM,
        compiler_params=grant(26),
        name="back_solve",
    )(pt, *factors)


def normals_kernel(info, far, qs, sums, inv_ref, reg_ref, out_ref, data, acc, sems):
    arcs, _, share = far.shape
    width = inv_ref.shape[0]
    blocks = share // BLK
    half = width // 2
    copies = []
    for arc in range(arcs):
        copies.append(pltpu.make_async_copy(far.at[arc], data.at[arc], sems.at[arc]))
        copies[arc].start()
    for block in range(blocks):
        acc[block] = sums[block]
    for arc in range(arcs):
        copies[arc].wait()

        def add(block, _):
            @pl.when(info[2 + block * 2 * arcs + arcs + arc] > 0)
            def _():
                at = pl.ds(pl.multiple_of(block * BLK, BLK), BLK)
                both = mm(qs[arc], data[arc, :, at])
                acc[block] += both[:width] + both[width:]

            return 0

        lax.fori_loop(0, blocks, add, 0)
    ih, il = split(inv_ref[...])
    row = lax.broadcasted_iota(jnp.int32, (width, BLK), 0) + info[1]
    col = lax.broadcasted_iota(jnp.int32, (width, BLK), 1)
    for block in range(blocks):
        at = slice(block * BLK, (block + 1) * BLK)
        hit = row == col + block * BLK
        th, tl = split(acc[block] + jnp.where(hit, reg_ref[:, at], 0.0))
        for top, end in ((0, half), (half, width)):
            value = mm(ih[top:end, :end], th[:end]) + mm(ih[top:end, :end], tl[:end])
            out_ref[top:end, at] = value + mm(il[top:end, :end], th[:end])


def normals_call(info, far, qfar, sums, inverse, reg):
    arcs, size, share = far.shape
    width = inverse.shape[0]
    hbm = pl.BlockSpec(memory_space=pltpu.HBM)
    return pl.pallas_call(
        normals_kernel,
        out_shape=jax.ShapeDtypeStruct((width, share), F32),
        in_specs=[SM, hbm, VM, VM, VM, VM],
        out_specs=VM,
        scratch_shapes=[
            pltpu.VMEM((arcs, size, share), BF16),
            pltpu.VMEM((share // BLK, width, BLK), F32),
            pltpu.SemaphoreType.DMA((arcs,)),
        ],
        compiler_params=grant(28),
        name="normals",
    )(info, far, qfar, sums, inverse, reg)


SUB = 8


def three(value):
    high = value.astype(BF16)
    rest = value - high.astype(F32)
    mid = rest.astype(BF16)
    return high, mid, (rest - mid.astype(F32)).astype(BF16)


def factor_diag(work, between):
    tn = ((0,), (0,))
    wide = work.shape[1]

    def across(value, at):
        return jnp.broadcast_to(value[:, at : at + 1], (1, LANE))

    def twice(value):
        return jnp.concatenate([value] * (wide // LANE), axis=1)

    rows = [work[i : i + 1, :] for i in range(SUB)]
    for top in range(0, LANE, SUB):
        e = {(j, i): across(rows[j], top + i) for j in range(SUB) for i in range(j, SUB)}
        for j in range(SUB):
            inv = lax.rsqrt(e[j, j])
            rows[j] = rows[j] * twice(inv)
            for i in range(j + 1, SUB):
                e[j, i] = e[j, i] * inv
            for i in range(j + 1, SUB):
                for k in range(i, SUB):
                    e[i, k] = e[i, k] - e[j, i] * e[j, k]
                rows[i] = rows[i] - twice(e[j, i]) * rows[j]
        part = jnp.concatenate(rows, axis=0)
        work[top : top + SUB, :] = part
        end = top + SUB
        if end < LANE:
            later = [work[end + i : end + i + 1, :] for i in range(SUB)]
            for i in range(SUB):
                for j in range(SUB):
                    later[i] = later[i] - twice(across(rows[j], end + i)) * rows[j]
            rows = later
        if end + SUB < LANE:
            h, m, l = three(part)
            lhs = jnp.concatenate([h, h, m, m, h, l], axis=0)[:, :LANE]
            rhs = jnp.concatenate([h, m, h, m, l, h], axis=0)
            gone = mm(lhs, rhs, tn)
            work[end + SUB :, :] = work[end + SUB :, :] - gone[end + SUB :, :]
        between()


def chol_body(block_ref, other_ref, reg_ref, out_ref, full, work, upper, between):
    size = block_ref.shape[0]
    row = lax.broadcasted_iota(jnp.int32, (size, size), 0)
    col = lax.broadcasted_iota(jnp.int32, (size, size), 1)
    full[...] = (block_ref[...] + other_ref[...]) + jnp.where(row == col, reg_ref[...], 0.0)
    r1 = lax.broadcasted_iota(jnp.int32, (LANE, LANE), 0)
    c1 = lax.broadcasted_iota(jnp.int32, (LANE, LANE), 1)
    out_ref[...] = jnp.zeros(out_ref.shape, F32)
    for top in range(0, size, LANE):
        end = top + LANE
        work[:, :LANE] = full[top:end, top:end]
        work[:, LANE:] = (r1 == c1).astype(F32)
        factor_diag(work, between)
        inverse = jnp.where(r1 >= c1, work[:, LANE:], 0.0)
        out_ref[top:end, top:end] = inverse
        if end < size:
            right = mm3(inverse, full[top:end, end:])
            upper[top:end, end:] = right
            rt = right.T
            full[end:, end:] = full[end:, end:] - mm3(rt, right)
    step = LANE
    while step < size:
        for base in range(0, size, 2 * step):
            left = slice(base, base + step)
            second = slice(base + step, base + 2 * step)
            low = upper[left, second].T
            out_ref[second, left] = -mm3(out_ref[second, second], mm3(low, out_ref[left, left]))
        step *= 2


def chol_kernel(*refs):
    chol_body(*refs, lambda: None)


def chol_normals_kernel(info, block_ref, other_ref, reg_ref, own, qs, out_ref, sums, full, work, upper, data, sems):
    arcs, size, share = data.shape
    width = block_ref.shape[0]
    blocks = share // BLK
    left = pl.multiple_of(info[0] * BLK, BLK)
    copies = []
    for arc in range(arcs):
        source = own.at[arc, :, pl.ds(left, share)]
        copies.append(pltpu.make_async_copy(source, data.at[arc], sems.at[arc]))
    for copy in copies:
        copy.start()
    for block in range(blocks + 1):
        sums[block] = jnp.zeros((width, BLK), F32)
    span = min(256, size)
    slices = [(arc, block, top) for arc in range(arcs) for block in range(blocks) for top in range(0, size, span)]
    panels = width // SUB
    delay = panels // 4
    state = [0, 0]

    def between():
        state[0] += 1
        if state[0] == delay:
            for copy in copies:
                copy.wait()
        goal = len(slices) * max(state[0] - delay, 0) // (panels - delay)
        while state[1] < goal:
            arc, block, top = slices[state[1]]
            state[1] += 1
            target = jnp.where(info[2 + block * 2 * arcs + arc] > 0, block, blocks)
            at = slice(block * BLK, (block + 1) * BLK)
            rows = slice(top, top + span)
            value = mm(qs[arc, :, rows], data[arc, rows, at])
            sums[target] += value[:width] + value[width:]

    chol_body(block_ref, other_ref, reg_ref, out_ref, full, work, upper, between)


def chol_normals(info, block, other, reg, own, qown):
    arcs, observed, _ = own.shape
    size = block.shape[0]
    share = own.shape[2] // 2
    hbm = pl.BlockSpec(memory_space=pltpu.HBM)
    return pl.pallas_call(
        chol_normals_kernel,
        out_shape=(
            jax.ShapeDtypeStruct((size, size), F32),
            jax.ShapeDtypeStruct((share // BLK + 1, size, BLK), F32),
        ),
        in_specs=[SM, VM, VM, VM, hbm, VM],
        out_specs=(VM, VM),
        scratch_shapes=[
            pltpu.VMEM((size, size), F32),
            pltpu.VMEM((LANE, 2 * LANE), F32),
            pltpu.VMEM((size, size), F32),
            pltpu.VMEM((arcs, observed, share), BF16),
            pltpu.SemaphoreType.DMA((arcs,)),
        ],
        compiler_params=grant(28),
        name="chol_normals",
    )(info, block, other, reg, own, qown)


def chol_inverse(block, other, reg):
    size = block.shape[0]
    vm = pl.BlockSpec(memory_space=pltpu.VMEM)
    return pl.pallas_call(
        chol_kernel,
        out_shape=jax.ShapeDtypeStruct((size, size), F32),
        in_specs=[vm, vm, vm],
        out_specs=vm,
        scratch_shapes=[
            pltpu.VMEM((size, size), F32),
            pltpu.VMEM((LANE, 2 * LANE), F32),
            pltpu.VMEM((size, size), F32),
        ],
        compiler_params=grant(12),
        name="chol_inverse",
    )(block, other, reg)


def block_hits(active, first, count):
    ids = first + jnp.arange(count, dtype=jnp.int32)
    return jnp.any(active[:, :, None] == ids[None, None, :], axis=1)


def general(design, cov_factor, active_blocks, panel_index, reg_diag):
    arcs, observed, columns = design.shape
    rows = cov_factor.shape[1]
    par_id = lax.axis_index("par")
    arc_id = lax.axis_index("arc")
    lower = lax.all_gather(factor_rows(cov_factor, par_id), "par", axis=1, tiled=True)
    local_blocks = columns // BLK
    hits = block_hits(active_blocks, par_id * local_blocks, local_blocks)
    masked = design * jnp.repeat(hits, BLK, axis=1).astype(BF16)[:, None, :]
    start = panel_index[0] * PANEL
    padded = jnp.pad(masked, ((0, 0), (0, 0), (PANEL, PANEL)))
    window = lax.dynamic_slice_in_dim(
        padded, jnp.clip(start - par_id * columns + PANEL, 0, columns + PANEL), PANEL, 2
    )
    panel = lax.psum(window.astype(F32).astype(BF16), "par")
    factors = invert_call(functools.partial(invert_dense_kernel, rows), arcs, observed, [lower], [])
    place = jnp.zeros((arcs,), jnp.int32)
    pt, block = panel_call(place, [panel[arc : arc + 1] for arc in range(arcs)], factors)
    qs = back_call(pt, factors)
    both = jnp.einsum("apo,aoc->pc", qs, masked, preferred_element_type=F32)
    gram = both[:PANEL] + both[PANEL:]
    share = columns // lax.axis_size("arc")
    gram, block = lax.psum((gram, block), "arc")
    gram = lax.dynamic_slice_in_dim(gram, arc_id * share, share, 1)
    reg_panel = lax.dynamic_slice_in_dim(reg_diag, start, PANEL)
    inverse = chol_inverse(block, jnp.zeros_like(block), reg_panel[None, :])
    global_cols = par_id * columns + arc_id * share + jnp.arange(share, dtype=jnp.int32)
    rows_at = start + jnp.arange(PANEL, dtype=jnp.int32)
    shifted = gram + jnp.where(global_cols[None, :] == rows_at[:, None], reg_panel[:, None], 0.0)
    return jnp.dot(inverse, shifted, precision=lax.Precision.HIGHEST, preferred_element_type=F32)


def paired(design, cov_factor, active_blocks, panel_index, reg_diag):
    arcs, observed, columns = design.shape
    rows = cov_factor.shape[1]
    chips = lax.axis_size("par")
    planes = chips // 4
    me = lax.axis_index("par")
    core = lax.axis_index("arc")
    sides = (me & 1, (me >> 1) & 1)
    plane = me >> 2
    share = columns // 2
    start = panel_index[0] * PANEL

    def swap(value):
        return lax.ppermute(value, "arc", [(0, 1), (1, 0)])

    def hop(value, bits):
        return lax.ppermute(value, "par", [(p, p ^ bits) for p in range(chips)])

    def spread(value, first):
        second = 3 - first
        direct, other = hop(value, first), hop(value, second)
        corner = hop(direct, second)
        return {0: value, first: direct, second: other, 3: corner}

    offset = start - me * columns
    inside = (offset >= 0) & (offset < columns)
    live = jnp.repeat(block_hits(active_blocks, start // BLK, PANEL // BLK) & inside, BLK, axis=1)
    left = jnp.clip(offset, 0, columns - PANEL)
    half, quarter = observed // 2, observed // 4

    def window(arc, top):
        value = lax.dynamic_slice(design, (jnp.int32(arc), top, left), (1, half, PANEL))[0]
        return jnp.where(live[arc][None, :], value, 0)

    sends = [window(arc, (1 - sides[arc % 2]) * half) for arc in range(arcs)]
    sends, cov_factor = lax.optimization_barrier((sends, cov_factor))
    keeps = [window(arc, sides[arc % 2] * half) for arc in range(arcs)]
    seeds = []
    for arc in range(arcs):
        first, second = arc % 2, 1 - arc % 2
        gone = hop(sends[arc], 1 << first)

        def piece(side):
            at = side * quarter
            return lax.dynamic_slice_in_dim(keeps[arc], at, quarter, 0) + lax.dynamic_slice_in_dim(
                gone, at, quarter, 0
            )

        again = piece(1 - sides[second])
        again = hop(again, 1 << second)
        value = piece(sides[second]) + again
        seeds.append(value.reshape(planes, rows, PANEL))
    seeds = jnp.stack(seeds, axis=1)
    chunk = lax.dynamic_index_in_dim(seeds, plane, 0, False)
    for k in range(1, planes):
        gone = hop(lax.dynamic_index_in_dim(seeds, plane ^ k, 0, False), 4 * k)
        chunk += gone

    lower = factor_rows(cov_factor, me)
    paired_rows = hop(lower, 12)
    ends = (plane == 0) | (plane == 3)
    above = jnp.where(plane < 2, lower, paired_rows)
    below = jnp.where(plane < 2, paired_rows, lower)

    def pack(top, bottom):
        widths = [LANE + 4 * rows * (index + 1) for index in (top, bottom)]
        return jnp.concatenate([above[:, :, : widths[0]], below[:, :, : widths[1]]], axis=2)

    packed = jnp.where(ends, pack(0, 3), pack(1, 2))
    others = hop(packed, 4)
    seats = (me & 3) ^ jnp.arange(4, dtype=jnp.int32)
    seats = jnp.concatenate([seats, ends.astype(jnp.int32)[None]])

    first_column = me * columns + core * share
    both = jnp.concatenate([active_blocks, swap(active_blocks)], axis=0)
    lives = block_hits(both, first_column // BLK, share // BLK).T.reshape(-1).astype(jnp.int32)
    info = jnp.stack([core * (share // BLK), start - first_column]).astype(jnp.int32)
    info = jnp.concatenate([info, lives])
    reg = lax.dynamic_slice_in_dim(reg_diag, first_column, share)[None, :]
    reg_panel = lax.dynamic_slice_in_dim(reg_diag, start, PANEL)[None, :]
    source = me ^ (
        jnp.arange(4, dtype=jnp.int32)[:, None] ^ (4 * jnp.arange(planes, dtype=jnp.int32)[None, :])
    )
    place = []
    for arc in range(arcs):
        bits = (source & 1, (source >> 1) & 1)
        order = (bits[arc % 2] * 2 + bits[1 - arc % 2]) * planes + (source >> 2)
        place.append(order.reshape(-1) * rows)
    place = jnp.concatenate(place)
    far = lax.dynamic_slice_in_dim(design, (1 - core) * share, share, 2)
    far = swap(far)
    chunk, seats, info, reg, reg_panel, place = lax.optimization_barrier(
        (chunk, seats, info, reg, reg_panel, place)
    )

    shares = [seats]
    for arc in range(arcs):
        for value in (packed, others):
            pieces = spread(value[arc], 1 + arc % 2)
            shares += [pieces[k] for k in range(4)]
    factors = invert_call(
        functools.partial(invert_pieces_kernel, rows), arcs, observed, shares,
        [pltpu.VMEM((arcs, observed, observed), BF16), pltpu.VMEM((arcs, observed, LANE), BF16)],
    )

    stack = [chunk]
    for k in range(1, planes):
        stack.append(hop(chunk, 4 * k))
    stack = jnp.stack(stack, axis=1)
    pieces = []
    for arc in range(arcs):
        found = spread(stack[arc], 1 + arc % 2)
        pieces += [found[k] for k in range(4)]
    pt, block = panel_call(place, pieces, factors)
    other = swap(block)
    qs = back_call(pt, factors)
    qs, other = lax.optimization_barrier((qs, other))
    inverse, sums = chol_normals(info, block, other, reg_panel, design, qs)
    return normals_call(info, far, swap(qs), sums, inverse, reg)


def whole(design, cov_factor, *rest):
    chips = lax.axis_size("par")
    columns = design.shape[2]
    fits = (
        lax.axis_size("arc") == 2
        and design.shape[0] == 2
        and chips == 16
        and 16 * cov_factor.shape[1] == cov_factor.shape[2]
        and columns % PANEL == 0
        and columns % (2 * BLK) == 0
        and LANE % cov_factor.shape[1] == 0
    )
    return (paired if fits else general)(design, cov_factor, *rest)


def solution(mesh):
    in_specs = (P("arc", None, "par"), P("arc", "par", None), P("arc", None), P(), P())
    out_specs = P(None, ("par", "arc"))
    return jax.shard_map(
        whole, mesh=mesh, in_specs=in_specs, out_specs=out_specs, check_vma=False
    )
```

```python
import functools

import jax
import jax.numpy as jnp
from jax import lax
from jax.experimental import pallas as pl
from jax.experimental.pallas import tpu as pltpu
from jax.sharding import PartitionSpec as P


PANEL = 512
BLK = 256
F32, BF16 = jnp.float32, jnp.bfloat16
LANE = 128


def split(value):
    high = value.astype(BF16)
    return high, (value - high.astype(F32)).astype(BF16)


def mm(a, b, dims=((1,), (0,))):
    return lax.dot_general(a, b, (dims, ((), ())), preferred_element_type=F32)


def mm3(a, b):
    ah, al = split(a)
    bh, bl = split(b)
    return mm(ah, bh) + (mm(ah, bl) + mm(al, bh))


def level_mask(step):
    rows = lax.broadcasted_iota(jnp.int32, (LANE, LANE), 0)
    cols = lax.broadcasted_iota(jnp.int32, (LANE, LANE), 1)
    return (
        (rows // (2 * step) == cols // (2 * step))
        & ((rows // step) % 2 == 1)
        & ((cols // step) % 2 == 0)
    )


def rows_kernel(place_ref, rows_ref, out_ref, square):
    arcs, rows, _ = rows_ref.shape
    at = pl.multiple_of(place_ref[0], LANE)
    off = pl.multiple_of(place_ref[1], 16)
    r = lax.broadcasted_iota(jnp.int32, (LANE, LANE), 0)
    c = lax.broadcasted_iota(jnp.int32, (LANE, LANE), 1)
    eye = r == c
    sub = lax.broadcasted_iota(jnp.int32, (rows, LANE), 1)
    own = (sub >= off) & (sub < off + rows)
    strips = [rows_ref[arc, :, pl.ds(at, LANE)] for arc in range(arcs)]
    for arc in range(arcs):
        out_ref[arc, :, LANE:] = rows_ref[arc].astype(BF16)
        square[arc] = eye.astype(F32)
        square[arc, pl.ds(off, rows), :] = jnp.where(own, strips[arc], 0.0)
    lowers = [square[arc] for arc in range(arcs)]
    invs = [jnp.where(eye, 1.0 / jnp.where(eye, low, 1.0), 0.0) for low in lowers]
    step = 1
    while step < rows:
        mask = level_mask(step)
        parts = [mm3(jnp.where(mask, low, 0.0), inv) for low, inv in zip(lowers, invs)]
        invs = [inv - mm3(inv, part) for inv, part in zip(invs, parts)]
        step *= 2
    for arc in range(arcs):
        square[arc] = invs[arc]
        value = jnp.where(own, square[arc, pl.ds(off, rows), :], strips[arc])
        high, low = split(value)
        out_ref[arc, :, pl.ds(at + LANE, LANE)] = high
        out_ref[arc, :, :LANE] = low


def factor_rows(cov_factor, me):
    arcs, rows, size = cov_factor.shape
    at = me * rows // LANE * LANE
    place = jnp.stack([at, me * rows - at]).astype(jnp.int32)
    return pl.pallas_call(
        rows_kernel,
        out_shape=jax.ShapeDtypeStruct((arcs, rows, LANE + size), BF16),
        in_specs=[pl.BlockSpec(memory_space=pltpu.SMEM), pl.BlockSpec(memory_space=pltpu.VMEM)],
        out_specs=pl.BlockSpec(memory_space=pltpu.VMEM),
        scratch_shapes=[pltpu.VMEM((arcs, LANE, LANE), F32)],
        compiler_params=pltpu.CompilerParams(vmem_limit_bytes=8 << 20),
        name="factor_rows",
    )(place, cov_factor)


def invert_factor(rest, fine, high, low, first):
    size = high.shape[0]
    half = max(size // 2, LANE)
    for top in range(0, size, half):
        for ref in (high, low):
            ref[top : top + half, top : top + half] = jnp.zeros((half, half), BF16)
    rows = lax.broadcasted_iota(jnp.int32, (LANE, LANE), 0) // first
    cols = lax.broadcasted_iota(jnp.int32, (LANE, LANE), 1) // first
    blocks = [
        rest[t : t + LANE, t : t + LANE].astype(F32) + fine[t : t + LANE, :].astype(F32)
        for t in range(0, size, LANE)
    ]
    invs = [jnp.where(rows == cols, block, 0.0) for block in blocks]
    step = first
    while step < LANE:
        mask = level_mask(step)
        parts = [mm3(jnp.where(mask, block, 0.0), inv) for block, inv in zip(blocks, invs)]
        invs = [inv - mm3(inv, part) for inv, part in zip(invs, parts)]
        step *= 2
    for index, inv in enumerate(invs):
        at = slice(index * LANE, (index + 1) * LANE)
        high[at, at], low[at, at] = split(inv)
    step = LANE
    while step < size:
        for base in range(0, size, 2 * step):
            left = slice(base, base + step)
            right = slice(base + step, base + 2 * step)
            below = rest[right, left]
            ph, pl_ = split(mm(below, high[left, left]) + mm(below, low[left, left]))
            ch, cl = high[right, right], low[right, right]
            high[right, left], low[right, left] = split(-(mm(ch, ph) + (mm(ch, pl_) + mm(cl, ph))))
        step *= 2


VM = pl.BlockSpec(memory_space=pltpu.VMEM)
SM = pl.BlockSpec(memory_space=pltpu.SMEM)
MIB = 1 << 20


def grant(mib):
    return pltpu.CompilerParams(vmem_limit_bytes=mib * MIB)


def invert_pieces_kernel(first, place_ref, *refs):
    pieces, (high, low, rest, fine) = refs[:-4], refs[-4:]
    arcs, _, _ = high.shape
    rows = pieces[0].shape[0]

    def unpack(outer):
        for index, piece in enumerate(pieces):
            arc, seat = index // 8, place_ref[index % 4]
            left = 0
            for plane in (0, 3) if (index // 4 % 2 == 0) == outer else (1, 2):
                width = 4 * rows * (plane + 1)
                at = pl.multiple_of((4 * plane + seat) * rows, 16)
                fine[arc, pl.ds(at, rows), :] = piece[:, left : left + LANE]
                rest[arc, pl.ds(at, rows), :width] = piece[:, left + LANE : left + LANE + width]
                left += LANE + width

    @pl.when(place_ref[4] > 0)
    def _():
        unpack(True)

    @pl.when(place_ref[4] == 0)
    def _():
        unpack(False)

    def one(arc, _):
        invert_factor(rest.at[arc], fine.at[arc], high.at[arc], low.at[arc], first)
        return 0

    lax.fori_loop(0, arcs, one, 0)


def invert_dense_kernel(first, rows_ref, high, low):
    def one(arc, _):
        both = rows_ref.at[arc]
        invert_factor(both.at[:, LANE:], both.at[:, :LANE], high.at[arc], low.at[arc], first)
        return 0

    lax.fori_loop(0, rows_ref.shape[0], one, 0)


def invert_call(kernel, arcs, size, operands, scratch):
    out = jax.ShapeDtypeStruct((arcs, size, size), BF16)
    return pl.pallas_call(
        kernel,
        out_shape=(out, out),
        in_specs=[SM if value.dtype == jnp.int32 else VM for value in operands],
        out_specs=(VM, VM),
        scratch_shapes=scratch,
        compiler_params=grant(28),
        name="invert_factor",
    )(*operands)


def panel_kernel(arcs, place_ref, *refs):
    pieces, (high, low, pt, block_ref, panel) = refs[:-5], refs[-5:]
    count = len(pieces) // arcs
    size = panel.shape[1]
    span = min(256, size)
    nt = ((1,), (1,))
    for arc in range(arcs):
        index = arc * pieces[0].shape[0] * count
        for piece in pieces[arc * count : (arc + 1) * count]:
            rows = piece.shape[1]
            for z in range(piece.shape[0]):
                at = pl.multiple_of(place_ref[index], 16)
                panel[arc, pl.ds(at, rows), :] = piece[z].astype(F32)
                index += 1
    half = panel.shape[2] // 2
    block_ref[...] = jnp.zeros_like(block_ref)
    for arc in range(arcs):
        raw = panel[arc].T.astype(BF16)
        for top in range(0, size, span):
            end = top + span
            value = mm(raw[:, :end], high[arc, top:end, :end], nt)
            value += mm(raw[:, :end], low[arc, top:end, :end], nt)
            pt[arc, :, top:end] = value.astype(BF16)
        block_ref[:half, :] += mm(pt[arc, :half], pt[arc], nt)
        block_ref[half:, half:] += mm(pt[arc, half:], pt[arc, half:], nt)


def back_kernel(pt, high, low, q_ref):
    arcs, width, size = pt.shape
    span = min(256, size)

    def one(arc, _):
        for top in range(0, size, span):
            end = top + span
            part = pt[arc, :, top:]
            value = mm(part, high[arc, top:, top:end]) + mm(part, low[arc, top:, top:end])
            q_ref[arc, :width, top:end], q_ref[arc, width:, top:end] = split(value)
        return 0

    lax.fori_loop(0, arcs, one, 0)


def panel_call(place, pieces, factors):
    arcs, size, _ = factors[0].shape
    width = pieces[0].shape[2]
    return pl.pallas_call(
        functools.partial(panel_kernel, arcs),
        out_shape=(
            jax.ShapeDtypeStruct((arcs, width, size), BF16),
            jax.ShapeDtypeStruct((width, width), F32),
        ),
        in_specs=[SM] + [VM] * (len(pieces) + len(factors)),
        out_specs=(VM, VM),
        scratch_shapes=[pltpu.VMEM((arcs, size, width), F32)],
        compiler_params=grant(26),
        name="panel_block",
    )(place, *pieces, *factors)


def back_call(pt, factors):
    arcs, width, size = pt.shape
    return pl.pallas_call(
        back_kernel,
        out_shape=jax.ShapeDtypeStruct((arcs, 2 * width, size), BF16),
        in_specs=[VM] * (1 + len(factors)),
        out_specs=VM,
        compiler_params=grant(26),
        name="back_solve",
    )(pt, *factors)


def normals_kernel(info, far, qs, sums, inv_ref, reg_ref, out_ref, data, acc, sems):
    arcs, _, share = far.shape
    width = inv_ref.shape[0]
    blocks = share // BLK
    half = width // 2
    copies = []
    for arc in range(arcs):
        copies.append(pltpu.make_async_copy(far.at[arc], data.at[arc], sems.at[arc]))
        copies[arc].start()
    for block in range(blocks):
        acc[block] = sums[block]
    for arc in range(arcs):
        copies[arc].wait()

        def add(block, _):
            @pl.when(info[2 + block * 2 * arcs + arcs + arc] > 0)
            def _():
                at = pl.ds(pl.multiple_of(block * BLK, BLK), BLK)
                both = mm(qs[arc], data[arc, :, at])
                acc[block] += both[:width] + both[width:]

            return 0

        lax.fori_loop(0, blocks, add, 0)
    ih, il = split(inv_ref[...])
    row = lax.broadcasted_iota(jnp.int32, (width, BLK), 0) + info[1]
    col = lax.broadcasted_iota(jnp.int32, (width, BLK), 1)
    for block in range(blocks):
        at = slice(block * BLK, (block + 1) * BLK)
        hit = row == col + block * BLK
        th, tl = split(acc[block] + jnp.where(hit, reg_ref[:, at], 0.0))
        for top, end in ((0, half), (half, width)):
            value = mm(ih[top:end, :end], th[:end]) + mm(ih[top:end, :end], tl[:end])
            out_ref[top:end, at] = value + mm(il[top:end, :end], th[:end])


def normals_call(info, far, qfar, sums, inverse, reg):
    arcs, size, share = far.shape
    width = inverse.shape[0]
    hbm = pl.BlockSpec(memory_space=pltpu.HBM)
    return pl.pallas_call(
        normals_kernel,
        out_shape=jax.ShapeDtypeStruct((width, share), F32),
        in_specs=[SM, hbm, VM, VM, VM, VM],
        out_specs=VM,
        scratch_shapes=[
            pltpu.VMEM((arcs, size, share), BF16),
            pltpu.VMEM((share // BLK, width, BLK), F32),
            pltpu.SemaphoreType.DMA((arcs,)),
        ],
        compiler_params=grant(28),
        name="normals",
    )(info, far, qfar, sums, inverse, reg)


SUB = 8


def three(value):
    high = value.astype(BF16)
    rest = value - high.astype(F32)
    mid = rest.astype(BF16)
    return high, mid, (rest - mid.astype(F32)).astype(BF16)


def factor_diag(work, between):
    tn = ((0,), (0,))
    wide = work.shape[1]

    def across(value, at):
        return jnp.broadcast_to(value[:, at : at + 1], (1, LANE))

    def twice(value):
        return jnp.concatenate([value] * (wide // LANE), axis=1)

    rows = [work[i : i + 1, :] for i in range(SUB)]
    for top in range(0, LANE, SUB):
        e = {(j, i): across(rows[j], top + i) for j in range(SUB) for i in range(j, SUB)}
        for j in range(SUB):
            inv = lax.rsqrt(e[j, j])
            rows[j] = rows[j] * twice(inv)
            for i in range(j + 1, SUB):
                e[j, i] = e[j, i] * inv
            for i in range(j + 1, SUB):
                for k in range(i, SUB):
                    e[i, k] = e[i, k] - e[j, i] * e[j, k]
                rows[i] = rows[i] - twice(e[j, i]) * rows[j]
        part = jnp.concatenate(rows, axis=0)
        work[top : top + SUB, :] = part
        end = top + SUB
        if end < LANE:
            later = [work[end + i : end + i + 1, :] for i in range(SUB)]
            for i in range(SUB):
                for j in range(SUB):
                    later[i] = later[i] - twice(across(rows[j], end + i)) * rows[j]
            rows = later
        if end + SUB < LANE:
            h, m, l = three(part)
            lhs = jnp.concatenate([h, h, m, m, h, l], axis=0)[:, :LANE]
            rhs = jnp.concatenate([h, m, h, m, l, h], axis=0)
            gone = mm(lhs, rhs, tn)
            work[end + SUB :, :] = work[end + SUB :, :] - gone[end + SUB :, :]
        between()


def chol_body(block_ref, other_ref, reg_ref, out_ref, full, work, upper, between):
    size = block_ref.shape[0]
    row = lax.broadcasted_iota(jnp.int32, (size, size), 0)
    col = lax.broadcasted_iota(jnp.int32, (size, size), 1)
    full[...] = (block_ref[...] + other_ref[...]) + jnp.where(row == col, reg_ref[...], 0.0)
    r1 = lax.broadcasted_iota(jnp.int32, (LANE, LANE), 0)
    c1 = lax.broadcasted_iota(jnp.int32, (LANE, LANE), 1)
    out_ref[...] = jnp.zeros(out_ref.shape, F32)
    for top in range(0, size, LANE):
        end = top + LANE
        work[:, :LANE] = full[top:end, top:end]
        work[:, LANE:] = (r1 == c1).astype(F32)
        factor_diag(work, between)
        inverse = jnp.where(r1 >= c1, work[:, LANE:], 0.0)
        out_ref[top:end, top:end] = inverse
        if end < size:
            right = mm3(inverse, full[top:end, end:])
            upper[top:end, end:] = right
            rt = right.T
            full[end:, end:] = full[end:, end:] - mm3(rt, right)
    step = LANE
    while step < size:
        for base in range(0, size, 2 * step):
            left = slice(base, base + step)
            second = slice(base + step, base + 2 * step)
            low = upper[left, second].T
            out_ref[second, left] = -mm3(out_ref[second, second], mm3(low, out_ref[left, left]))
        step *= 2


def chol_kernel(*refs):
    chol_body(*refs, lambda: None)


def chol_normals_kernel(info, block_ref, other_ref, reg_ref, own, qs, out_ref, sums, full, work, upper, data, sems):
    arcs, size, share = data.shape
    width = block_ref.shape[0]
    blocks = share // BLK
    left = pl.multiple_of(info[0] * BLK, BLK)
    copies = []
    for arc in range(arcs):
        source = own.at[arc, :, pl.ds(left, share)]
        copies.append(pltpu.make_async_copy(source, data.at[arc], sems.at[arc]))
    for copy in copies:
        copy.start()
    for block in range(blocks + 1):
        sums[block] = jnp.zeros((width, BLK), F32)
    span = min(256, size)
    slices = [(arc, block, top) for arc in range(arcs) for block in range(blocks) for top in range(0, size, span)]
    panels = width // SUB
    delay = panels // 4
    state = [0, 0]

    def between():
        state[0] += 1
        if state[0] == delay:
            for copy in copies:
                copy.wait()
        goal = len(slices) * max(state[0] - delay, 0) // (panels - delay)
        while state[1] < goal:
            arc, block, top = slices[state[1]]
            state[1] += 1
            target = jnp.where(info[2 + block * 2 * arcs + arc] > 0, block, blocks)
            at = slice(block * BLK, (block + 1) * BLK)
            rows = slice(top, top + span)
            value = mm(qs[arc, :, rows], data[arc, rows, at])
            sums[target] += value[:width] + value[width:]

    chol_body(block_ref, other_ref, reg_ref, out_ref, full, work, upper, between)


def chol_normals(info, block, other, reg, own, qown):
    arcs, observed, _ = own.shape
    size = block.shape[0]
    share = own.shape[2] // 2
    hbm = pl.BlockSpec(memory_space=pltpu.HBM)
    return pl.pallas_call(
        chol_normals_kernel,
        out_shape=(
            jax.ShapeDtypeStruct((size, size), F32),
            jax.ShapeDtypeStruct((share // BLK + 1, size, BLK), F32),
        ),
        in_specs=[SM, VM, VM, VM, hbm, VM],
        out_specs=(VM, VM),
        scratch_shapes=[
            pltpu.VMEM((size, size), F32),
            pltpu.VMEM((LANE, 2 * LANE), F32),
            pltpu.VMEM((size, size), F32),
            pltpu.VMEM((arcs, observed, share), BF16),
            pltpu.SemaphoreType.DMA((arcs,)),
        ],
        compiler_params=grant(28),
        name="chol_normals",
    )(info, block, other, reg, own, qown)


def chol_inverse(block, other, reg):
    size = block.shape[0]
    vm = pl.BlockSpec(memory_space=pltpu.VMEM)
    return pl.pallas_call(
        chol_kernel,
        out_shape=jax.ShapeDtypeStruct((size, size), F32),
        in_specs=[vm, vm, vm],
        out_specs=vm,
        scratch_shapes=[
            pltpu.VMEM((size, size), F32),
            pltpu.VMEM((LANE, 2 * LANE), F32),
            pltpu.VMEM((size, size), F32),
        ],
        compiler_params=grant(12),
        name="chol_inverse",
    )(block, other, reg)


def block_hits(active, first, count):
    ids = first + jnp.arange(count, dtype=jnp.int32)
    return jnp.any(active[:, :, None] == ids[None, None, :], axis=1)


def general(design, cov_factor, active_blocks, panel_index, reg_diag):
    arcs, observed, columns = design.shape
    rows = cov_factor.shape[1]
    par_id = lax.axis_index("par")
    arc_id = lax.axis_index("arc")
    lower = lax.all_gather(factor_rows(cov_factor, par_id), "par", axis=1, tiled=True)
    local_blocks = columns // BLK
    hits = block_hits(active_blocks, par_id * local_blocks, local_blocks)
    masked = design * jnp.repeat(hits, BLK, axis=1).astype(BF16)[:, None, :]
    start = panel_index[0] * PANEL
    padded = jnp.pad(masked, ((0, 0), (0, 0), (PANEL, PANEL)))
    window = lax.dynamic_slice_in_dim(
        padded, jnp.clip(start - par_id * columns + PANEL, 0, columns + PANEL), PANEL, 2
    )
    panel = lax.psum(window.astype(F32).astype(BF16), "par")
    factors = invert_call(functools.partial(invert_dense_kernel, rows), arcs, observed, [lower], [])
    place = jnp.zeros((arcs,), jnp.int32)
    pt, block = panel_call(place, [panel[arc : arc + 1] for arc in range(arcs)], factors)
    qs = back_call(pt, factors)
    both = jnp.einsum("apo,aoc->pc", qs, masked, preferred_element_type=F32)
    gram = both[:PANEL] + both[PANEL:]
    share = columns // lax.axis_size("arc")
    gram, block = lax.psum((gram, block), "arc")
    gram = lax.dynamic_slice_in_dim(gram, arc_id * share, share, 1)
    reg_panel = lax.dynamic_slice_in_dim(reg_diag, start, PANEL)
    inverse = chol_inverse(block, jnp.zeros_like(block), reg_panel[None, :])
    global_cols = par_id * columns + arc_id * share + jnp.arange(share, dtype=jnp.int32)
    rows_at = start + jnp.arange(PANEL, dtype=jnp.int32)
    shifted = gram + jnp.where(global_cols[None, :] == rows_at[:, None], reg_panel[:, None], 0.0)
    return jnp.dot(inverse, shifted, precision=lax.Precision.HIGHEST, preferred_element_type=F32)


def paired(design, cov_factor, active_blocks, panel_index, reg_diag):
    arcs, observed, columns = design.shape
    rows = cov_factor.shape[1]
    chips = lax.axis_size("par")
    planes = chips // 4
    me = lax.axis_index("par")
    core = lax.axis_index("arc")
    sides = (me & 1, (me >> 1) & 1)
    plane = me >> 2
    share = columns // 2
    start = panel_index[0] * PANEL

    def swap(value):
        return lax.ppermute(value, "arc", [(0, 1), (1, 0)])

    def hop(value, bits):
        return lax.ppermute(value, "par", [(p, p ^ bits) for p in range(chips)])

    def spread(value, first):
        second = 3 - first
        direct, other = hop(value, first), hop(value, second)
        corner = hop(direct, second)
        return {0: value, first: direct, second: other, 3: corner}

    offset = start - me * columns
    inside = (offset >= 0) & (offset < columns)
    live = jnp.repeat(block_hits(active_blocks, start // BLK, PANEL // BLK) & inside, BLK, axis=1)
    left = jnp.clip(offset, 0, columns - PANEL)
    half, quarter = observed // 2, observed // 4

    def window(arc, top):
        value = lax.dynamic_slice(design, (jnp.int32(arc), top, left), (1, half, PANEL))[0]
        return jnp.where(live[arc][None, :], value, 0)

    sends = [window(arc, (1 - sides[arc % 2]) * half) for arc in range(arcs)]
    sends, cov_factor, listed = lax.optimization_barrier((sends, cov_factor, active_blocks))
    keeps = [window(arc, sides[arc % 2] * half) for arc in range(arcs)]
    seeds = []
    for arc in range(arcs):
        first, second = arc % 2, 1 - arc % 2
        gone = hop(sends[arc], 1 << first)

        def piece(side):
            at = side * quarter
            return lax.dynamic_slice_in_dim(keeps[arc], at, quarter, 0) + lax.dynamic_slice_in_dim(
                gone, at, quarter, 0
            )

        again = piece(1 - sides[second])
        again = hop(again, 1 << second)
        value = piece(sides[second]) + again
        seeds.append(value.reshape(planes, rows, PANEL))
    seeds = jnp.stack(seeds, axis=1)
    chunk = lax.dynamic_index_in_dim(seeds, plane, 0, False)
    for k in range(1, planes):
        gone = hop(lax.dynamic_index_in_dim(seeds, plane ^ k, 0, False), 4 * k)
        chunk += gone

    lower = factor_rows(cov_factor, me)
    paired_rows = hop(lower, 12)
    ends = (plane == 0) | (plane == 3)
    above = jnp.where(plane < 2, lower, paired_rows)
    below = jnp.where(plane < 2, paired_rows, lower)

    def pack(top, bottom):
        widths = [LANE + 4 * rows * (index + 1) for index in (top, bottom)]
        return jnp.concatenate([above[:, :, : widths[0]], below[:, :, : widths[1]]], axis=2)

    packed = jnp.where(ends, pack(0, 3), pack(1, 2))
    others = hop(packed, 4)
    seats = (me & 3) ^ jnp.arange(4, dtype=jnp.int32)
    seats = jnp.concatenate([seats, ends.astype(jnp.int32)[None]])

    first_column = me * columns + core * share
    both = jnp.concatenate([listed, swap(listed)], axis=0)
    lives = block_hits(both, first_column // BLK, share // BLK).T.reshape(-1).astype(jnp.int32)
    info = jnp.stack([core * (share // BLK), start - first_column]).astype(jnp.int32)
    info = jnp.concatenate([info, lives])
    reg = lax.dynamic_slice_in_dim(reg_diag, first_column, share)[None, :]
    reg_panel = lax.dynamic_slice_in_dim(reg_diag, start, PANEL)[None, :]
    source = me ^ (
        jnp.arange(4, dtype=jnp.int32)[:, None] ^ (4 * jnp.arange(planes, dtype=jnp.int32)[None, :])
    )
    place = []
    for arc in range(arcs):
        bits = (source & 1, (source >> 1) & 1)
        order = (bits[arc % 2] * 2 + bits[1 - arc % 2]) * planes + (source >> 2)
        place.append(order.reshape(-1) * rows)
    place = jnp.concatenate(place)
    far = lax.dynamic_slice_in_dim(design, (1 - core) * share, share, 2)
    far = swap(far)
    chunk, seats, info, reg, reg_panel, place = lax.optimization_barrier(
        (chunk, seats, info, reg, reg_panel, place)
    )

    shares = [seats]
    for arc in range(arcs):
        for value in (packed, others):
            pieces = spread(value[arc], 1 + arc % 2)
            shares += [pieces[k] for k in range(4)]
    factors = invert_call(
        functools.partial(invert_pieces_kernel, rows), arcs, observed, shares,
        [pltpu.VMEM((arcs, observed, observed), BF16), pltpu.VMEM((arcs, observed, LANE), BF16)],
    )

    stack = [chunk]
    for k in range(1, planes):
        stack.append(hop(chunk, 4 * k))
    stack = jnp.stack(stack, axis=1)
    pieces = []
    for arc in range(arcs):
        found = spread(stack[arc], 1 + arc % 2)
        pieces += [found[k] for k in range(4)]
    pt, block = panel_call(place, pieces, factors)
    other = swap(block)
    qs = back_call(pt, factors)
    qs, other = lax.optimization_barrier((qs, other))
    inverse, sums = chol_normals(info, block, other, reg_panel, design, qs)
    return normals_call(info, far, swap(qs), sums, inverse, reg)


def whole(design, cov_factor, *rest):
    chips = lax.axis_size("par")
    columns = design.shape[2]
    fits = (
        lax.axis_size("arc") == 2
        and design.shape[0] == 2
        and chips == 16
        and 16 * cov_factor.shape[1] == cov_factor.shape[2]
        and columns % PANEL == 0
        and columns % (2 * BLK) == 0
        and LANE % cov_factor.shape[1] == 0
    )
    return (paired if fits else general)(design, cov_factor, *rest)


def solution(mesh):
    in_specs = (P("arc", None, "par"), P("arc", "par", None), P("arc", None), P(), P())
    out_specs = P(None, ("par", "arc"))
    return jax.shard_map(
        whole, mesh=mesh, in_specs=in_specs, out_specs=out_specs, check_vma=False
    )
```
